128 devices in a mesh: rows: 32 (over x_lo, y, z), offs: 4 (over x_hi, core).
Axes of the slice: x: 4 (x_hi: 2, x_lo: 2; x = x_hi * 2 + x_lo), y: 4, z: 4, core: 2. Of those that a mesh axis runs over, the one named last changes fastest.
Arguments:
- coherency_field: float32 [9, 2048, 1024], P(None, 'rows', 'offs'), may hold values from -2 to 5, as said below
- offsets: int32 [120, 2], replicated, may hold values from -6 to 6, as said below
Outputs:
- despeckled: float32 [9, 2048, 1024], P(None, 'rows', 'offs')
The draws below stay inside these ranges and needn't reach their ends.
Inputs may be any that keep to these rules, and one draw needn't show every extreme that they name: `coherency_field`: each pixel's channels form a positive definite Hermitian matrix in the layout of the steps. The offsets are distinct, none is (0, 0), and both components of each lie in -6..6.
All inputs are finite; a program needn't handle non-finite values.
Results may differ from the reference program's by a relative error of at most 0.0001.
Values sent between devices are 32-bit elements; how exact they have to be, the bound alone decides.
A program may use at most 64 MiB of HBM per device.

```python
import math
import jax
import jax.numpy as jnp
from jax import lax

SEARCH = 6
PATCH = 3
OFFSETS = 120
NROWS = 2048
NCOLS = 1024


def draw_coherency_field(key, part):
    keys = jax.random.split(key, 3)
    shape = (3, NROWS, NCOLS)
    logs = jnp.clip(0.6 * jax.random.normal(keys[0], shape, jnp.float32), -1.5, 1.5)
    magnitude = jax.random.uniform(keys[1], shape, jnp.float32, 0.0, 0.4)
    phase = jax.random.uniform(keys[2], shape, jnp.float32, -math.pi, math.pi)
    diagonal = jnp.exp(logs)
    roots = jnp.sqrt(diagonal)
    pair_scale = jnp.stack([roots[0] * roots[1], roots[0] * roots[2], roots[1] * roots[2]], 0) * magnitude
    real_part = pair_scale * jnp.cos(phase)
    imag_part = pair_scale * jnp.sin(phase)
    return jnp.concatenate([diagonal, real_part, imag_part], 0).astype(jnp.float32)


def draw_offsets(key, part):
    side = 2 * SEARCH + 1
    total = side * side
    center = SEARCH * side + SEARCH
    order = jax.random.permutation(jax.random.fold_in(key, 11), total - 3).astype(jnp.int32) + 1
    order = order + (order >= center).astype(jnp.int32)
    corners = jnp.array([0, total - 1], jnp.int32)
    picked = jnp.concatenate([corners, order[:OFFSETS - 2]], 0)
    mixing = jax.random.permutation(jax.random.fold_in(key, 23), OFFSETS).astype(jnp.int32)
    picked = picked[mixing]
    row_part = picked // side - SEARCH
    col_part = picked % side - SEARCH
    return jnp.stack([row_part, col_part], 1).astype(jnp.int32)


def setup_inputs(seed: int = 0) -> dict:
    key_list = jax.random.split(jax.random.key(seed), 3)
    coherency_field = draw_coherency_field(jax.random.fold_in(key_list[2], 71), 0)
    offsets = draw_offsets(jax.random.fold_in(key_list[2], 71), 0)
    return dict(coherency_field=coherency_field, offsets=offsets)


filter_strength = 1.5


def hermitian_inverse(matrix):
    diag_one, diag_two, diag_three = matrix[0], matrix[1], matrix[2]
    re_onetwo, re_onethree, re_twothree = matrix[3], matrix[4], matrix[5]
    im_onetwo, im_onethree, im_twothree = matrix[6], matrix[7], matrix[8]
    abs_onetwo = re_onetwo * re_onetwo + im_onetwo * im_onetwo
    abs_onethree = re_onethree * re_onethree + im_onethree * im_onethree
    abs_twothree = re_twothree * re_twothree + im_twothree * im_twothree
    yz_real = re_onethree * re_twothree + im_onethree * im_twothree
    yz_imag = im_onethree * re_twothree - re_onethree * im_twothree
    xz_real = re_onetwo * re_twothree - im_onetwo * im_twothree
    xz_imag = re_onetwo * im_twothree + im_onetwo * re_twothree
    yx_real = re_onethree * re_onetwo + im_onethree * im_onetwo
    yx_imag = im_onethree * re_onetwo - re_onethree * im_onetwo
    triple_real = xz_real * re_onethree + xz_imag * im_onethree
    determinant = (diag_one * diag_two * diag_three + 2.0 * triple_real
                   - diag_one * abs_twothree - diag_two * abs_onethree - diag_three * abs_onetwo)
    adjugate = jnp.stack([
        diag_two * diag_three - abs_twothree,
        diag_one * diag_three - abs_onethree,
        diag_one * diag_two - abs_onetwo,
        -(re_onetwo * diag_three - yz_real),
        xz_real - re_onethree * diag_two,
        -(diag_one * re_twothree - yx_real),
        -(im_onetwo * diag_three - yz_imag),
        xz_imag - im_onethree * diag_two,
        -(diag_one * im_twothree - yx_imag),
    ], 0)
    return adjugate / determinant[None]


def pair_trace(left, right):
    return jnp.sum(left[:3] * right[:3], 0) + 2.0 * jnp.sum(left[3:] * right[3:], 0)


def window_sum(values, row_count, col_count):
    side = 2 * PATCH + 1
    partial_rows = values[0:row_count]
    for shift in range(1, side):
        partial_rows = partial_rows + values[shift:shift + row_count]
    total = partial_rows[:, 0:col_count]
    for shift in range(1, side):
        total = total + partial_rows[:, shift:shift + col_count]
    return total


def accumulate(coherency, inverse, validity, offset_list, row_count, col_count):
    span_rows = row_count + 2 * PATCH
    span_cols = col_count + 2 * PATCH
    own_cov = coherency[:, SEARCH:SEARCH + span_rows, SEARCH:SEARCH + span_cols]
    own_inv = inverse[:, SEARCH:SEARCH + span_rows, SEARCH:SEARCH + span_cols]
    own_valid = validity[SEARCH:SEARCH + span_rows, SEARCH:SEARCH + span_cols]
    chans = coherency.shape[0]

    def advance(turn, totals):
        numerator, denominator = totals
        top = SEARCH + offset_list[turn, 0]
        left = SEARCH + offset_list[turn, 1]
        anchor = jnp.zeros((), jnp.int32)
        other_cov = lax.dynamic_slice(coherency, (anchor, top, left), (chans, span_rows, span_cols))
        other_inv = lax.dynamic_slice(inverse, (anchor, top, left), (chans, span_rows, span_cols))
        other_valid = lax.dynamic_slice(validity, (top, left), (span_rows, span_cols))
        distance = (pair_trace(own_inv, other_cov) + pair_trace(own_cov, other_inv) - 6.0) * (own_valid * other_valid)
        patch = window_sum(distance, row_count, col_count) / float((2 * PATCH + 1) ** 2)
        weight = jnp.exp(-patch / filter_strength) * other_valid[PATCH:PATCH + row_count, PATCH:PATCH + col_count]
        numerator = numerator + weight[None] * other_cov[:, PATCH:PATCH + row_count, PATCH:PATCH + col_count]
        denominator = denominator + weight
        return numerator, denominator

    start = (jnp.zeros((chans, row_count, col_count), jnp.float32), jnp.zeros((row_count, col_count), jnp.float32))
    return lax.fori_loop(0, offset_list.shape[0], advance, start)


def reference(coherency_field, offsets):
    rim = SEARCH + PATCH
    padded = jnp.pad(coherency_field, ((0, 0), (rim, rim), (rim, rim)))
    validity = jnp.pad(jnp.ones((NROWS, NCOLS), jnp.float32), ((rim, rim), (rim, rim)))
    inverse = jnp.where(validity[None] > 0, hermitian_inverse(padded), 0.0)
    numerator, denominator = accumulate(padded, inverse, validity, offsets, NROWS, NCOLS)
    return (coherency_field + numerator) / (1.0 + denominator)[None]
```

```python
import functools
import math

import jax
import jax.numpy as jnp
import numpy as np
from jax import lax
from jax.experimental import pallas as pl
from jax.experimental.pallas import tpu as pltpu
from jax.sharding import PartitionSpec as P

SEARCH = 6
PATCH = 3
SIDE = 2 * PATCH + 1
SPAN = 2 * SEARCH + 1
RIM = SEARCH + PATCH
STRENGTH = 1.5
LANES = 128
PAD = 16
CHANS = 9
FEATS = 2 * CHANS + 1
BATCH = 8
EXPONENT = -math.log2(math.e) / (STRENGTH * SIDE * SIDE)


def hermitian_inverse(matrix):
    diag_one, diag_two, diag_three = matrix[0], matrix[1], matrix[2]
    re_onetwo, re_onethree, re_twothree = matrix[3], matrix[4], matrix[5]
    im_onetwo, im_onethree, im_twothree = matrix[6], matrix[7], matrix[8]
    abs_onetwo = re_onetwo * re_onetwo + im_onetwo * im_onetwo
    abs_onethree = re_onethree * re_onethree + im_onethree * im_onethree
    abs_twothree = re_twothree * re_twothree + im_twothree * im_twothree
    yz_real = re_onethree * re_twothree + im_onethree * im_twothree
    yz_imag = im_onethree * re_twothree - re_onethree * im_twothree
    xz_real = re_onetwo * re_twothree - im_onetwo * im_twothree
    xz_imag = re_onetwo * im_twothree + im_onetwo * re_twothree
    yx_real = re_onethree * re_onetwo + im_onethree * im_onetwo
    yx_imag = im_onethree * re_onetwo - re_onethree * im_onetwo
    triple_real = xz_real * re_onethree + xz_imag * im_onethree
    determinant = (
        diag_one * diag_two * diag_three
        + 2.0 * triple_real
        - diag_one * abs_twothree
        - diag_two * abs_onethree
        - diag_three * abs_onetwo
    )
    adjugate = [
        diag_two * diag_three - abs_twothree,
        diag_one * diag_three - abs_onethree,
        diag_one * diag_two - abs_onetwo,
        -(re_onetwo * diag_three - yz_real),
        xz_real - re_onethree * diag_two,
        -(diag_one * re_twothree - yx_real),
        -(im_onetwo * diag_three - yz_imag),
        xz_imag - im_onethree * diag_two,
        -(diag_one * im_twothree - yx_imag),
    ]
    return adjugate, determinant


def band_matrix(cols):
    source = np.arange(cols)[:, None]
    target = np.arange(cols)[None, :]
    main = (np.abs(source - target) <= PATCH).astype(np.float32)
    edge = np.zeros((LANES, cols), np.float32)
    for turn in range(SPAN):
        for place in range(2 * PATCH):
            column = place - PATCH if place < PATCH else cols + place - PATCH
            edge[8 * turn + place] = np.abs(np.arange(cols) - column) <= PATCH
    return np.concatenate([main, main, edge, edge], 0)


def select_matrix():
    pick = np.zeros((LANES, 2 * LANES), np.float32)
    for turn in range(SPAN):
        for place in range(2 * PATCH):
            lane = 32 + place - PATCH if place < PATCH else 96 + place - PATCH
            pick[lane, 8 * turn + place] = 1.0
            pick[lane + turn - SEARCH, LANES + 8 * turn + place] = 1.0
    return pick


def gain(feature):
    if feature == 2 * CHANS:
        return -6.0
    return 1.0 if feature % CHANS < 3 else 2.0


def partner(feature):
    if feature == 2 * CHANS:
        return feature
    return (feature + CHANS) % (2 * CHANS)


def despeckle(
    sizes, offs_ref, origin_ref, main_ref, left_ref, right_ref, band_ref, pick_ref, out_ref,
    feats, moved, own, edges, edge_own, edge_other, edge_dist, edge_sum, dist, sums, weights, totals,
):
    rows, cols, row_total, col_total = sizes
    span_rows = rows + 2 * PAD
    row_tiles = span_rows // 8
    halves = cols // LANES
    dist_rows = rows + 8
    lane = lax.broadcasted_iota(jnp.int32, (8, LANES), 1)
    sub = lax.broadcasted_iota(jnp.int32, (8, LANES), 0)
    row_start, col_start = origin_ref[0], origin_ref[1]
    f32, bf16 = jnp.float32, jnp.bfloat16

    def features(tile, _):
        at = pl.ds(pl.multiple_of(tile * 8, 8), 8)
        row = tile * 8 - PAD + sub
        in_rows = (row >= -RIM) & (row < rows + RIM) & (row + row_start >= 0) & (row + row_start < row_total)
        for group in range(halves + 2):
            col = (group - 1) * LANES + lane
            inside = (
                in_rows & (col >= -RIM) & (col < cols + RIM)
                & (col + col_start >= 0) & (col + col_start < col_total)
            )
            if group == 0:
                cells = [left_ref[c, at, :] for c in range(CHANS)]
            elif group == halves + 1:
                cells = [right_ref[c, at, :] for c in range(CHANS)]
            else:
                cells = [main_ref[c, at, (group - 1) * LANES : group * LANES] for c in range(CHANS)]
            adjugate, determinant = hermitian_inverse(cells)
            scale = 1.0 / determinant
            for c in range(CHANS):
                feats[c, group, at, :] = jnp.where(inside, cells[c], 0.0)
                feats[CHANS + c, group, at, :] = jnp.where(inside, adjugate[c] * scale, 0.0)
            feats[2 * CHANS, group, at, :] = jnp.where(inside, 1.0, 0.0)
        return 0

    lax.fori_loop(0, row_tiles, features, 0)

    def shifts(turn, _):
        c, tile = turn // row_tiles, turn % row_tiles
        at = pl.ds(pl.multiple_of(tile * 8, 8), 8)
        cells = [feats[c, group, at, :] for group in range(halves + 2)]
        for step in range(-SEARCH, SEARCH + 1):
            for half in range(halves):
                here = cells[half + 1]
                if step > 0:
                    value = pltpu.roll(jnp.where(lane >= step, here, cells[half + 2]), LANES - step, 1)
                elif step < 0:
                    value = pltpu.roll(jnp.where(lane < LANES + step, here, cells[half]), -step, 1)
                else:
                    value = here
                moved[step + SEARCH, c, half, at, :] = value
        near = pltpu.roll(jnp.where(lane >= 96, cells[0], cells[1]), 32, 1)
        far = pltpu.roll(jnp.where(lane >= 96, cells[halves], cells[halves + 1]), 96, 1)
        edges[c, at, :] = jnp.where(lane < 64, near, far)
        return 0

    lax.fori_loop(0, FEATS * row_tiles, shifts, 0)

    def edge_pick(c, _):
        both = jnp.dot(edges[c], pick_ref[...], precision=lax.Precision.HIGHEST, preferred_element_type=f32)
        edge_own[c] = both[:, :LANES]
        edge_other[c] = both[:, LANES:]
        return 0

    lax.fori_loop(0, FEATS, edge_pick, 0)

    def own_tiles(tile, _):
        at = pl.ds(pl.multiple_of(tile * 8, 8), 8)
        for half in range(halves):
            for c in range(FEATS):
                own[c, half, at, :] = gain(c) * feats[partner(c), half + 1, pl.ds(tile * 8 + PAD - PATCH, 8), :]
        return 0

    lax.fori_loop(0, dist_rows // 8, own_tiles, 0)

    def edge_tiles(tile, _):
        at = pl.ds(pl.multiple_of(tile * 8, 8), 8)
        mine = [gain(c) * edge_own[partner(c), pl.ds(tile * 8 + PAD - PATCH, 8), :] for c in range(FEATS)]
        for step in range(SPAN):
            value = None
            for c in range(FEATS):
                term = mine[c] * edge_other[c, pl.ds(tile * 8 + PAD - PATCH - SEARCH + step, 8), :]
                value = term if value is None else value + term
            edge_dist[step, at, :] = value
        return 0

    lax.fori_loop(0, dist_rows // 8, edge_tiles, 0)

    def split(value):
        high = value.astype(bf16)
        return high, (value - high.astype(f32)).astype(bf16)

    def edge_sums(step, _):
        for part in range(rows // 16):
            value = edge_dist[step, pl.ds(16 * part, 16), :]
            for s in range(1, SIDE):
                value = value + edge_dist[step, pl.ds(16 * part + s, 16), :]
            high, low = split(value)
            edge_sum[step, 16 * part : 16 * part + 16, :LANES] = high
            edge_sum[step, 16 * part : 16 * part + 16, LANES:] = low
        return 0

    lax.fori_loop(0, SPAN, edge_sums, 0)
    totals[...] = jnp.zeros_like(totals)
    edge_lane = lax.broadcasted_iota(jnp.int32, (16, LANES), 1)

    def batch(turn, _):
        downs = [offs_ref[turn * BATCH + j, 0] for j in range(BATCH)]
        sides = [offs_ref[turn * BATCH + j, 1] + SEARCH for j in range(BATCH)]

        def distances(tile, _):
            at = pl.ds(pl.multiple_of(tile * 8, 8), 8)
            for half in range(halves):
                mine = [own[c, half, at, :] for c in range(FEATS)]
                for j in range(BATCH):
                    rows_at = pl.ds(tile * 8 + PAD - PATCH + downs[j], 8)
                    value = None
                    for c in range(FEATS):
                        term = mine[c] * moved[sides[j], c, half, rows_at, :]
                        value = term if value is None else value + term
                    dist[j, half, at, :] = value
            return 0

        lax.fori_loop(0, dist_rows // 8, distances, 0)

        def window(j, _):
            down = offs_ref[turn * BATCH + j, 0] + SEARCH
            side = offs_ref[turn * BATCH + j, 1] + SEARCH
            keep = jnp.where(edge_lane // 8 == side, 1.0, 0.0).astype(bf16)
            for part in range(rows // 16):
                at = pl.ds(pl.multiple_of(j * rows + 16 * part, 16), 16)
                for half in range(halves):
                    value = dist[j, half, pl.ds(16 * part, 16), :]
                    for s in range(1, SIDE):
                        value = value + dist[j, half, pl.ds(16 * part + s, 16), :]
                    high, low = split(value)
                    sums[at, half * LANES : (half + 1) * LANES] = high
                    sums[at, cols + half * LANES : cols + (half + 1) * LANES] = low
                for k in range(2):
                    sums[at, 2 * cols + k * LANES : 2 * cols + (k + 1) * LANES] = (
                        edge_sum[down, 16 * part : 16 * part + 16, k * LANES : (k + 1) * LANES] * keep
                    )
            return 0

        lax.fori_loop(0, BATCH, window, 0)

        patch = jnp.dot(sums[...], band_ref[...], preferred_element_type=f32)
        weights[...] = jnp.exp2(patch * EXPONENT)

        def accumulate(tile, _):
            at = pl.ds(pl.multiple_of(tile * 8, 8), 8)
            for half in range(halves):
                total = [totals[c, half, at, :] for c in range(CHANS + 1)]
                for j in range(BATCH):
                    rows_at = pl.ds(tile * 8 + PAD + downs[j], 8)
                    weight = weights[
                        pl.ds(pl.multiple_of(j * rows + tile * 8, 8), 8), half * LANES : (half + 1) * LANES
                    ]
                    for c in range(CHANS):
                        total[c] = total[c] + weight * moved[sides[j], c, half, rows_at, :]
                    total[CHANS] = total[CHANS] + weight * moved[sides[j], 2 * CHANS, half, rows_at, :]
                for c in range(CHANS + 1):
                    totals[c, half, at, :] = total[c]
            return 0

        lax.fori_loop(0, rows // 8, accumulate, 0)
        return 0

    lax.fori_loop(0, offs_ref.shape[0] // BATCH, batch, 0)

    def finish(tile, _):
        at = pl.ds(pl.multiple_of(tile * 8, 8), 8)
        for half in range(halves):
            scale = 1.0 / (1.0 + totals[CHANS, half, at, :])
            for c in range(CHANS):
                out_ref[c, at, half * LANES : (half + 1) * LANES] = (
                    feats[c, half + 1, pl.ds(pl.multiple_of(tile * 8 + PAD, 8), 8), :] + totals[c, half, at, :]
                ) * scale
        return 0

    lax.fori_loop(0, rows // 8, finish, 0)


def exchange(cells, axis, width, dim):
    count = lax.axis_size(axis)
    ends = count - 1
    head = lax.slice_in_dim(cells, 0, width, axis=dim)
    tail = lax.slice_in_dim(cells, cells.shape[dim] - width, cells.shape[dim], axis=dim)
    before = lax.ppermute(tail, axis, [(i, i + 1) for i in range(ends)])
    after = lax.ppermute(head, axis, [(i + 1, i) for i in range(ends)])
    return before, after


def per_device(coherency_field, offsets):
    _, rows, cols = coherency_field.shape
    row_total = rows * lax.axis_size("rows")
    col_total = cols * lax.axis_size("offs")
    origin = jnp.stack([lax.axis_index("rows") * rows, lax.axis_index("offs") * cols]).astype(jnp.int32)
    above, below = exchange(coherency_field, "rows", PAD, 1)
    main = jnp.concatenate([above, coherency_field, below], 1)
    left, right = exchange(main, "offs", RIM, 2)
    left = jnp.pad(left, ((0, 0), (0, 0), (LANES - RIM, 0)))
    right = jnp.pad(right, ((0, 0), (0, 0), (0, LANES - RIM)))
    span_rows = rows + 2 * PAD
    halves = cols // LANES
    vmem = pl.BlockSpec(memory_space=pltpu.VMEM)
    smem = pl.BlockSpec(memory_space=pltpu.SMEM)
    f32, bf16 = jnp.float32, jnp.bfloat16
    return pl.pallas_call(
        functools.partial(despeckle, (rows, cols, row_total, col_total)),
        out_shape=jax.ShapeDtypeStruct((CHANS, rows, cols), f32),
        in_specs=[smem, smem, vmem, vmem, vmem, vmem, vmem],
        out_specs=vmem,
        scratch_shapes=[
            pltpu.VMEM((FEATS, halves + 2, span_rows, LANES), f32),
            pltpu.VMEM((SPAN, FEATS, halves, span_rows, LANES), f32),
            pltpu.VMEM((FEATS, halves, rows + 8, LANES), f32),
            pltpu.VMEM((FEATS, span_rows, LANES), f32),
            pltpu.VMEM((FEATS, span_rows, LANES), f32),
            pltpu.VMEM((FEATS, span_rows, LANES), f32),
            pltpu.VMEM((SPAN, rows + 8, LANES), f32),
            pltpu.VMEM((SPAN, rows, 2 * LANES), bf16),
            pltpu.VMEM((BATCH, halves, rows + 8, LANES), f32),
            pltpu.VMEM((BATCH * rows, 2 * cols + 2 * LANES), bf16),
            pltpu.VMEM((BATCH * rows, cols), f32),
            pltpu.VMEM((CHANS + 1, halves, rows, LANES), f32),
        ],
        compiler_params=pltpu.CompilerParams(vmem_limit_bytes=56 * 1024 * 1024),
    )(
        offsets, origin, main, left, right,
        jnp.asarray(band_matrix(cols), bf16), jnp.asarray(select_matrix(), f32),
    )


def solution(mesh):
    in_specs = (P(None, "rows", "offs"), P())
    out_specs = P(None, "rows", "offs")
    return jax.shard_map(
        per_device, mesh=mesh, in_specs=in_specs, out_specs=out_specs, check_vma=False
    )
```

```python
import functools
import math

import jax
import jax.numpy as jnp
import numpy as np
from jax import lax
from jax.experimental import pallas as pl
from jax.experimental.pallas import tpu as pltpu
from jax.sharding import PartitionSpec as P

SEARCH = 6
PATCH = 3
SIDE = 2 * PATCH + 1
SPAN = 2 * SEARCH + 1
RIM = SEARCH + PATCH
STRENGTH = 1.5
LANES = 128
PAD = 16
CHANS = 9
FEATS = 2 * CHANS + 1
BATCH = 24
BANKS = 16
EXPONENT = -math.log2(math.e) / (STRENGTH * SIDE * SIDE)


def hermitian_inverse(matrix):
    diag_one, diag_two, diag_three = matrix[0], matrix[1], matrix[2]
    re_onetwo, re_onethree, re_twothree = matrix[3], matrix[4], matrix[5]
    im_onetwo, im_onethree, im_twothree = matrix[6], matrix[7], matrix[8]
    abs_onetwo = re_onetwo * re_onetwo + im_onetwo * im_onetwo
    abs_onethree = re_onethree * re_onethree + im_onethree * im_onethree
    abs_twothree = re_twothree * re_twothree + im_twothree * im_twothree
    yz_real = re_onethree * re_twothree + im_onethree * im_twothree
    yz_imag = im_onethree * re_twothree - re_onethree * im_twothree
    xz_real = re_onetwo * re_twothree - im_onetwo * im_twothree
    xz_imag = re_onetwo * im_twothree + im_onetwo * re_twothree
    yx_real = re_onethree * re_onetwo + im_onethree * im_onetwo
    yx_imag = im_onethree * re_onetwo - re_onethree * im_onetwo
    triple_real = xz_real * re_onethree + xz_imag * im_onethree
    determinant = (
        diag_one * diag_two * diag_three
        + 2.0 * triple_real
        - diag_one * abs_twothree
        - diag_two * abs_onethree
        - diag_three * abs_onetwo
    )
    adjugate = [
        diag_two * diag_three - abs_twothree,
        diag_one * diag_three - abs_onethree,
        diag_one * diag_two - abs_onetwo,
        -(re_onetwo * diag_three - yz_real),
        xz_real - re_onethree * diag_two,
        -(diag_one * re_twothree - yx_real),
        -(im_onetwo * diag_three - yz_imag),
        xz_imag - im_onethree * diag_two,
        -(diag_one * im_twothree - yx_imag),
    ]
    return adjugate, determinant


def band_matrix(cols):
    source = np.arange(cols)[:, None]
    target = np.arange(cols)[None, :]
    main = (np.abs(source - target) <= PATCH).astype(np.float32)
    edge = np.zeros((LANES, cols), np.float32)
    for turn in range(SPAN):
        for place in range(2 * PATCH):
            column = place - PATCH if place < PATCH else cols + place - PATCH
            edge[8 * turn + place] = np.abs(np.arange(cols) - column) <= PATCH
    return np.concatenate([main, main, edge, edge], 0)


def select_matrix():
    pick = np.zeros((LANES, 2 * LANES), np.float32)
    for turn in range(SPAN):
        for place in range(2 * PATCH):
            lane = 32 + place - PATCH if place < PATCH else 96 + place - PATCH
            pick[lane, 8 * turn + place] = 1.0
            pick[lane + turn - SEARCH, LANES + 8 * turn + place] = 1.0
    return np.concatenate([pick] * 3, 0)


def gain(feature):
    if feature == 2 * CHANS:
        return -6.0
    return 1.0 if feature % CHANS < 3 else 2.0


def partner(feature):
    if feature == 2 * CHANS:
        return feature
    return (feature + CHANS) % (2 * CHANS)


def despeckle(
    sizes, offs_ref, origin_ref, field_ref, above_ref, below_ref, left_ref, right_ref, band_ref, pick_ref, out_ref,
    feats, moved, own, edges, edge_own, edge_other, edge_dist, edge_sum, dist, sums, weights, totals,
):
    rows, cols, row_total, col_total = sizes
    span_rows = rows + 2 * PAD
    row_tiles = span_rows // 8
    halves = cols // LANES
    dist_rows = rows + 8
    lane = lax.broadcasted_iota(jnp.int32, (8, LANES), 1)
    sub = lax.broadcasted_iota(jnp.int32, (8, LANES), 0)
    row_start, col_start = origin_ref[0], origin_ref[1]
    f32, bf16 = jnp.float32, jnp.bfloat16

    def features(source_ref, first, tile, _):
        at = pl.ds(pl.multiple_of(tile * 8, 8), 8)
        source_at = pl.ds(pl.multiple_of(tile * 8 - first, 8), 8)
        row = tile * 8 - PAD + sub
        in_rows = (row >= -RIM) & (row < rows + RIM) & (row + row_start >= 0) & (row + row_start < row_total)
        for group in range(halves + 2):
            col = (group - 1) * LANES + lane
            inside = (
                in_rows & (col >= -RIM) & (col < cols + RIM)
                & (col + col_start >= 0) & (col + col_start < col_total)
            )
            if group == 0:
                packed = left_ref[at, :]
                cells = [pltpu.roll(packed, LANES - RIM - RIM * c, 1) for c in range(CHANS)]
            elif group == halves + 1:
                packed = right_ref[at, :]
                cells = [pltpu.roll(packed, LANES - RIM * c, 1) if c else packed for c in range(CHANS)]
            else:
                cells = [source_ref[c, source_at, (group - 1) * LANES : group * LANES] for c in range(CHANS)]
            adjugate, determinant = hermitian_inverse(cells)
            scale = 1.0 / determinant
            for c in range(CHANS):
                feats[group, c, at, :] = jnp.where(inside, cells[c], 0.0)
                feats[group, CHANS + c, at, :] = jnp.where(inside, adjugate[c] * scale, 0.0)
            feats[group, 2 * CHANS, at, :] = jnp.where(inside, 1.0, 0.0)
        return 0

    head, tail = PAD // 8, (PAD + rows) // 8
    lax.fori_loop(0, head, functools.partial(features, above_ref, 0), 0)
    lax.fori_loop(head, tail, functools.partial(features, field_ref, PAD), 0)
    lax.fori_loop(tail, row_tiles, functools.partial(features, below_ref, PAD + rows), 0)

    def split(value):
        high = value.astype(bf16)
        return high, (value - high.astype(f32)).astype(bf16)

    def shifts(tile, _):
        at = pl.ds(pl.multiple_of(tile * 8, 8), 8)
        for c in range(FEATS):
            cells = [feats[group, c, at, :] for group in range(halves + 2)]
            for step in range(-SEARCH, SEARCH + 1):
                for half in range(halves):
                    here = cells[half + 1]
                    if step > 0:
                        value = pltpu.roll(jnp.where(lane >= step, here, cells[half + 2]), LANES - step, 1)
                    elif step < 0:
                        value = pltpu.roll(jnp.where(lane < LANES + step, here, cells[half]), -step, 1)
                    else:
                        value = here
                    moved[step + SEARCH, half, c, at, :] = value
            near = pltpu.roll(jnp.where(lane >= 96, cells[0], cells[1]), 32, 1)
            far = pltpu.roll(jnp.where(lane >= 96, cells[halves], cells[halves + 1]), 96, 1)
            edges[pl.ds(pl.multiple_of(c * span_rows + tile * 8, 8), 8), :] = jnp.where(lane < 64, near, far)
        return 0

    lax.fori_loop(0, row_tiles, shifts, 0)

    def edge_pick(c, _):
        value = edges[pl.ds(pl.multiple_of(c * span_rows, 8), span_rows), :]
        high, rest = value.astype(bf16), value - value.astype(bf16).astype(f32)
        middle, low = split(rest)
        parts = jnp.concatenate([high, middle, low], 1)
        both = jnp.dot(parts, pick_ref[...], preferred_element_type=f32)
        edge_own[c, :span_rows] = both[:, :LANES]
        edge_other[c, :span_rows] = both[:, LANES:]
        return 0

    lax.fori_loop(0, FEATS, edge_pick, 0)

    def own_tiles(tile, _):
        at = pl.ds(pl.multiple_of(tile * 8, 8), 8)
        for half in range(halves):
            for c in range(FEATS):
                own[half, c, at, :] = gain(c) * feats[half + 1, partner(c), pl.ds(tile * 8 + PAD - PATCH, 8), :]
        return 0

    lax.fori_loop(0, dist_rows // 8, own_tiles, 0)

    def edge_tiles(tile, _):
        at = pl.ds(pl.multiple_of(tile * 8, 8), 8)
        mine = [gain(c) * edge_own[partner(c), pl.ds(tile * 8 + PAD - PATCH, 8), :] for c in range(FEATS)]
        for step in range(SPAN):
            value = None
            for c in range(FEATS):
                term = mine[c] * edge_other[c, pl.ds(tile * 8 + PAD - PATCH - SEARCH + step, 8), :]
                value = term if value is None else value + term
            edge_dist[step, at, :] = value
        return 0

    lax.fori_loop(0, dist_rows // 8, edge_tiles, 0)

    def edge_sums(step, _):
        for part in range(rows // 16):
            value = edge_dist[step, pl.ds(16 * part, 16), :]
            for s in range(1, SIDE):
                value = value + edge_dist[step, pl.ds(16 * part + s, 16), :]
            high, low = split(value)
            edge_sum[step, 16 * part : 16 * part + 16, :LANES] = high
            edge_sum[step, 16 * part : 16 * part + 16, LANES:] = low
        return 0

    lax.fori_loop(0, SPAN, edge_sums, 0)
    totals[...] = jnp.zeros_like(totals)
    edge_lane = lax.broadcasted_iota(jnp.int32, (16, LANES), 1)

    def batch(turn, _):
        downs = [offs_ref[turn * BATCH + j, 0] for j in range(BATCH)]
        sides = [offs_ref[turn * BATCH + j, 1] + SEARCH for j in range(BATCH)]

        def distances(step, _):
            half, tile = step % halves, step // halves
            at = pl.ds(pl.multiple_of(tile * 8, 8), 8)
            mine = [own[half, c, at, :] for c in range(FEATS)]
            for j in range(BATCH):
                rows_at = pl.ds(tile * 8 + PAD - PATCH + downs[j], 8)
                value = None
                for c in range(FEATS):
                    term = mine[c] * moved[sides[j], half, c, rows_at, :]
                    value = term if value is None else value + term
                dist[j, half, at, :] = value
            return 0

        lax.fori_loop(0, halves * dist_rows // 8, distances, 0)

        def window(j, _):
            down = offs_ref[turn * BATCH + j, 0] + SEARCH
            side = offs_ref[turn * BATCH + j, 1] + SEARCH
            keep = jnp.where(edge_lane // 8 == side, 1.0, 0.0).astype(bf16)
            for part in range(rows // 16):
                at = pl.ds(pl.multiple_of(j * rows + 16 * part, 16), 16)
                for half in range(halves):
                    value = dist[j, half, pl.ds(16 * part, 16), :]
                    for s in range(1, SIDE):
                        value = value + dist[j, half, pl.ds(16 * part + s, 16), :]
                    high, low = split(value)
                    sums[at, half * LANES : (half + 1) * LANES] = high
                    sums[at, cols + half * LANES : cols + (half + 1) * LANES] = low
                for k in range(2):
                    sums[at, 2 * cols + k * LANES : 2 * cols + (k + 1) * LANES] = (
                        edge_sum[down, 16 * part : 16 * part + 16, k * LANES : (k + 1) * LANES] * keep
                    )
            return 0

        lax.fori_loop(0, BATCH, window, 0)

        patch = jnp.dot(sums[...], band_ref[...], preferred_element_type=f32)
        weights[...] = jnp.exp2(patch * EXPONENT)

        def accumulate(tile, _):
            at = pl.ds(pl.multiple_of(tile * 8, 8), 8)
            for half in range(halves):
                total = [totals[half, c, at, :] for c in range(CHANS + 1)]
                for j in range(BATCH):
                    rows_at = pl.ds(tile * 8 + PAD + downs[j], 8)
                    weight = weights[
                        pl.ds(pl.multiple_of(j * rows + tile * 8, 8), 8), half * LANES : (half + 1) * LANES
                    ]
                    for c in range(CHANS):
                        total[c] = total[c] + weight * moved[sides[j], half, c, rows_at, :]
                    total[CHANS] = total[CHANS] + weight * moved[sides[j], half, 2 * CHANS, rows_at, :]
                for c in range(CHANS + 1):
                    totals[half, c, at, :] = total[c]
            return 0

        lax.fori_loop(0, rows // 8, accumulate, 0)
        return 0

    lax.fori_loop(0, offs_ref.shape[0] // BATCH, batch, 0)

    def finish(tile, _):
        at = pl.ds(pl.multiple_of(tile * 8, 8), 8)
        for half in range(halves):
            span = slice(half * LANES, (half + 1) * LANES)
            scale = 1.0 / (1.0 + totals[half, CHANS, at, :])
            for c in range(CHANS):
                out_ref[c, at, span] = (field_ref[c, at, span] + totals[half, c, at, :]) * scale
        return 0

    lax.fori_loop(0, rows // 8, finish, 0)


def swap_halo(field_ref, above_ref, below_ref, left_ref, right_ref, packs, send_sems, recv_sems):
    rows, cols = field_ref.shape[1:]
    row, col = lax.axis_index("rows"), lax.axis_index("offs")
    row_count, col_count = lax.axis_size("rows"), lax.axis_size("offs")

    def device(down, side):
        return (lax.rem(row + down + row_count, row_count), lax.rem(col + side + col_count, col_count))

    around = [(down, side) for down in (-1, 0, 1) for side in (-1, 0, 1) if (down, side) != (0, 0)]
    barrier = pltpu.get_barrier_semaphore()
    for down, side in around:
        pl.semaphore_signal(barrier, inc=1, device_id=device(down, side), device_id_type=pl.DeviceIdType.MESH)

    lane = lax.broadcasted_iota(jnp.int32, (rows, LANES), 1)
    first = field_ref[0, :, :LANES]
    last = pltpu.roll(field_ref[0, :, cols - LANES :], RIM, 1)
    for c in range(1, CHANS):
        here = (lane >= RIM * c) & (lane < RIM * (c + 1))
        first = jnp.where(here, pltpu.roll(field_ref[c, :, :LANES], RIM * c, 1), first)
        last = jnp.where(here, pltpu.roll(field_ref[c, :, cols - LANES :], (RIM * c + RIM) % LANES, 1), last)
    packs[0] = first
    packs[1] = last
    pl.semaphore_wait(barrier, len(around))

    copies = []
    for k, (down, side) in enumerate(around):
        start, size, put = {-1: (0, PAD, PAD + rows), 0: (0, rows, PAD), 1: (rows - PAD, PAD, 0)}[down]
        if side == 0:
            source = field_ref.at[:, start : start + size, :]
            target = below_ref if down < 0 else above_ref
        else:
            source = packs.at[0 if side < 0 else 1, start : start + size, :]
            target = (right_ref if side < 0 else left_ref).at[put : put + size, :]
        copies.append(pltpu.make_async_remote_copy(
            src_ref=source, dst_ref=target, send_sem=send_sems.at[k], recv_sem=recv_sems.at[k],
            device_id=device(down, side), device_id_type=pl.DeviceIdType.MESH,
        ))
    for copy in copies:
        copy.start()
    for copy in copies:
        copy.wait()


def exchange(field):
    _, rows, cols = field.shape
    vmem = pl.BlockSpec(memory_space=pltpu.VMEM)
    slab = jax.ShapeDtypeStruct((CHANS, PAD, cols), jnp.float32)
    side = jax.ShapeDtypeStruct((rows + 2 * PAD, LANES), jnp.float32)
    return pl.pallas_call(
        swap_halo,
        out_shape=(slab, slab, side, side),
        in_specs=[vmem],
        out_specs=(vmem, vmem, vmem, vmem),
        scratch_shapes=[
            pltpu.VMEM((2, rows, LANES), jnp.float32),
            pltpu.SemaphoreType.DMA((8,)),
            pltpu.SemaphoreType.DMA((8,)),
        ],
        compiler_params=pltpu.CompilerParams(collective_id=0, has_side_effects=True),
    )(field)


def filter_block(sizes, offsets, origin, field, above, below, left, right):
    rows, cols = sizes[:2]
    span_rows = rows + 2 * PAD
    halves = cols // LANES
    vmem = pl.BlockSpec(memory_space=pltpu.VMEM)
    smem = pl.BlockSpec(memory_space=pltpu.SMEM)
    f32, bf16 = jnp.float32, jnp.bfloat16
    return pl.pallas_call(
        functools.partial(despeckle, sizes),
        out_shape=jax.ShapeDtypeStruct((CHANS, rows, cols), f32),
        in_specs=[smem, smem] + [vmem] * 7,
        out_specs=vmem,
        scratch_shapes=[
            pltpu.VMEM((halves + 2, FEATS, span_rows + BANKS, LANES), f32),
            pltpu.VMEM((SPAN, halves, FEATS, span_rows + BANKS, LANES), f32),
            pltpu.VMEM((halves, FEATS, rows + BANKS, LANES), f32),
            pltpu.VMEM((FEATS * span_rows, LANES), f32),
            pltpu.VMEM((FEATS, span_rows + BANKS, LANES), f32),
            pltpu.VMEM((FEATS, span_rows + BANKS, LANES), f32),
            pltpu.VMEM((SPAN, rows + 8, LANES), f32),
            pltpu.VMEM((SPAN, rows, 2 * LANES), bf16),
            pltpu.VMEM((BATCH, halves, rows + 8, LANES), f32),
            pltpu.VMEM((BATCH * rows, 2 * cols + 2 * LANES), bf16),
            pltpu.VMEM((BATCH * rows, cols), f32),
            pltpu.VMEM((halves, CHANS + 1, rows + BANKS, LANES), f32),
        ],
        compiler_params=pltpu.CompilerParams(vmem_limit_bytes=56 * 1024 * 1024),
    )(
        offsets, origin, field, above, below, left, right,
        jnp.asarray(band_matrix(cols), bf16), jnp.asarray(select_matrix(), bf16),
    )


def per_device(coherency_field, offsets):
    _, rows, cols = coherency_field.shape
    row_total = rows * lax.axis_size("rows")
    col_total = cols * lax.axis_size("offs")
    origin = jnp.stack([lax.axis_index("rows") * rows, lax.axis_index("offs") * cols]).astype(jnp.int32)
    halo = exchange(coherency_field)
    return filter_block((rows, cols, row_total, col_total), offsets, origin, coherency_field, *halo)


def solution(mesh):
    in_specs = (P(None, "rows", "offs"), P())
    out_specs = P(None, "rows", "offs")
    return jax.shard_map(
        per_device, mesh=mesh, in_specs=in_specs, out_specs=out_specs, check_vma=False
    )
```

```python
import functools
import math

import jax
import jax.numpy as jnp
import numpy as np
from jax import lax
from jax.experimental import pallas as pl
from jax.experimental.pallas import tpu as pltpu
from jax.sharding import PartitionSpec as P

SEARCH = 6
PATCH = 3
SIDE = 2 * PATCH + 1
SPAN = 2 * SEARCH + 1
RIM = SEARCH + PATCH
STRENGTH = 1.5
LANES = 128
PAD = 16
CHANS = 9
FEATS = 2 * CHANS + 1
BATCH = 24
BANKS = 16
EXPONENT = -math.log2(math.e) / (STRENGTH * SIDE * SIDE)


def hermitian_inverse(matrix):
    diag_one, diag_two, diag_three = matrix[0], matrix[1], matrix[2]
    re_onetwo, re_onethree, re_twothree = matrix[3], matrix[4], matrix[5]
    im_onetwo, im_onethree, im_twothree = matrix[6], matrix[7], matrix[8]
    abs_onetwo = re_onetwo * re_onetwo + im_onetwo * im_onetwo
    abs_onethree = re_onethree * re_onethree + im_onethree * im_onethree
    abs_twothree = re_twothree * re_twothree + im_twothree * im_twothree
    yz_real = re_onethree * re_twothree + im_onethree * im_twothree
    yz_imag = im_onethree * re_twothree - re_onethree * im_twothree
    xz_real = re_onetwo * re_twothree - im_onetwo * im_twothree
    xz_imag = re_onetwo * im_twothree + im_onetwo * re_twothree
    yx_real = re_onethree * re_onetwo + im_onethree * im_onetwo
    yx_imag = im_onethree * re_onetwo - re_onethree * im_onetwo
    triple_real = xz_real * re_onethree + xz_imag * im_onethree
    determinant = (
        diag_one * diag_two * diag_three
        + 2.0 * triple_real
        - diag_one * abs_twothree
        - diag_two * abs_onethree
        - diag_three * abs_onetwo
    )
    adjugate = [
        diag_two * diag_three - abs_twothree,
        diag_one * diag_three - abs_onethree,
        diag_one * diag_two - abs_onetwo,
        -(re_onetwo * diag_three - yz_real),
        xz_real - re_onethree * diag_two,
        -(diag_one * re_twothree - yx_real),
        -(im_onetwo * diag_three - yz_imag),
        xz_imag - im_onethree * diag_two,
        -(diag_one * im_twothree - yx_imag),
    ]
    return adjugate, determinant


def band_matrix(cols):
    source = np.arange(cols)[:, None]
    target = np.arange(cols)[None, :]
    main = (np.abs(source - target) <= PATCH).astype(np.float32)
    edge = np.zeros((LANES, cols), np.float32)
    for turn in range(SPAN):
        for place in range(2 * PATCH):
            column = place - PATCH if place < PATCH else cols + place - PATCH
            edge[8 * turn + place] = np.abs(np.arange(cols) - column) <= PATCH
    return np.concatenate([main, main, edge, edge], 0)


def select_matrix():
    pick = np.zeros((LANES, 2 * LANES), np.float32)
    for turn in range(SPAN):
        for place in range(2 * PATCH):
            lane = 32 + place - PATCH if place < PATCH else 96 + place - PATCH
            pick[lane, 8 * turn + place] = 1.0
            pick[lane + turn - SEARCH, LANES + 8 * turn + place] = 1.0
    return np.concatenate([pick] * 3, 0)


def gain(feature):
    if feature == 2 * CHANS:
        return -6.0
    return 1.0 if feature % CHANS < 3 else 2.0


def partner(feature):
    if feature == 2 * CHANS:
        return feature
    return (feature + CHANS) % (2 * CHANS)


def despeckle(
    sizes, offs_ref, field_ref, band_ref, pick_ref, out_ref,
    above_ref, below_ref, left_ref, right_ref, packs, send_sems, recv_sems, feats, moved, own, edges, edge_own, edge_other, edge_dist, edge_sum, dist, sums, weights, totals,
):
    rows, cols, row_total, col_total = sizes
    span_rows = rows + 2 * PAD
    row_tiles = span_rows // 8
    halves = cols // LANES
    dist_rows = rows + 8
    lane = lax.broadcasted_iota(jnp.int32, (8, LANES), 1)
    sub = lax.broadcasted_iota(jnp.int32, (8, LANES), 0)
    row_start, col_start = lax.axis_index("rows") * rows, lax.axis_index("offs") * cols
    swap_halo(field_ref, above_ref, below_ref, left_ref, right_ref, packs, send_sems, recv_sems)
    f32, bf16 = jnp.float32, jnp.bfloat16

    def features(source_ref, first, tile, _):
        at = pl.ds(pl.multiple_of(tile * 8, 8), 8)
        source_at = pl.ds(pl.multiple_of(tile * 8 - first, 8), 8)
        row = tile * 8 - PAD + sub
        in_rows = (row >= -RIM) & (row < rows + RIM) & (row + row_start >= 0) & (row + row_start < row_total)
        for group in range(halves + 2):
            col = (group - 1) * LANES + lane
            inside = (
                in_rows & (col >= -RIM) & (col < cols + RIM)
                & (col + col_start >= 0) & (col + col_start < col_total)
            )
            if group == 0:
                packed = left_ref[at, :]
                cells = [pltpu.roll(packed, LANES - RIM - RIM * c, 1) for c in range(CHANS)]
            elif group == halves + 1:
                packed = right_ref[at, :]
                cells = [pltpu.roll(packed, LANES - RIM * c, 1) if c else packed for c in range(CHANS)]
            else:
                cells = [source_ref[c, source_at, (group - 1) * LANES : group * LANES] for c in range(CHANS)]
            adjugate, determinant = hermitian_inverse(cells)
            scale = 1.0 / determinant
            for c in range(CHANS):
                feats[group, c, at, :] = jnp.where(inside, cells[c], 0.0)
                feats[group, CHANS + c, at, :] = jnp.where(inside, adjugate[c] * scale, 0.0)
            feats[group, 2 * CHANS, at, :] = jnp.where(inside, 1.0, 0.0)
        return 0

    head, tail = PAD // 8, (PAD + rows) // 8
    lax.fori_loop(0, head, functools.partial(features, above_ref, 0), 0)
    lax.fori_loop(head, tail, functools.partial(features, field_ref, PAD), 0)
    lax.fori_loop(tail, row_tiles, functools.partial(features, below_ref, PAD + rows), 0)

    def split(value):
        high = value.astype(bf16)
        return high, (value - high.astype(f32)).astype(bf16)

    def shifts(tile, _):
        at = pl.ds(pl.multiple_of(tile * 8, 8), 8)
        for c in range(FEATS):
            cells = [feats[group, c, at, :] for group in range(halves + 2)]
            for step in range(-SEARCH, SEARCH + 1):
                for half in range(halves):
                    here = cells[half + 1]
                    if step > 0:
                        value = pltpu.roll(jnp.where(lane >= step, here, cells[half + 2]), LANES - step, 1)
                    elif step < 0:
                        value = pltpu.roll(jnp.where(lane < LANES + step, here, cells[half]), -step, 1)
                    else:
                        value = here
                    moved[step + SEARCH, half, c, at, :] = value
            near = pltpu.roll(jnp.where(lane >= 96, cells[0], cells[1]), 32, 1)
            far = pltpu.roll(jnp.where(lane >= 96, cells[halves], cells[halves + 1]), 96, 1)
            edges[pl.ds(pl.multiple_of(c * span_rows + tile * 8, 8), 8), :] = jnp.where(lane < 64, near, far)
        return 0

    lax.fori_loop(0, row_tiles, shifts, 0)

    def edge_pick(c, _):
        value = edges[pl.ds(pl.multiple_of(c * span_rows, 8), span_rows), :]
        high, rest = value.astype(bf16), value - value.astype(bf16).astype(f32)
        middle, low = split(rest)
        parts = jnp.concatenate([high, middle, low], 1)
        both = jnp.dot(parts, pick_ref[...], preferred_element_type=f32)
        edge_own[c, :span_rows] = both[:, :LANES]
        edge_other[c, :span_rows] = both[:, LANES:]
        return 0

    lax.fori_loop(0, FEATS, edge_pick, 0)

    def own_tiles(tile, _):
        at = pl.ds(pl.multiple_of(tile * 8, 8), 8)
        for half in range(halves):
            for c in range(FEATS):
                own[half, c, at, :] = gain(c) * feats[half + 1, partner(c), pl.ds(tile * 8 + PAD - PATCH, 8), :]
        return 0

    lax.fori_loop(0, dist_rows // 8, own_tiles, 0)

    def edge_tiles(tile, _):
        at = pl.ds(pl.multiple_of(tile * 8, 8), 8)
        mine = [gain(c) * edge_own[partner(c), pl.ds(tile * 8 + PAD - PATCH, 8), :] for c in range(FEATS)]
        for step in range(SPAN):
            value = None
            for c in range(FEATS):
                term = mine[c] * edge_other[c, pl.ds(tile * 8 + PAD - PATCH - SEARCH + step, 8), :]
                value = term if value is None else value + term
            edge_dist[step, at, :] = value
        return 0

    lax.fori_loop(0, dist_rows // 8, edge_tiles, 0)

    def edge_sums(step, _):
        for part in range(rows // 16):
            value = edge_dist[step, pl.ds(16 * part, 16), :]
            for s in range(1, SIDE):
                value = value + edge_dist[step, pl.ds(16 * part + s, 16), :]
            high, low = split(value)
            edge_sum[step, 16 * part : 16 * part + 16, :LANES] = high
            edge_sum[step, 16 * part : 16 * part + 16, LANES:] = low
        return 0

    lax.fori_loop(0, SPAN, edge_sums, 0)
    totals[...] = jnp.zeros_like(totals)
    edge_lane = lax.broadcasted_iota(jnp.int32, (16, LANES), 1)

    def batch(turn, _):
        downs = [offs_ref[turn * BATCH + j, 0] for j in range(BATCH)]
        sides = [offs_ref[turn * BATCH + j, 1] + SEARCH for j in range(BATCH)]

        def distances(step, _):
            half, tile = step % halves, step // halves
            at = pl.ds(pl.multiple_of(tile * 8, 8), 8)
            mine = [own[half, c, at, :] for c in range(FEATS)]
            for j in range(BATCH):
                rows_at = pl.ds(tile * 8 + PAD - PATCH + downs[j], 8)
                value = None
                for c in range(FEATS):
                    term = mine[c] * moved[sides[j], half, c, rows_at, :]
                    value = term if value is None else value + term
                dist[j, half, at, :] = value
            return 0

        lax.fori_loop(0, halves * dist_rows // 8, distances, 0)

        def window(j, _):
            down = offs_ref[turn * BATCH + j, 0] + SEARCH
            side = offs_ref[turn * BATCH + j, 1] + SEARCH
            keep = jnp.where(edge_lane // 8 == side, 1.0, 0.0).astype(bf16)
            for part in range(rows // 16):
                at = pl.ds(pl.multiple_of(j * rows + 16 * part, 16), 16)
                for half in range(halves):
                    value = dist[j, half, pl.ds(16 * part, 16), :]
                    for s in range(1, SIDE):
                        value = value + dist[j, half, pl.ds(16 * part + s, 16), :]
                    high, low = split(value)
                    sums[at, half * LANES : (half + 1) * LANES] = high
                    sums[at, cols + half * LANES : cols + (half + 1) * LANES] = low
                for k in range(2):
                    sums[at, 2 * cols + k * LANES : 2 * cols + (k + 1) * LANES] = (
                        edge_sum[down, 16 * part : 16 * part + 16, k * LANES : (k + 1) * LANES] * keep
                    )
            return 0

        lax.fori_loop(0, BATCH, window, 0)

        patch = jnp.dot(sums[...], band_ref[...], preferred_element_type=f32)
        weights[...] = jnp.exp2(patch * EXPONENT)

        def accumulate(tile, _):
            at = pl.ds(pl.multiple_of(tile * 8, 8), 8)
            for half in range(halves):
                total = [totals[half, c, at, :] for c in range(CHANS + 1)]
                for j in range(BATCH):
                    rows_at = pl.ds(tile * 8 + PAD + downs[j], 8)
                    weight = weights[
                        pl.ds(pl.multiple_of(j * rows + tile * 8, 8), 8), half * LANES : (half + 1) * LANES
                    ]
                    for c in range(CHANS):
                        total[c] = total[c] + weight * moved[sides[j], half, c, rows_at, :]
                    total[CHANS] = total[CHANS] + weight * moved[sides[j], half, 2 * CHANS, rows_at, :]
                for c in range(CHANS + 1):
                    totals[half, c, at, :] = total[c]
            return 0

        lax.fori_loop(0, rows // 8, accumulate, 0)
        return 0

    lax.fori_loop(0, offs_ref.shape[0] // BATCH, batch, 0)

    def finish(tile, _):
        at = pl.ds(pl.multiple_of(tile * 8, 8), 8)
        for half in range(halves):
            span = slice(half * LANES, (half + 1) * LANES)
            scale = 1.0 / (1.0 + totals[half, CHANS, at, :])
            for c in range(CHANS):
                out_ref[c, at, span] = (field_ref[c, at, span] + totals[half, c, at, :]) * scale
        return 0

    lax.fori_loop(0, rows // 8, finish, 0)


def swap_halo(field_ref, above_ref, below_ref, left_ref, right_ref, packs, send_sems, recv_sems):
    rows, cols = field_ref.shape[1:]
    row, col = lax.axis_index("rows"), lax.axis_index("offs")
    row_count, col_count = lax.axis_size("rows"), lax.axis_size("offs")

    def device(down, side):
        return (lax.rem(row + down + row_count, row_count), lax.rem(col + side + col_count, col_count))

    around = [(down, side) for down in (-1, 0, 1) for side in (-1, 0, 1) if (down, side) != (0, 0)]
    barrier = pltpu.get_barrier_semaphore()
    for down, side in around:
        pl.semaphore_signal(barrier, inc=1, device_id=device(down, side), device_id_type=pl.DeviceIdType.MESH)

    lane = lax.broadcasted_iota(jnp.int32, (rows, LANES), 1)
    first = field_ref[0, :, :LANES]
    last = pltpu.roll(field_ref[0, :, cols - LANES :], RIM, 1)
    for c in range(1, CHANS):
        here = (lane >= RIM * c) & (lane < RIM * (c + 1))
        first = jnp.where(here, pltpu.roll(field_ref[c, :, :LANES], RIM * c, 1), first)
        last = jnp.where(here, pltpu.roll(field_ref[c, :, cols - LANES :], (RIM * c + RIM) % LANES, 1), last)
    packs[0] = first
    packs[1] = last
    pl.semaphore_wait(barrier, len(around))

    copies = []
    for k, (down, side) in enumerate(around):
        start, size, put = {-1: (0, PAD, PAD + rows), 0: (0, rows, PAD), 1: (rows - PAD, PAD, 0)}[down]
        if side == 0:
            source = field_ref.at[:, start : start + size, :]
            target = below_ref if down < 0 else above_ref
        else:
            source = packs.at[0 if side < 0 else 1, start : start + size, :]
            target = (right_ref if side < 0 else left_ref).at[put : put + size, :]
        copies.append(pltpu.make_async_remote_copy(
            src_ref=source, dst_ref=target, send_sem=send_sems.at[k], recv_sem=recv_sems.at[k],
            device_id=device(down, side), device_id_type=pl.DeviceIdType.MESH,
        ))
    for copy in copies:
        copy.start()
    for copy in copies:
        copy.wait()


def filter_block(sizes, offsets, field):
    rows, cols = sizes[:2]
    span_rows = rows + 2 * PAD
    halves = cols // LANES
    vmem = pl.BlockSpec(memory_space=pltpu.VMEM)
    smem = pl.BlockSpec(memory_space=pltpu.SMEM)
    f32, bf16 = jnp.float32, jnp.bfloat16
    return pl.pallas_call(
        functools.partial(despeckle, sizes),
        out_shape=jax.ShapeDtypeStruct((CHANS, rows, cols), f32),
        in_specs=[smem] + [vmem] * 3,
        out_specs=vmem,
        scratch_shapes=[
            pltpu.VMEM((CHANS, PAD, cols), f32),
            pltpu.VMEM((CHANS, PAD, cols), f32),
            pltpu.VMEM((span_rows, LANES), f32),
            pltpu.VMEM((span_rows, LANES), f32),
            pltpu.VMEM((2, rows, LANES), f32),
            pltpu.SemaphoreType.DMA((8,)),
            pltpu.SemaphoreType.DMA((8,)),
            pltpu.VMEM((halves + 2, FEATS, span_rows + BANKS, LANES), f32),
            pltpu.VMEM((SPAN, halves, FEATS, span_rows + BANKS, LANES), f32),
            pltpu.VMEM((halves, FEATS, rows + BANKS, LANES), f32),
            pltpu.VMEM((FEATS * span_rows, LANES), f32),
            pltpu.VMEM((FEATS, span_rows + BANKS, LANES), f32),
            pltpu.VMEM((FEATS, span_rows + BANKS, LANES), f32),
            pltpu.VMEM((SPAN, rows + 8, LANES), f32),
            pltpu.VMEM((SPAN, rows, 2 * LANES), bf16),
            pltpu.VMEM((BATCH, halves, rows + 8, LANES), f32),
            pltpu.VMEM((BATCH * rows, 2 * cols + 2 * LANES), bf16),
            pltpu.VMEM((BATCH * rows, cols), f32),
            pltpu.VMEM((halves, CHANS + 1, rows + BANKS, LANES), f32),
        ],
        compiler_params=pltpu.CompilerParams(
            vmem_limit_bytes=56 * 1024 * 1024, collective_id=0, has_side_effects=True
        ),
    )(
        offsets, field, jnp.asarray(band_matrix(cols), bf16), jnp.asarray(select_matrix(), bf16),
    )


def per_device(coherency_field, offsets):
    _, rows, cols = coherency_field.shape
    row_total = rows * lax.axis_size("rows")
    col_total = cols * lax.axis_size("offs")
    return filter_block((rows, cols, row_total, col_total), offsets, coherency_field)


def solution(mesh):
    in_specs = (P(None, "rows", "offs"), P())
    out_specs = P(None, "rows", "offs")
    return jax.shard_map(
        per_device, mesh=mesh, in_specs=in_specs, out_specs=out_specs, check_vma=False
    )
```

```python
import functools
import math

import jax
import jax.numpy as jnp
import numpy as np
from jax import lax
from jax.experimental import pallas as pl
from jax.experimental.pallas import tpu as pltpu
from jax.sharding import PartitionSpec as P

SEARCH = 6
PATCH = 3
SIDE = 2 * PATCH + 1
SPAN = 2 * SEARCH + 1
RIM = SEARCH + PATCH
STRENGTH = 1.5
LANES = 128
PAD = 16
CHANS = 9
FEATS = 2 * CHANS + 1
BATCH = 24
GROUP = 12
BANKS = 16
EXPONENT = -math.log2(math.e) / (STRENGTH * SIDE * SIDE)


def hermitian_inverse(matrix):
    diag_one, diag_two, diag_three = matrix[0], matrix[1], matrix[2]
    re_onetwo, re_onethree, re_twothree = matrix[3], matrix[4], matrix[5]
    im_onetwo, im_onethree, im_twothree = matrix[6], matrix[7], matrix[8]
    abs_onetwo = re_onetwo * re_onetwo + im_onetwo * im_onetwo
    abs_onethree = re_onethree * re_onethree + im_onethree * im_onethree
    abs_twothree = re_twothree * re_twothree + im_twothree * im_twothree
    yz_real = re_onethree * re_twothree + im_onethree * im_twothree
    yz_imag = im_onethree * re_twothree - re_onethree * im_twothree
    xz_real = re_onetwo * re_twothree - im_onetwo * im_twothree
    xz_imag = re_onetwo * im_twothree + im_onetwo * re_twothree
    yx_real = re_onethree * re_onetwo + im_onethree * im_onetwo
    yx_imag = im_onethree * re_onetwo - re_onethree * im_onetwo
    triple_real = xz_real * re_onethree + xz_imag * im_onethree
    determinant = (
        diag_one * diag_two * diag_three
        + 2.0 * triple_real
        - diag_one * abs_twothree
        - diag_two * abs_onethree
        - diag_three * abs_onetwo
    )
    adjugate = [
        diag_two * diag_three - abs_twothree,
        diag_one * diag_three - abs_onethree,
        diag_one * diag_two - abs_onetwo,
        -(re_onetwo * diag_three - yz_real),
        xz_real - re_onethree * diag_two,
        -(diag_one * re_twothree - yx_real),
        -(im_onetwo * diag_three - yz_imag),
        xz_imag - im_onethree * diag_two,
        -(diag_one * im_twothree - yx_imag),
    ]
    return adjugate, determinant


def edge_pairs(cols):
    pairs = []
    for step in range(-SEARCH, SEARCH + 1):
        for column in range(-PATCH, cols + PATCH):
            if not (0 <= column < cols and 0 <= column + step < cols):
                pairs.append((step, column))
    return pairs


def band_matrix(cols):
    source = np.arange(cols)[:, None]
    target = np.arange(cols)[None, :]
    main = (np.abs(source - target) <= PATCH).astype(np.float32)
    edge = np.zeros((LANES, cols), np.float32)
    for lane, (_, column) in enumerate(edge_pairs(cols)):
        edge[lane] = np.abs(np.arange(cols) - column) <= PATCH
    return np.concatenate([main, main, edge, edge], 0)


def select_matrix(cols):
    pick = np.zeros((LANES, 2 * LANES), np.float32)
    for lane, (step, column) in enumerate(edge_pairs(cols)):
        source = column + 32 if column < 32 else column - cols + 96
        pick[source, lane] = 1.0
        pick[source + step, LANES + lane] = 1.0
    return np.concatenate([pick] * 3, 0)


def keep_masks(cols):
    keep = np.zeros((SPAN, 16, LANES), np.float32)
    for lane, (step, _) in enumerate(edge_pairs(cols)):
        keep[step + SEARCH, :, lane] = 1.0
    return keep


def gain(feature):
    if feature == 2 * CHANS:
        return -6.0
    return 1.0 if feature % CHANS < 3 else 2.0


def partner(feature):
    if feature == 2 * CHANS:
        return feature
    return (feature + CHANS) % (2 * CHANS)


def despeckle(
    sizes, offs_ref, field_ref, band_ref, pick_ref, keep_ref, out_ref,
    above_ref, below_ref, left_ref, right_ref, packs, send_sems, recv_sems,
    feats, moved, own, edges, edge_own, edge_other, edge_dist, edge_sum, dist, sums, weights, totals,
):
    rows, cols, row_total, col_total = sizes
    span_rows = rows + 2 * PAD
    edge_rows = edges.shape[0] // FEATS
    row_tiles = span_rows // 8
    head, tail = PAD // 8, (PAD + rows) // 8
    halves = cols // LANES
    dist_tiles = (rows + 8) // 8
    near_tile, far_tile = 2, dist_tiles - 2
    count = offs_ref.shape[0]
    lane = lax.broadcasted_iota(jnp.int32, (8, LANES), 1)
    sub = lax.broadcasted_iota(jnp.int32, (8, LANES), 0)
    row, col = lax.axis_index("rows"), lax.axis_index("offs")
    row_start, col_start = row * rows, col * cols
    row_count, col_count = lax.axis_size("rows"), lax.axis_size("offs")
    f32, bf16 = jnp.float32, jnp.bfloat16

    def device(down, side):
        return (lax.rem(row + down + row_count, row_count), lax.rem(col + side + col_count, col_count))

    around = [(down, side) for down in (-1, 0, 1) for side in (-1, 0, 1) if (down, side) != (0, 0)]
    barrier = pltpu.get_barrier_semaphore()
    for down, side in around:
        pl.semaphore_signal(barrier, inc=1, device_id=device(down, side), device_id_type=pl.DeviceIdType.MESH)

    def pack(tile, _):
        at = pl.ds(pl.multiple_of(tile * 8, 8), 8)
        first = field_ref[0, at, :LANES]
        last = pltpu.roll(field_ref[0, at, cols - LANES :], RIM, 1)
        for c in range(1, CHANS):
            here = (lane >= RIM * c) & (lane < RIM * (c + 1))
            first = jnp.where(here, pltpu.roll(field_ref[c, at, :LANES], RIM * c, 1), first)
            last = jnp.where(here, pltpu.roll(field_ref[c, at, cols - LANES :], (RIM * c + RIM) % LANES, 1), last)
        packs[0, at, :] = first
        packs[1, at, :] = last
        return 0

    lax.fori_loop(0, rows // 8, pack, 0)

    copies = []
    for k, (down, side) in enumerate(around):
        start, size, put = {-1: (0, PAD, PAD + rows), 0: (0, rows, PAD), 1: (rows - PAD, PAD, 0)}[down]
        if side == 0:
            source = field_ref.at[:, start : start + size, :]
            target = below_ref if down < 0 else above_ref
        else:
            source = packs.at[0 if side < 0 else 1, start : start + size, :]
            target = (right_ref if side < 0 else left_ref).at[put : put + size, :]
        copies.append(pltpu.make_async_remote_copy(
            src_ref=source, dst_ref=target, send_sem=send_sems.at[k], recv_sem=recv_sems.at[k],
            device_id=device(down, side), device_id_type=pl.DeviceIdType.MESH,
        ))

    def features(source_ref, first, groups, tile, _):
        at = pl.ds(pl.multiple_of(tile * 8, 8), 8)
        source_at = pl.ds(pl.multiple_of(tile * 8 - first, 8), 8)
        place = tile * 8 - PAD + sub
        in_rows = (place >= -RIM) & (place < rows + RIM) & (place + row_start >= 0) & (place + row_start < row_total)
        for group in groups:
            column = (group - 1) * LANES + lane
            inside = (
                in_rows & (column >= -RIM) & (column < cols + RIM)
                & (column + col_start >= 0) & (column + col_start < col_total)
            )
            if group == 0:
                packed = left_ref[at, :]
                cells = [pltpu.roll(packed, LANES - RIM - RIM * c, 1) for c in range(CHANS)]
            elif group == halves + 1:
                packed = right_ref[at, :]
                cells = [pltpu.roll(packed, LANES - RIM * c, 1) if c else packed for c in range(CHANS)]
            else:
                cells = [source_ref[c, source_at, (group - 1) * LANES : group * LANES] for c in range(CHANS)]
            adjugate, determinant = hermitian_inverse(cells)
            scale = 1.0 / determinant
            for c in range(CHANS):
                feats[group, c, at, :] = jnp.where(inside, cells[c], 0.0)
                feats[group, CHANS + c, at, :] = jnp.where(inside, adjugate[c] * scale, 0.0)
            feats[group, 2 * CHANS, at, :] = jnp.where(inside, 1.0, 0.0)
        return 0

    def shifts(tile, _):
        at = pl.ds(pl.multiple_of(tile * 8, 8), 8)
        for c in range(FEATS):
            zero = jnp.zeros((8, LANES), f32)
            cells = [zero] + [feats[half + 1, c, at, :] for half in range(halves)] + [zero]
            for step in range(-SEARCH, SEARCH + 1):
                for half in range(halves):
                    here = cells[half + 1]
                    if step > 0:
                        value = pltpu.roll(jnp.where(lane >= step, here, cells[half + 2]), LANES - step, 1)
                    elif step < 0:
                        value = pltpu.roll(jnp.where(lane < LANES + step, here, cells[half]), -step, 1)
                    else:
                        value = here
                    moved[step + SEARCH, half, c, at, :] = value
        return 0

    def own_tiles(tile, _):
        at = pl.ds(pl.multiple_of(tile * 8, 8), 8)
        for half in range(halves):
            for c in range(FEATS):
                own[half, c, at, :] = gain(c) * feats[half + 1, partner(c), pl.ds(tile * 8 + PAD - PATCH, 8), :]
        return 0

    def distances(turn, downs, sides, step, _):
        half, tile = step % halves, step // halves
        at = pl.ds(pl.multiple_of(tile * 8, 8), 8)
        mine = [own[half, c, at, :] for c in range(FEATS)]
        for j in range(BATCH):
            rows_at = pl.ds(tile * 8 + PAD - PATCH + downs[j], 8)
            value = None
            for c in range(FEATS):
                term = mine[c] * moved[sides[j], half, c, rows_at, :]
                value = term if value is None else value + term
            dist[turn * BATCH + j, half, at, :] = value
        return 0

    def distance_batch(spans, turn, _):
        downs = [offs_ref[turn * BATCH + j, 0] for j in range(BATCH)]
        sides = [offs_ref[turn * BATCH + j, 1] + SEARCH for j in range(BATCH)]
        for start, stop in spans:
            lax.fori_loop(start * halves, stop * halves, functools.partial(distances, turn, downs, sides), 0)
        return 0

    inner = tuple(range(1, halves + 1))
    lax.fori_loop(head, tail, functools.partial(features, field_ref, PAD, inner), 0)
    lax.fori_loop(head, tail, shifts, 0)
    lax.fori_loop(near_tile, far_tile, own_tiles, 0)
    pl.semaphore_wait(barrier, len(around))
    for copy in copies:
        copy.start()
    lax.fori_loop(0, count // BATCH, functools.partial(distance_batch, ((near_tile, far_tile),)), 0)
    for copy in copies:
        copy.wait()

    outer = (0, halves + 1)
    lax.fori_loop(0, head, functools.partial(features, above_ref, 0, outer + inner), 0)
    lax.fori_loop(head, tail, functools.partial(features, field_ref, PAD, outer), 0)
    lax.fori_loop(tail, row_tiles, functools.partial(features, below_ref, PAD + rows, outer + inner), 0)
    lax.fori_loop(0, head, shifts, 0)
    lax.fori_loop(tail, row_tiles, shifts, 0)
    lax.fori_loop(0, near_tile, own_tiles, 0)
    lax.fori_loop(far_tile, dist_tiles, own_tiles, 0)
    late = ((0, near_tile), (far_tile, dist_tiles))
    lax.fori_loop(0, count // BATCH, functools.partial(distance_batch, late), 0)

    def split(value):
        high = value.astype(bf16)
        return high, (value - high.astype(f32)).astype(bf16)

    def patches(tile, _):
        at = pl.ds(pl.multiple_of(tile * 8, 8), 8)
        for c in range(FEATS):
            cells = [feats[group, c, at, :] for group in range(halves + 2)]
            before = pltpu.roll(jnp.where(lane >= 96, cells[0], cells[1]), 32, 1)
            after = pltpu.roll(jnp.where(lane >= 96, cells[halves], cells[halves + 1]), 96, 1)
            value = jnp.where(lane < 64, before, after)
            high, rest = value.astype(bf16), value - value.astype(bf16).astype(f32)
            middle, low = split(rest)
            edge_at = pl.ds(pl.multiple_of(c * edge_rows + tile * 8, 8), 8)
            edges[edge_at, :LANES] = high.astype(f32)
            edges[edge_at, LANES : 2 * LANES] = middle.astype(f32)
            edges[edge_at, 2 * LANES :] = low.astype(f32)
            if c < CHANS or c == 2 * CHANS:
                for step in range(1, SEARCH + 1):
                    up, down = (step + SEARCH, halves - 1, c, at), (SEARCH - step, 0, c, at)
                    moved[up] = jnp.where(
                        lane >= LANES - step, pltpu.roll(cells[halves + 1], LANES - step, 1), moved[up]
                    )
                    moved[down] = jnp.where(lane < step, pltpu.roll(cells[0], step, 1), moved[down])
        return 0

    lax.fori_loop(0, row_tiles, patches, 0)

    def edge_pick(c, _):
        at = pl.ds(pl.multiple_of(c * edge_rows, 8), edge_rows)
        both = jnp.dot(edges[at, :].astype(bf16), pick_ref[...], preferred_element_type=f32)
        edge_own[at, :] = both[:, :LANES]
        edge_other[at, :] = both[:, LANES:]
        return 0

    lax.fori_loop(0, FEATS, edge_pick, 0)

    def edge_tiles(tile, _):
        at = pl.ds(pl.multiple_of(tile * 8, 8), 8)
        mine = [
            gain(c) * edge_own[pl.ds(partner(c) * edge_rows + tile * 8 + PAD - PATCH, 8), :]
            for c in range(FEATS)
        ]
        for step in range(SPAN):
            value = None
            for c in range(FEATS):
                rows_at = pl.ds(c * edge_rows + tile * 8 + PAD - PATCH - SEARCH + step, 8)
                term = mine[c] * edge_other[rows_at, :]
                value = term if value is None else value + term
            edge_dist[step, at, :] = value
        return 0

    lax.fori_loop(0, dist_tiles, edge_tiles, 0)

    def edge_sums(step, _):
        for part in range(rows // 16):
            value = edge_dist[step, pl.ds(16 * part, 16), :]
            for s in range(1, SIDE):
                value = value + edge_dist[step, pl.ds(16 * part + s, 16), :]
            high, low = split(value)
            edge_sum[step, 16 * part : 16 * part + 16, :LANES] = high
            edge_sum[step, 16 * part : 16 * part + 16, LANES:] = low
        return 0

    lax.fori_loop(0, SPAN, edge_sums, 0)
    totals[...] = jnp.zeros_like(totals)

    def batch(turn, _):
        downs = [offs_ref[turn * GROUP + j, 0] for j in range(GROUP)]
        sides = [offs_ref[turn * GROUP + j, 1] + SEARCH for j in range(GROUP)]

        def window(j, _):
            k = turn * GROUP + j
            down = offs_ref[k, 0] + SEARCH
            keep = keep_ref[offs_ref[k, 1] + SEARCH]
            for part in range(rows // 16):
                at = pl.ds(pl.multiple_of(j * rows + 16 * part, 16), 16)
                for half in range(halves):
                    value = dist[k, half, pl.ds(16 * part, 16), :]
                    for s in range(1, SIDE):
                        value = value + dist[k, half, pl.ds(16 * part + s, 16), :]
                    high, low = split(value)
                    sums[at, half * LANES : (half + 1) * LANES] = high
                    sums[at, cols + half * LANES : cols + (half + 1) * LANES] = low
                for k2 in range(2):
                    sums[at, 2 * cols + k2 * LANES : 2 * cols + (k2 + 1) * LANES] = (
                        edge_sum[down, 16 * part : 16 * part + 16, k2 * LANES : (k2 + 1) * LANES] * keep
                    )
            return 0

        lax.fori_loop(0, GROUP, window, 0)

        patch = jnp.dot(sums[...], band_ref[...], preferred_element_type=f32)
        weights[...] = jnp.exp2(patch * EXPONENT)

        def accumulate(tile, _):
            at = pl.ds(pl.multiple_of(tile * 8, 8), 8)
            for half in range(halves):
                total = [totals[half, c, at, :] for c in range(CHANS + 1)]
                for j in range(GROUP):
                    rows_at = pl.ds(tile * 8 + PAD + downs[j], 8)
                    weight = weights[
                        pl.ds(pl.multiple_of(j * rows + tile * 8, 8), 8), half * LANES : (half + 1) * LANES
                    ]
                    for c in range(CHANS):
                        total[c] = total[c] + weight * moved[sides[j], half, c, rows_at, :]
                    total[CHANS] = total[CHANS] + weight * moved[sides[j], half, 2 * CHANS, rows_at, :]
                for c in range(CHANS + 1):
                    totals[half, c, at, :] = total[c]
            return 0

        lax.fori_loop(0, rows // 8, accumulate, 0)
        return 0

    lax.fori_loop(0, count // GROUP, batch, 0)

    def finish(tile, _):
        at = pl.ds(pl.multiple_of(tile * 8, 8), 8)
        for half in range(halves):
            span = slice(half * LANES, (half + 1) * LANES)
            scale = 1.0 / (1.0 + totals[half, CHANS, at, :])
            for c in range(CHANS):
                out_ref[c, at, span] = (field_ref[c, at, span] + totals[half, c, at, :]) * scale
        return 0

    lax.fori_loop(0, rows // 8, finish, 0)


def filter_block(sizes, offsets, field):
    rows, cols = sizes[:2]
    span_rows = rows + 2 * PAD
    edge_rows = span_rows + 8
    halves = cols // LANES
    vmem = pl.BlockSpec(memory_space=pltpu.VMEM)
    smem = pl.BlockSpec(memory_space=pltpu.SMEM)
    f32, bf16 = jnp.float32, jnp.bfloat16
    return pl.pallas_call(
        functools.partial(despeckle, sizes),
        out_shape=jax.ShapeDtypeStruct((CHANS, rows, cols), f32),
        in_specs=[smem] + [vmem] * 4,
        out_specs=vmem,
        scratch_shapes=[
            pltpu.VMEM((CHANS, PAD, cols), f32),
            pltpu.VMEM((CHANS, PAD, cols), f32),
            pltpu.VMEM((span_rows, LANES), f32),
            pltpu.VMEM((span_rows, LANES), f32),
            pltpu.VMEM((2, rows, LANES), f32),
            pltpu.SemaphoreType.DMA((8,)),
            pltpu.SemaphoreType.DMA((8,)),
            pltpu.VMEM((halves + 2, FEATS, span_rows + BANKS, LANES), f32),
            pltpu.VMEM((SPAN, halves, FEATS, span_rows + BANKS, LANES), f32),
            pltpu.VMEM((halves, FEATS, rows + BANKS, LANES), f32),
            pltpu.VMEM((FEATS * edge_rows, 3 * LANES), f32),
            pltpu.VMEM((FEATS * edge_rows, LANES), f32),
            pltpu.VMEM((FEATS * edge_rows, LANES), f32),
            pltpu.VMEM((SPAN, rows + 8, LANES), f32),
            pltpu.VMEM((SPAN, rows, 2 * LANES), bf16),
            pltpu.VMEM((offsets.shape[0], halves, rows + 8, LANES), f32),
            pltpu.VMEM((GROUP * rows, 2 * cols + 2 * LANES), bf16),
            pltpu.VMEM((GROUP * rows, cols), f32),
            pltpu.VMEM((halves, CHANS + 1, rows + BANKS, LANES), f32),
        ],
        compiler_params=pltpu.CompilerParams(
            vmem_limit_bytes=62 * 1024 * 1024, collective_id=0, has_side_effects=True
        ),
    )(
        offsets, field, jnp.asarray(band_matrix(cols), bf16), jnp.asarray(select_matrix(cols), bf16),
        jnp.asarray(keep_masks(cols), bf16),
    )


def per_device(coherency_field, offsets):
    _, rows, cols = coherency_field.shape
    row_total = rows * lax.axis_size("rows")
    col_total = cols * lax.axis_size("offs")
    return filter_block((rows, cols, row_total, col_total), offsets, coherency_field)


def solution(mesh):
    in_specs = (P(None, "rows", "offs"), P())
    out_specs = P(None, "rows", "offs")
    return jax.shard_map(
        per_device, mesh=mesh, in_specs=in_specs, out_specs=out_specs, check_vma=False
    )
```

```python
import functools
import math

import jax
import jax.numpy as jnp
import numpy as np
from jax import lax
from jax.experimental import pallas as pl
from jax.experimental.pallas import tpu as pltpu
from jax.sharding import PartitionSpec as P

SEARCH = 6
PATCH = 3
SIDE = 2 * PATCH + 1
SPAN = 2 * SEARCH + 1
RIM = SEARCH + PATCH
STRENGTH = 1.5
LANES = 128
PAD = 16
CHANS = 9
FEATS = 2 * CHANS + 1
BATCH = 40
GROUP = 24
BANKS = 16
EXPONENT = -math.log2(math.e) / (STRENGTH * SIDE * SIDE)


def hermitian_inverse(matrix):
    diag_one, diag_two, diag_three = matrix[0], matrix[1], matrix[2]
    re_onetwo, re_onethree, re_twothree = matrix[3], matrix[4], matrix[5]
    im_onetwo, im_onethree, im_twothree = matrix[6], matrix[7], matrix[8]
    abs_onetwo = re_onetwo * re_onetwo + im_onetwo * im_onetwo
    abs_onethree = re_onethree * re_onethree + im_onethree * im_onethree
    abs_twothree = re_twothree * re_twothree + im_twothree * im_twothree
    yz_real = re_onethree * re_twothree + im_onethree * im_twothree
    yz_imag = im_onethree * re_twothree - re_onethree * im_twothree
    xz_real = re_onetwo * re_twothree - im_onetwo * im_twothree
    xz_imag = re_onetwo * im_twothree + im_onetwo * re_twothree
    yx_real = re_onethree * re_onetwo + im_onethree * im_onetwo
    yx_imag = im_onethree * re_onetwo - re_onethree * im_onetwo
    triple_real = xz_real * re_onethree + xz_imag * im_onethree
    determinant = (
        diag_one * diag_two * diag_three
        + 2.0 * triple_real
        - diag_one * abs_twothree
        - diag_two * abs_onethree
        - diag_three * abs_onetwo
    )
    adjugate = [
        diag_two * diag_three - abs_twothree,
        diag_one * diag_three - abs_onethree,
        diag_one * diag_two - abs_onetwo,
        -(re_onetwo * diag_three - yz_real),
        xz_real - re_onethree * diag_two,
        -(diag_one * re_twothree - yx_real),
        -(im_onetwo * diag_three - yz_imag),
        xz_imag - im_onethree * diag_two,
        -(diag_one * im_twothree - yx_imag),
    ]
    return adjugate, determinant


def edge_pairs(cols):
    pairs = []
    for step in range(-SEARCH, SEARCH + 1):
        for column in range(-PATCH, cols + PATCH):
            if not (0 <= column < cols and 0 <= column + step < cols):
                pairs.append((step, column))
    return pairs


def band_matrix(cols):
    source = np.arange(cols)[:, None]
    target = np.arange(cols)[None, :]
    main = (np.abs(source - target) <= PATCH).astype(np.float32)
    edge = np.zeros((LANES, cols), np.float32)
    for lane, (_, column) in enumerate(edge_pairs(cols)):
        edge[lane] = np.abs(np.arange(cols) - column) <= PATCH
    return np.concatenate([main, main, edge, edge], 0)


def select_matrix(cols):
    pick = np.zeros((LANES, 2 * LANES), np.float32)
    for lane, (step, column) in enumerate(edge_pairs(cols)):
        source = column + 32 if column < 32 else column - cols + 96
        pick[source, lane] = 1.0
        pick[source + step, LANES + lane] = 1.0
    return np.concatenate([pick] * 3, 0)


def keep_masks(cols):
    keep = np.zeros((SPAN, 16, LANES), np.float32)
    for lane, (step, _) in enumerate(edge_pairs(cols)):
        keep[step + SEARCH, :, lane] = 1.0
    return keep


def gain(feature):
    if feature == 2 * CHANS:
        return -6.0
    return 1.0 if feature % CHANS < 3 else 2.0


def partner(feature):
    if feature == 2 * CHANS:
        return feature
    return (feature + CHANS) % (2 * CHANS)


def despeckle(
    sizes, offs_ref, field_ref, band_ref, pick_ref, keep_ref, out_ref,
    above_ref, below_ref, left_ref, right_ref, packs, send_sems, recv_sems,
    feats, moved, own, edges, edge_own, edge_other, edge_dist, edge_sum, dist, sums, weights,
):
    rows, cols, row_total, col_total = sizes
    span_rows = rows + 2 * PAD
    edge_rows = edges.shape[0] // FEATS
    row_tiles = span_rows // 8
    head, tail = PAD // 8, (PAD + rows) // 8
    halves = cols // LANES
    dist_tiles = (rows + 8) // 8
    near_tile, far_tile = 2, dist_tiles - 2
    count = offs_ref.shape[1]
    lane = lax.broadcasted_iota(jnp.int32, (8, LANES), 1)
    sub = lax.broadcasted_iota(jnp.int32, (8, LANES), 0)
    wide_lane = lax.broadcasted_iota(jnp.int32, (16, LANES), 1)
    row, col = lax.axis_index("rows"), lax.axis_index("offs")
    row_start, col_start = row * rows, col * cols
    row_count, col_count = lax.axis_size("rows"), lax.axis_size("offs")
    f32, bf16 = jnp.float32, jnp.bfloat16

    def device(down, side):
        return (lax.rem(row + down + row_count, row_count), lax.rem(col + side + col_count, col_count))

    around = [(down, side) for down in (-1, 0, 1) for side in (-1, 0, 1) if (down, side) != (0, 0)]
    barrier = pltpu.get_barrier_semaphore()
    for down, side in around:
        pl.semaphore_signal(barrier, inc=1, device_id=device(down, side), device_id_type=pl.DeviceIdType.MESH)

    def pack(tile, _):
        at = pl.ds(pl.multiple_of(tile * 8, 8), 8)
        first = field_ref[0, at, :LANES]
        last = pltpu.roll(field_ref[0, at, cols - LANES :], RIM, 1)
        for c in range(1, CHANS):
            here = (lane >= RIM * c) & (lane < RIM * (c + 1))
            first = jnp.where(here, pltpu.roll(field_ref[c, at, :LANES], RIM * c, 1), first)
            last = jnp.where(here, pltpu.roll(field_ref[c, at, cols - LANES :], (RIM * c + RIM) % LANES, 1), last)
        packs[0, at, :] = first
        packs[1, at, :] = last
        return 0

    lax.fori_loop(0, rows // 8, pack, 0)

    copies = []
    for k, (down, side) in enumerate(around):
        start, size, put = {-1: (0, PAD, PAD + rows), 0: (0, rows, PAD), 1: (rows - PAD, PAD, 0)}[down]
        if side == 0:
            source = field_ref.at[:, start : start + size, :]
            target = below_ref if down < 0 else above_ref
        else:
            source = packs.at[0 if side < 0 else 1, start : start + size, :]
            target = (right_ref if side < 0 else left_ref).at[put : put + size, :]
        copies.append(pltpu.make_async_remote_copy(
            src_ref=source, dst_ref=target, send_sem=send_sems.at[k], recv_sem=recv_sems.at[k],
            device_id=device(down, side), device_id_type=pl.DeviceIdType.MESH,
        ))

    def features(source_ref, first, groups, tile, _):
        at = pl.ds(pl.multiple_of(tile * 8, 8), 8)
        source_at = pl.ds(pl.multiple_of(tile * 8 - first, 8), 8)
        place = tile * 8 - PAD + sub
        in_rows = (place >= -RIM) & (place < rows + RIM) & (place + row_start >= 0) & (place + row_start < row_total)
        for group in groups:
            column = (group - 1) * LANES + lane
            inside = (
                in_rows & (column >= -RIM) & (column < cols + RIM)
                & (column + col_start >= 0) & (column + col_start < col_total)
            )
            if group == 0:
                packed = left_ref[at, :]
                cells = [pltpu.roll(packed, LANES - RIM - RIM * c, 1) for c in range(CHANS)]
            elif group == halves + 1:
                packed = right_ref[at, :]
                cells = [pltpu.roll(packed, LANES - RIM * c, 1) if c else packed for c in range(CHANS)]
            else:
                cells = [source_ref[c, source_at, (group - 1) * LANES : group * LANES] for c in range(CHANS)]
            adjugate, determinant = hermitian_inverse(cells)
            scale = 1.0 / determinant
            for c in range(CHANS):
                feats[group, c, at, :] = jnp.where(inside, cells[c], 0.0)
                feats[group, CHANS + c, at, :] = jnp.where(inside, adjugate[c] * scale, 0.0)
            feats[group, 2 * CHANS, at, :] = jnp.where(inside, 1.0, 0.0)
        return 0

    def shifts(tile, _):
        at = pl.ds(pl.multiple_of(tile * 8, 8), 8)
        zero = jnp.zeros((8, LANES), f32)
        for step in range(-SEARCH, SEARCH + 1):
            for half in range(halves):
                partner_col = half * LANES + lane + step
                moved[step + SEARCH, half, 2 * CHANS, at, :] = jnp.where(
                    (partner_col >= 0) & (partner_col < cols), feats[half + 1, 2 * CHANS, at, :], 0.0
                )
        for c in range(2 * CHANS):
            cells = [zero] + [feats[half + 1, c, at, :] for half in range(halves)] + [zero]
            for step in range(-SEARCH, SEARCH + 1):
                for half in range(halves):
                    here = cells[half + 1]
                    if step > 0:
                        value = pltpu.roll(jnp.where(lane >= step, here, cells[half + 2]), LANES - step, 1)
                    elif step < 0:
                        value = pltpu.roll(jnp.where(lane < LANES + step, here, cells[half]), -step, 1)
                    else:
                        value = here
                    moved[step + SEARCH, half, c, at, :] = value
        return 0

    def own_tiles(tile, _):
        at = pl.ds(pl.multiple_of(tile * 8, 8), 8)
        for half in range(halves):
            for c in range(FEATS):
                own[half, c, at, :] = gain(c) * feats[half + 1, partner(c), pl.ds(tile * 8 + PAD - PATCH, 8), :]
        return 0

    def distances(turn, downs, sides, step, _):
        half, tile = step % halves, step // halves
        at = pl.ds(pl.multiple_of(tile * 8, 8), 8)
        mine = [own[half, c, at, :] for c in range(FEATS)]
        for j in range(BATCH):
            rows_at = pl.ds(tile * 8 + PAD - PATCH + downs[j], 8)
            terms = [None, None]
            for c in range(FEATS):
                term = mine[c] * moved[sides[j], half, c, rows_at, :]
                terms[c % 2] = term if terms[c % 2] is None else terms[c % 2] + term
            dist[turn * BATCH + j, half, at, :] = terms[0] + terms[1]
        return 0

    def distance_batch(spans, turn, _):
        downs = [offs_ref[0, turn * BATCH + j] for j in range(BATCH)]
        sides = [offs_ref[1, turn * BATCH + j] + SEARCH for j in range(BATCH)]
        for start, stop in spans:
            lax.fori_loop(start * halves, stop * halves, functools.partial(distances, turn, downs, sides), 0)
        return 0

    inner = tuple(range(1, halves + 1))
    lax.fori_loop(head, tail, functools.partial(features, field_ref, PAD, inner), 0)
    lax.fori_loop(head, tail - 3, shifts, 0)
    pl.semaphore_wait(barrier, len(around))
    for copy in copies:
        copy.start()
    lax.fori_loop(tail - 3, tail, shifts, 0)
    lax.fori_loop(near_tile, far_tile, own_tiles, 0)
    lax.fori_loop(0, count // BATCH, functools.partial(distance_batch, ((near_tile, far_tile),)), 0)
    for copy in copies:
        copy.wait()

    outer = (0, halves + 1)
    lax.fori_loop(0, head, functools.partial(features, above_ref, 0, outer + inner), 0)
    lax.fori_loop(head, tail, functools.partial(features, field_ref, PAD, outer), 0)
    lax.fori_loop(tail, row_tiles, functools.partial(features, below_ref, PAD + rows, outer + inner), 0)
    lax.fori_loop(0, head, shifts, 0)
    lax.fori_loop(tail, row_tiles, shifts, 0)
    lax.fori_loop(0, near_tile, own_tiles, 0)
    lax.fori_loop(far_tile, dist_tiles, own_tiles, 0)
    late = ((0, near_tile), (far_tile, dist_tiles))
    lax.fori_loop(0, count // BATCH, functools.partial(distance_batch, late), 0)

    def split(value):
        high = value.astype(bf16)
        return high, (value - high.astype(f32)).astype(bf16)

    def patches(tile, _):
        at = pl.ds(pl.multiple_of(tile * 16, 16), 16)
        for c in range(FEATS):
            cells = [feats[group, c, at, :] for group in range(halves + 2)]
            before = pltpu.roll(jnp.where(wide_lane >= 96, cells[0], cells[1]), 32, 1)
            after = pltpu.roll(jnp.where(wide_lane >= 96, cells[halves], cells[halves + 1]), 96, 1)
            value = jnp.where(wide_lane < 64, before, after)
            high = value.astype(bf16)
            middle, low = split(value - high.astype(f32))
            edge_at = pl.ds(pl.multiple_of(c * edge_rows + tile * 16, 16), 16)
            edges[edge_at, :LANES] = high
            edges[edge_at, LANES : 2 * LANES] = middle
            edges[edge_at, 2 * LANES :] = low
            if c < CHANS or c == 2 * CHANS:
                for step in range(1, SEARCH + 1):
                    up, down = (step + SEARCH, halves - 1, c, at), (SEARCH - step, 0, c, at)
                    moved[up] = jnp.where(
                        wide_lane >= LANES - step, pltpu.roll(cells[halves + 1], LANES - step, 1), moved[up]
                    )
                    moved[down] = jnp.where(wide_lane < step, pltpu.roll(cells[0], step, 1), moved[down])
        return 0

    lax.fori_loop(0, row_tiles // 2, patches, 0)
    both = jnp.dot(edges[...], pick_ref[...], preferred_element_type=f32)
    edge_own[...] = both[:, :LANES]
    edge_other[...] = both[:, LANES:]

    def edge_tiles(tile, _):
        at = pl.ds(pl.multiple_of(tile * 8, 8), 8)
        mine = [
            gain(c) * edge_own[pl.ds(partner(c) * edge_rows + tile * 8 + PAD - PATCH, 8), :]
            for c in range(FEATS)
        ]
        for step in range(SPAN):
            value = None
            for c in range(FEATS):
                rows_at = pl.ds(c * edge_rows + tile * 8 + PAD - PATCH - SEARCH + step, 8)
                term = mine[c] * edge_other[rows_at, :]
                value = term if value is None else value + term
            edge_dist[step, at, :] = value
        return 0

    lax.fori_loop(0, dist_tiles, edge_tiles, 0)

    def edge_sums(step, _):
        for part in range(rows // 16):
            value = edge_dist[step, pl.ds(16 * part, 16), :]
            for s in range(1, SIDE):
                value = value + edge_dist[step, pl.ds(16 * part + s, 16), :]
            high, low = split(value)
            edge_sum[step, 16 * part : 16 * part + 16, :LANES] = high
            edge_sum[step, 16 * part : 16 * part + 16, LANES:] = low
        return 0

    lax.fori_loop(0, SPAN, edge_sums, 0)
    out_ref[...] = jnp.zeros_like(out_ref)
    chunk = GROUP * rows // 2

    def window(turn, j, _):
        k = turn * GROUP + j
        down = offs_ref[0, k] + SEARCH
        keep = keep_ref[offs_ref[1, k] + SEARCH]
        for part in range(rows // 16):
            at = pl.ds(pl.multiple_of(j * rows + 16 * part, 16), 16)
            for half in range(halves):
                value = dist[k, half, pl.ds(16 * part, 16), :]
                for s in range(1, SIDE):
                    value = value + dist[k, half, pl.ds(16 * part + s, 16), :]
                high, low = split(value)
                sums[at, half * LANES : (half + 1) * LANES] = high
                sums[at, cols + half * LANES : cols + (half + 1) * LANES] = low
            for which in range(2):
                span = slice(which * LANES, (which + 1) * LANES)
                sums[at, 2 * cols + which * LANES : 2 * cols + (which + 1) * LANES] = (
                    edge_sum[down, 16 * part : 16 * part + 16, span] * keep
                )
        return 0

    def weigh(piece, _):
        at = pl.ds(pl.multiple_of(piece * chunk, chunk), chunk)
        patch = jnp.dot(sums[at, :], band_ref[...], preferred_element_type=f32)
        weights[at, :] = jnp.exp2(patch * EXPONENT)
        return 0

    def accumulate(turn, downs, sides, tile, _):
        at = pl.ds(pl.multiple_of(tile * 8, 8), 8)
        for half in range(halves):
            span = slice(half * LANES, (half + 1) * LANES)
            total = [out_ref[c, at, span] for c in range(CHANS + 1)]
            for j in range(GROUP):
                rows_at = pl.ds(tile * 8 + PAD + downs[j], 8)
                weight = weights[pl.ds(pl.multiple_of(j * rows + tile * 8, 8), 8), span]
                for c in range(CHANS):
                    total[c] = total[c] + weight * moved[sides[j], half, c, rows_at, :]
                total[CHANS] = total[CHANS] + weight * moved[sides[j], half, 2 * CHANS, rows_at, :]
            for c in range(CHANS + 1):
                out_ref[c, at, span] = total[c]
        return 0

    def group(turn, _):
        downs = [offs_ref[0, turn * GROUP + j] for j in range(GROUP)]
        sides = [offs_ref[1, turn * GROUP + j] + SEARCH for j in range(GROUP)]
        lax.fori_loop(0, GROUP, functools.partial(window, turn), 0)
        lax.fori_loop(0, 2, weigh, 0)
        lax.fori_loop(0, rows // 8, functools.partial(accumulate, turn, downs, sides), 0)
        return 0

    lax.fori_loop(0, count // GROUP, group, 0)


def filter_block(sizes, offsets, field):
    rows, cols = sizes[:2]
    span_rows = rows + 2 * PAD
    edge_rows = span_rows + BANKS
    halves = cols // LANES
    vmem = pl.BlockSpec(memory_space=pltpu.VMEM)
    smem = pl.BlockSpec(memory_space=pltpu.SMEM)
    f32, bf16 = jnp.float32, jnp.bfloat16
    return pl.pallas_call(
        functools.partial(despeckle, sizes),
        out_shape=jax.ShapeDtypeStruct((CHANS + 1, rows, cols), f32),
        in_specs=[smem] + [vmem] * 4,
        out_specs=vmem,
        scratch_shapes=[
            pltpu.VMEM((CHANS, PAD, cols), f32),
            pltpu.VMEM((CHANS, PAD, cols), f32),
            pltpu.VMEM((span_rows, LANES), f32),
            pltpu.VMEM((span_rows, LANES), f32),
            pltpu.VMEM((2, rows, LANES), f32),
            pltpu.SemaphoreType.DMA((8,)),
            pltpu.SemaphoreType.DMA((8,)),
            pltpu.VMEM((halves + 2, FEATS, span_rows + BANKS, LANES), f32),
            pltpu.VMEM((SPAN, halves, FEATS, span_rows + BANKS, LANES), f32),
            pltpu.VMEM((halves, FEATS, rows + BANKS, LANES), f32),
            pltpu.VMEM((FEATS * edge_rows, 3 * LANES), bf16),
            pltpu.VMEM((FEATS * edge_rows, LANES), f32),
            pltpu.VMEM((FEATS * edge_rows, LANES), f32),
            pltpu.VMEM((SPAN, rows + 8, LANES), f32),
            pltpu.VMEM((SPAN, rows, 2 * LANES), bf16),
            pltpu.VMEM((offsets.shape[0], halves, rows + 8, LANES), f32),
            pltpu.VMEM((GROUP * rows, 2 * cols + 2 * LANES), bf16),
            pltpu.VMEM((GROUP * rows, cols), f32),
        ],
        compiler_params=pltpu.CompilerParams(
            vmem_limit_bytes=62 * 1024 * 1024, collective_id=0, has_side_effects=True
        ),
    )(
        offsets.T, field, jnp.asarray(band_matrix(cols), bf16), jnp.asarray(select_matrix(cols), bf16),
        jnp.asarray(keep_masks(cols), bf16),
    )


def per_device(coherency_field, offsets):
    _, rows, cols = coherency_field.shape
    row_total = rows * lax.axis_size("rows")
    col_total = cols * lax.axis_size("offs")
    sums = filter_block((rows, cols, row_total, col_total), offsets, coherency_field)
    return (coherency_field + sums[:CHANS]) / (1.0 + sums[CHANS])


def solution(mesh):
    in_specs = (P(None, "rows", "offs"), P())
    out_specs = P(None, "rows", "offs")
    return jax.shard_map(
        per_device, mesh=mesh, in_specs=in_specs, out_specs=out_specs, check_vma=False
    )
```

```python
import functools
import math

import jax
import jax.numpy as jnp
import numpy as np
from jax import lax
from jax.experimental import pallas as pl
from jax.experimental.pallas import tpu as pltpu
from jax.sharding import PartitionSpec as P

SEARCH = 6
PATCH = 3
SIDE = 2 * PATCH + 1
SPAN = 2 * SEARCH + 1
RIM = SEARCH + PATCH
STRENGTH = 1.5
LANES = 128
PAD = 16
CHANS = 9
FEATS = 2 * CHANS + 1
BATCH = 40
GROUP = 24
BANKS = 16
EXPONENT = -math.log2(math.e) / (STRENGTH * SIDE * SIDE)


def hermitian_inverse(matrix):
    diag_one, diag_two, diag_three = matrix[0], matrix[1], matrix[2]
    re_onetwo, re_onethree, re_twothree = matrix[3], matrix[4], matrix[5]
    im_onetwo, im_onethree, im_twothree = matrix[6], matrix[7], matrix[8]
    abs_onetwo = re_onetwo * re_onetwo + im_onetwo * im_onetwo
    abs_onethree = re_onethree * re_onethree + im_onethree * im_onethree
    abs_twothree = re_twothree * re_twothree + im_twothree * im_twothree
    yz_real = re_onethree * re_twothree + im_onethree * im_twothree
    yz_imag = im_onethree * re_twothree - re_onethree * im_twothree
    xz_real = re_onetwo * re_twothree - im_onetwo * im_twothree
    xz_imag = re_onetwo * im_twothree + im_onetwo * re_twothree
    yx_real = re_onethree * re_onetwo + im_onethree * im_onetwo
    yx_imag = im_onethree * re_onetwo - re_onethree * im_onetwo
    triple_real = xz_real * re_onethree + xz_imag * im_onethree
    determinant = (
        diag_one * diag_two * diag_three
        + 2.0 * triple_real
        - diag_one * abs_twothree
        - diag_two * abs_onethree
        - diag_three * abs_onetwo
    )
    adjugate = [
        diag_two * diag_three - abs_twothree,
        diag_one * diag_three - abs_onethree,
        diag_one * diag_two - abs_onetwo,
        -(re_onetwo * diag_three - yz_real),
        xz_real - re_onethree * diag_two,
        -(diag_one * re_twothree - yx_real),
        -(im_onetwo * diag_three - yz_imag),
        xz_imag - im_onethree * diag_two,
        -(diag_one * im_twothree - yx_imag),
    ]
    return adjugate, determinant


def edge_pairs(cols):
    pairs = []
    for step in range(-SEARCH, SEARCH + 1):
        for column in range(-PATCH, cols + PATCH):
            if not (0 <= column < cols and 0 <= column + step < cols):
                pairs.append((step, column))
    return pairs


def band_matrix(cols):
    source = np.arange(cols)[:, None]
    target = np.arange(cols)[None, :]
    main = (np.abs(source - target) <= PATCH).astype(np.float32)
    edge = np.zeros((LANES, cols), np.float32)
    for lane, (_, column) in enumerate(edge_pairs(cols)):
        edge[lane] = np.abs(np.arange(cols) - column) <= PATCH
    return np.concatenate([main, main, edge, edge], 0)


def select_matrix(cols):
    pick = np.zeros((LANES, 2 * LANES), np.float32)
    for lane, (step, column) in enumerate(edge_pairs(cols)):
        source = column + 32 if column < 32 else column - cols + 96
        pick[source, lane] = 1.0
        pick[source + step, LANES + lane] = 1.0
    return np.concatenate([pick] * 3, 0)


def keep_masks(cols):
    keep = np.zeros((SPAN, 16, LANES), np.float32)
    for lane, (step, _) in enumerate(edge_pairs(cols)):
        keep[step + SEARCH, :, lane] = 1.0
    return keep


def gain(feature):
    if feature == 2 * CHANS:
        return -6.0
    return 1.0 if feature % CHANS < 3 else 2.0


def partner(feature):
    if feature == 2 * CHANS:
        return feature
    return (feature + CHANS) % (2 * CHANS)


def despeckle(
    sizes, offs_ref, field_ref, band_ref, pick_ref, keep_ref, out_ref,
    above_ref, below_ref, left_ref, right_ref, packs, send_sems, recv_sems,
    feats, moved, own, edges, edge_own, edge_other, edge_dist, edge_sum, dist, sums, weights,
):
    rows, cols, row_total, col_total = sizes
    span_rows = rows + 2 * PAD
    edge_rows = edges.shape[0] // FEATS
    row_tiles = span_rows // 8
    head, tail = PAD // 8, (PAD + rows) // 8
    halves = cols // LANES
    dist_tiles = (rows + 8) // 8
    near_tile, far_tile = 2, dist_tiles - 2
    count = offs_ref.shape[1]
    lane = lax.broadcasted_iota(jnp.int32, (8, LANES), 1)
    sub = lax.broadcasted_iota(jnp.int32, (8, LANES), 0)
    wide_lane = lax.broadcasted_iota(jnp.int32, (16, LANES), 1)
    row, col = lax.axis_index("rows"), lax.axis_index("offs")
    row_start, col_start = row * rows, col * cols
    row_count, col_count = lax.axis_size("rows"), lax.axis_size("offs")
    f32, bf16 = jnp.float32, jnp.bfloat16

    def present(down, side):
        return (row + down >= 0) & (row + down < row_count) & (col + side >= 0) & (col + side < col_count)

    around = [(down, side) for down in (-1, 0, 1) for side in (-1, 0, 1) if (down, side) != (0, 0)]
    barrier = pltpu.get_barrier_semaphore()
    for down, side in around:

        @pl.when(present(down, side))
        def _(down=down, side=side):
            pl.semaphore_signal(
                barrier, inc=1, device_id=(row + down, col + side), device_id_type=pl.DeviceIdType.MESH
            )


    def pack(tile, _):
        at = pl.ds(pl.multiple_of(tile * 8, 8), 8)
        first = field_ref[0, at, :LANES]
        last = pltpu.roll(field_ref[0, at, cols - LANES :], RIM, 1)
        for c in range(1, CHANS):
            here = (lane >= RIM * c) & (lane < RIM * (c + 1))
            first = jnp.where(here, pltpu.roll(field_ref[c, at, :LANES], RIM * c, 1), first)
            last = jnp.where(here, pltpu.roll(field_ref[c, at, cols - LANES :], (RIM * c + RIM) % LANES, 1), last)
        packs[0, at, :] = first
        packs[1, at, :] = last
        return 0

    lax.fori_loop(0, rows // 8, pack, 0)

    copies = []
    for k, (down, side) in enumerate(around):
        start, size, put = {-1: (0, PAD, PAD + rows), 0: (0, rows, PAD), 1: (rows - PAD, PAD, 0)}[down]
        if side == 0:
            source = field_ref.at[:, start : start + size, :]
            target = below_ref if down < 0 else above_ref
        else:
            source = packs.at[0 if side < 0 else 1, start : start + size, :]
            target = (right_ref if side < 0 else left_ref).at[put : put + size, :]
        copies.append(pltpu.make_async_remote_copy(
            src_ref=source, dst_ref=target, send_sem=send_sems.at[k], recv_sem=recv_sems.at[k],
            device_id=(row + down, col + side), device_id_type=pl.DeviceIdType.MESH,
        ))

    def features(source_ref, first, groups, tile, _):
        at = pl.ds(pl.multiple_of(tile * 8, 8), 8)
        source_at = pl.ds(pl.multiple_of(tile * 8 - first, 8), 8)
        place = tile * 8 - PAD + sub
        in_rows = (place >= -RIM) & (place < rows + RIM) & (place + row_start >= 0) & (place + row_start < row_total)
        for group in groups:
            column = (group - 1) * LANES + lane
            inside = (
                in_rows & (column >= -RIM) & (column < cols + RIM)
                & (column + col_start >= 0) & (column + col_start < col_total)
            )
            if group == 0:
                packed = left_ref[at, :]
                cells = [pltpu.roll(packed, LANES - RIM - RIM * c, 1) for c in range(CHANS)]
            elif group == halves + 1:
                packed = right_ref[at, :]
                cells = [pltpu.roll(packed, LANES - RIM * c, 1) if c else packed for c in range(CHANS)]
            else:
                cells = [source_ref[c, source_at, (group - 1) * LANES : group * LANES] for c in range(CHANS)]
            adjugate, determinant = hermitian_inverse(cells)
            scale = 1.0 / determinant
            for c in range(CHANS):
                feats[group, c, at, :] = jnp.where(inside, cells[c], 0.0)
                feats[group, CHANS + c, at, :] = jnp.where(inside, adjugate[c] * scale, 0.0)
            feats[group, 2 * CHANS, at, :] = jnp.where(inside, 1.0, 0.0)
        return 0

    def shifts(tile, _):
        at = pl.ds(pl.multiple_of(tile * 8, 8), 8)
        zero = jnp.zeros((8, LANES), f32)
        for step in range(-SEARCH, SEARCH + 1):
            for half in range(halves):
                partner_col = half * LANES + lane + step
                moved[step + SEARCH, half, 2 * CHANS, at, :] = jnp.where(
                    (partner_col >= 0) & (partner_col < cols), feats[half + 1, 2 * CHANS, at, :], 0.0
                )
        for c in range(2 * CHANS):
            cells = [zero] + [feats[half + 1, c, at, :] for half in range(halves)] + [zero]
            for step in range(-SEARCH, SEARCH + 1):
                for half in range(halves):
                    here = cells[half + 1]
                    if step > 0:
                        value = pltpu.roll(jnp.where(lane >= step, here, cells[half + 2]), LANES - step, 1)
                    elif step < 0:
                        value = pltpu.roll(jnp.where(lane < LANES + step, here, cells[half]), -step, 1)
                    else:
                        value = here
                    moved[step + SEARCH, half, c, at, :] = value
        return 0

    def own_tiles(tile, _):
        at = pl.ds(pl.multiple_of(tile * 8, 8), 8)
        for half in range(halves):
            for c in range(FEATS):
                own[half, c, at, :] = gain(c) * feats[half + 1, partner(c), pl.ds(tile * 8 + PAD - PATCH, 8), :]
        return 0

    def distances(turn, downs, sides, step, _):
        half, tile = step % halves, step // halves
        at = pl.ds(pl.multiple_of(tile * 8, 8), 8)
        mine = [own[half, c, at, :] for c in range(FEATS)]
        for j in range(BATCH):
            rows_at = pl.ds(tile * 8 + PAD - PATCH + downs[j], 8)
            terms = [None, None]
            for c in range(FEATS):
                term = mine[c] * moved[sides[j], half, c, rows_at, :]
                terms[c % 2] = term if terms[c % 2] is None else terms[c % 2] + term
            dist[turn * BATCH + j, half, at, :] = terms[0] + terms[1]
        return 0

    def distance_batch(spans, turn, _):
        downs = [offs_ref[0, turn * BATCH + j] for j in range(BATCH)]
        sides = [offs_ref[1, turn * BATCH + j] + SEARCH for j in range(BATCH)]
        for start, stop in spans:
            lax.fori_loop(start * halves, stop * halves, functools.partial(distances, turn, downs, sides), 0)
        return 0

    inner = tuple(range(1, halves + 1))
    lax.fori_loop(head, tail, functools.partial(features, field_ref, PAD, inner), 0)
    lax.fori_loop(head, tail - 1, shifts, 0)
    over = 1 + (row > 0).astype(jnp.int32) + (row < row_count - 1).astype(jnp.int32)
    across = 1 + (col > 0).astype(jnp.int32) + (col < col_count - 1).astype(jnp.int32)
    pl.semaphore_wait(barrier, over * across - 1)
    for (down, side), copy in zip(around, copies):
        pl.when(present(down, side))(copy.start)
    lax.fori_loop(tail - 1, tail, shifts, 0)
    lax.fori_loop(near_tile, far_tile, own_tiles, 0)
    lax.fori_loop(0, count // BATCH, functools.partial(distance_batch, ((near_tile, far_tile),)), 0)
    for (down, side), copy in zip(around, copies):
        pl.when(present(down, side))(copy.wait_send)
        pl.when(present(-down, -side))(copy.wait_recv)

    outer = (0, halves + 1)
    lax.fori_loop(0, head, functools.partial(features, above_ref, 0, outer + inner), 0)
    lax.fori_loop(head, tail, functools.partial(features, field_ref, PAD, outer), 0)
    lax.fori_loop(tail, row_tiles, functools.partial(features, below_ref, PAD + rows, outer + inner), 0)
    lax.fori_loop(0, head, shifts, 0)
    lax.fori_loop(tail, row_tiles, shifts, 0)
    lax.fori_loop(0, near_tile, own_tiles, 0)
    lax.fori_loop(far_tile, dist_tiles, own_tiles, 0)
    late = ((0, near_tile), (far_tile, dist_tiles))
    lax.fori_loop(0, count // BATCH, functools.partial(distance_batch, late), 0)

    def split(value):
        high = value.astype(bf16)
        return high, (value - high.astype(f32)).astype(bf16)

    def patches(tile, _):
        at = pl.ds(pl.multiple_of(tile * 16, 16), 16)
        for c in range(FEATS):
            cells = [feats[group, c, at, :] for group in range(halves + 2)]
            before = pltpu.roll(jnp.where(wide_lane >= 96, cells[0], cells[1]), 32, 1)
            after = pltpu.roll(jnp.where(wide_lane >= 96, cells[halves], cells[halves + 1]), 96, 1)
            value = jnp.where(wide_lane < 64, before, after)
            high = value.astype(bf16)
            middle, low = split(value - high.astype(f32))
            edge_at = pl.ds(pl.multiple_of(c * edge_rows + tile * 16, 16), 16)
            edges[edge_at, :LANES] = high
            edges[edge_at, LANES : 2 * LANES] = middle
            edges[edge_at, 2 * LANES :] = low
            if c < CHANS or c == 2 * CHANS:
                for step in range(1, SEARCH + 1):
                    up, down = (step + SEARCH, halves - 1, c, at), (SEARCH - step, 0, c, at)
                    moved[up] = jnp.where(
                        wide_lane >= LANES - step, pltpu.roll(cells[halves + 1], LANES - step, 1), moved[up]
                    )
                    moved[down] = jnp.where(wide_lane < step, pltpu.roll(cells[0], step, 1), moved[down])
        return 0

    lax.fori_loop(0, row_tiles // 2, patches, 0)
    both = jnp.dot(edges[...], pick_ref[...], preferred_element_type=f32)
    edge_own[...] = both[:, :LANES]
    edge_other[...] = both[:, LANES:]

    def edge_tiles(tile, _):
        at = pl.ds(pl.multiple_of(tile * 8, 8), 8)
        mine = [
            gain(c) * edge_own[pl.ds(partner(c) * edge_rows + tile * 8 + PAD - PATCH, 8), :]
            for c in range(FEATS)
        ]
        for step in range(SPAN):
            value = None
            for c in range(FEATS):
                rows_at = pl.ds(c * edge_rows + tile * 8 + PAD - PATCH - SEARCH + step, 8)
                term = mine[c] * edge_other[rows_at, :]
                value = term if value is None else value + term
            edge_dist[step, at, :] = value
        return 0

    lax.fori_loop(0, dist_tiles, edge_tiles, 0)

    def edge_sums(step, _):
        for part in range(rows // 16):
            value = edge_dist[step, pl.ds(16 * part, 16), :]
            for s in range(1, SIDE):
                value = value + edge_dist[step, pl.ds(16 * part + s, 16), :]
            high, low = split(value)
            edge_sum[step, 16 * part : 16 * part + 16, :LANES] = high
            edge_sum[step, 16 * part : 16 * part + 16, LANES:] = low
        return 0

    lax.fori_loop(0, SPAN, edge_sums, 0)
    out_ref[...] = jnp.zeros_like(out_ref)
    chunk = GROUP * rows // 2

    def window(turn, j, _):
        k = turn * GROUP + j
        down = offs_ref[0, k] + SEARCH
        keep = keep_ref[offs_ref[1, k] + SEARCH]
        for part in range(rows // 16):
            at = pl.ds(pl.multiple_of(j * rows + 16 * part, 16), 16)
            for half in range(halves):
                value = dist[k, half, pl.ds(16 * part, 16), :]
                for s in range(1, SIDE):
                    value = value + dist[k, half, pl.ds(16 * part + s, 16), :]
                high, low = split(value)
                sums[at, half * LANES : (half + 1) * LANES] = high
                sums[at, cols + half * LANES : cols + (half + 1) * LANES] = low
            for which in range(2):
                span = slice(which * LANES, (which + 1) * LANES)
                sums[at, 2 * cols + which * LANES : 2 * cols + (which + 1) * LANES] = (
                    edge_sum[down, 16 * part : 16 * part + 16, span] * keep
                )
        return 0

    def weigh(piece, _):
        at = pl.ds(pl.multiple_of(piece * chunk, chunk), chunk)
        patch = jnp.dot(sums[at, :], band_ref[...], preferred_element_type=f32)
        weights[at, :] = jnp.exp2(patch * EXPONENT)
        return 0

    def accumulate(turn, downs, sides, tile, _):
        at = pl.ds(pl.multiple_of(tile * 8, 8), 8)
        for half in range(halves):
            span = slice(half * LANES, (half + 1) * LANES)
            total = [out_ref[c, at, span] for c in range(CHANS + 1)]
            for j in range(GROUP):
                rows_at = pl.ds(tile * 8 + PAD + downs[j], 8)
                weight = weights[pl.ds(pl.multiple_of(j * rows + tile * 8, 8), 8), span]
                for c in range(CHANS):
                    total[c] = total[c] + weight * moved[sides[j], half, c, rows_at, :]
                total[CHANS] = total[CHANS] + weight * moved[sides[j], half, 2 * CHANS, rows_at, :]
            for c in range(CHANS + 1):
                out_ref[c, at, span] = total[c]
        return 0

    def group(turn, _):
        downs = [offs_ref[0, turn * GROUP + j] for j in range(GROUP)]
        sides = [offs_ref[1, turn * GROUP + j] + SEARCH for j in range(GROUP)]
        lax.fori_loop(0, GROUP, functools.partial(window, turn), 0)
        lax.fori_loop(0, 2, weigh, 0)
        lax.fori_loop(0, rows // 8, functools.partial(accumulate, turn, downs, sides), 0)
        return 0

    lax.fori_loop(0, count // GROUP, group, 0)


def finish(field_ref, sums_ref, out_ref):
    def tile_rows(tile, _):
        at = pl.ds(pl.multiple_of(tile * 8, 8), 8)
        scale = 1.0 / (1.0 + sums_ref[CHANS, at, :])
        for c in range(CHANS):
            out_ref[c, at, :] = (field_ref[c, at, :] + sums_ref[c, at, :]) * scale
        return 0

    lax.fori_loop(0, field_ref.shape[1] // 8, tile_rows, 0)


def filter_block(sizes, offsets, field):
    rows, cols = sizes[:2]
    span_rows = rows + 2 * PAD
    edge_rows = span_rows + BANKS
    halves = cols // LANES
    vmem = pl.BlockSpec(memory_space=pltpu.VMEM)
    smem = pl.BlockSpec(memory_space=pltpu.SMEM)
    f32, bf16 = jnp.float32, jnp.bfloat16
    return pl.pallas_call(
        functools.partial(despeckle, sizes),
        out_shape=jax.ShapeDtypeStruct((CHANS + 1, rows, cols), f32),
        in_specs=[smem] + [vmem] * 4,
        out_specs=vmem,
        scratch_shapes=[
            pltpu.VMEM((CHANS, PAD, cols), f32),
            pltpu.VMEM((CHANS, PAD, cols), f32),
            pltpu.VMEM((span_rows, LANES), f32),
            pltpu.VMEM((span_rows, LANES), f32),
            pltpu.VMEM((2, rows, LANES), f32),
            pltpu.SemaphoreType.DMA((8,)),
            pltpu.SemaphoreType.DMA((8,)),
            pltpu.VMEM((halves + 2, FEATS, span_rows + BANKS, LANES), f32),
            pltpu.VMEM((SPAN, halves, FEATS, span_rows + BANKS, LANES), f32),
            pltpu.VMEM((halves, FEATS, rows + BANKS, LANES), f32),
            pltpu.VMEM((FEATS * edge_rows, 3 * LANES), bf16),
            pltpu.VMEM((FEATS * edge_rows, LANES), f32),
            pltpu.VMEM((FEATS * edge_rows, LANES), f32),
            pltpu.VMEM((SPAN, rows + 8, LANES), f32),
            pltpu.VMEM((SPAN, rows, 2 * LANES), bf16),
            pltpu.VMEM((offsets.shape[0], halves, rows + 8, LANES), f32),
            pltpu.VMEM((GROUP * rows, 2 * cols + 2 * LANES), bf16),
            pltpu.VMEM((GROUP * rows, cols), f32),
        ],
        compiler_params=pltpu.CompilerParams(
            vmem_limit_bytes=62 * 1024 * 1024, collective_id=0, has_side_effects=True
        ),
    )(
        offsets.T, field, jnp.asarray(band_matrix(cols), bf16), jnp.asarray(select_matrix(cols), bf16),
        jnp.asarray(keep_masks(cols), bf16),
    )


def per_device(coherency_field, offsets):
    _, rows, cols = coherency_field.shape
    row_total = rows * lax.axis_size("rows")
    col_total = cols * lax.axis_size("offs")
    sums = filter_block((rows, cols, row_total, col_total), offsets, coherency_field)
    vmem = pl.BlockSpec(memory_space=pltpu.VMEM)
    return pl.pallas_call(
        finish,
        out_shape=jax.ShapeDtypeStruct(coherency_field.shape, jnp.float32),
        in_specs=[vmem, vmem],
        out_specs=vmem,
    )(coherency_field, sums)


def solution(mesh):
    in_specs = (P(None, "rows", "offs"), P())
    out_specs = P(None, "rows", "offs")
    return jax.shard_map(
        per_device, mesh=mesh, in_specs=in_specs, out_specs=out_specs, check_vma=False
    )
```

```python
import functools
import math

import jax
import jax.numpy as jnp
import numpy as np
from jax import lax
from jax.experimental import pallas as pl
from jax.experimental.pallas import tpu as pltpu
from jax.sharding import PartitionSpec as P

SEARCH = 6
PATCH = 3
SIDE = 2 * PATCH + 1
SPAN = 2 * SEARCH + 1
RIM = SEARCH + PATCH
STRENGTH = 1.5
LANES = 128
PAD = 16
CHANS = 9
FEATS = 2 * CHANS + 1
BATCH = 40
AHEAD = 1
GROUP = 24
BANKS = 16
EXPONENT = -math.log2(math.e) / (STRENGTH * SIDE * SIDE)


def hermitian_inverse(matrix):
    diag_one, diag_two, diag_three = matrix[0], matrix[1], matrix[2]
    re_onetwo, re_onethree, re_twothree = matrix[3], matrix[4], matrix[5]
    im_onetwo, im_onethree, im_twothree = matrix[6], matrix[7], matrix[8]
    abs_onetwo = re_onetwo * re_onetwo + im_onetwo * im_onetwo
    abs_onethree = re_onethree * re_onethree + im_onethree * im_onethree
    abs_twothree = re_twothree * re_twothree + im_twothree * im_twothree
    yz_real = re_onethree * re_twothree + im_onethree * im_twothree
    yz_imag = im_onethree * re_twothree - re_onethree * im_twothree
    xz_real = re_onetwo * re_twothree - im_onetwo * im_twothree
    xz_imag = re_onetwo * im_twothree + im_onetwo * re_twothree
    yx_real = re_onethree * re_onetwo + im_onethree * im_onetwo
    yx_imag = im_onethree * re_onetwo - re_onethree * im_onetwo
    triple_real = xz_real * re_onethree + xz_imag * im_onethree
    determinant = (
        diag_one * diag_two * diag_three
        + 2.0 * triple_real
        - diag_one * abs_twothree
        - diag_two * abs_onethree
        - diag_three * abs_onetwo
    )
    adjugate = [
        diag_two * diag_three - abs_twothree,
        diag_one * diag_three - abs_onethree,
        diag_one * diag_two - abs_onetwo,
        -(re_onetwo * diag_three - yz_real),
        xz_real - re_onethree * diag_two,
        -(diag_one * re_twothree - yx_real),
        -(im_onetwo * diag_three - yz_imag),
        xz_imag - im_onethree * diag_two,
        -(diag_one * im_twothree - yx_imag),
    ]
    return adjugate, determinant


def edge_pairs(cols):
    pairs = []
    for step in range(-SEARCH, SEARCH + 1):
        for column in range(-PATCH, cols + PATCH):
            if not (0 <= column < cols and 0 <= column + step < cols):
                pairs.append((step, column))
    return pairs


def band_matrix(cols):
    source = np.arange(cols)[:, None]
    target = np.arange(cols)[None, :]
    main = (np.abs(source - target) <= PATCH).astype(np.float32)
    edge = np.zeros((LANES, cols), np.float32)
    for lane, (_, column) in enumerate(edge_pairs(cols)):
        edge[lane] = np.abs(np.arange(cols) - column) <= PATCH
    return np.concatenate([main, main, edge, edge], 0)


def select_matrix(cols):
    pick = np.zeros((LANES, 2 * LANES), np.float32)
    for lane, (step, column) in enumerate(edge_pairs(cols)):
        source = column + 32 if column < 32 else column - cols + 96
        pick[source, lane] = 1.0
        pick[source + step, LANES + lane] = 1.0
    return np.concatenate([pick] * 3, 0)


def keep_masks(cols):
    keep = np.zeros((SPAN, 16, LANES), np.float32)
    for lane, (step, _) in enumerate(edge_pairs(cols)):
        keep[step + SEARCH, :, lane] = 1.0
    return keep


def gain(feature):
    if feature == 2 * CHANS:
        return -6.0
    return 1.0 if feature % CHANS < 3 else 2.0


def partner(feature):
    if feature == 2 * CHANS:
        return feature
    return (feature + CHANS) % (2 * CHANS)


def despeckle(
    sizes, offs_ref, field_ref, band_ref, pick_ref, keep_ref, out_ref,
    above_ref, below_ref, left_ref, right_ref, packs, send_sems, recv_sems,
    feats, moved, own, edges, edge_own, edge_other, edge_dist, edge_sum, dist, sums, weights,
):
    rows, cols, row_total, col_total = sizes
    span_rows = rows + 2 * PAD
    edge_rows = edges.shape[0] // FEATS
    row_tiles = span_rows // 8
    head, tail = PAD // 8, (PAD + rows) // 8
    halves = cols // LANES
    dist_tiles = (rows + 8) // 8
    near_tile, far_tile = 2, dist_tiles - 2
    count = offs_ref.shape[1]
    lane = lax.broadcasted_iota(jnp.int32, (8, LANES), 1)
    sub = lax.broadcasted_iota(jnp.int32, (8, LANES), 0)
    wide_lane = lax.broadcasted_iota(jnp.int32, (16, LANES), 1)
    row, col = lax.axis_index("rows"), lax.axis_index("offs")
    row_start, col_start = row * rows, col * cols
    row_count, col_count = lax.axis_size("rows"), lax.axis_size("offs")
    f32, bf16 = jnp.float32, jnp.bfloat16

    def present(down, side):
        return (row + down >= 0) & (row + down < row_count) & (col + side >= 0) & (col + side < col_count)

    around = [(down, side) for down in (-1, 0, 1) for side in (-1, 0, 1) if (down, side) != (0, 0)]
    barrier = pltpu.get_barrier_semaphore()
    for down, side in around:

        @pl.when(present(down, side))
        def _(down=down, side=side):
            pl.semaphore_signal(
                barrier, inc=1, device_id=(row + down, col + side), device_id_type=pl.DeviceIdType.MESH
            )


    def pack(tile, _):
        at = pl.ds(pl.multiple_of(tile * 8, 8), 8)
        first = field_ref[0, at, :LANES]
        last = pltpu.roll(field_ref[0, at, cols - LANES :], RIM, 1)
        for c in range(1, CHANS):
            here = (lane >= RIM * c) & (lane < RIM * (c + 1))
            first = jnp.where(here, pltpu.roll(field_ref[c, at, :LANES], RIM * c, 1), first)
            last = jnp.where(here, pltpu.roll(field_ref[c, at, cols - LANES :], (RIM * c + RIM) % LANES, 1), last)
        packs[0, at, :] = first
        packs[1, at, :] = last
        return 0

    lax.fori_loop(0, rows // 8, pack, 0)

    copies = []
    for k, (down, side) in enumerate(around):
        start, size, put = {-1: (0, PAD, PAD + rows), 0: (0, rows, PAD), 1: (rows - PAD, PAD, 0)}[down]
        if side == 0:
            source = field_ref.at[:, start : start + size, :]
            target = below_ref if down < 0 else above_ref
        else:
            source = packs.at[0 if side < 0 else 1, start : start + size, :]
            target = (right_ref if side < 0 else left_ref).at[put : put + size, :]
        copies.append(pltpu.make_async_remote_copy(
            src_ref=source, dst_ref=target, send_sem=send_sems.at[k], recv_sem=recv_sems.at[k],
            device_id=(row + down, col + side), device_id_type=pl.DeviceIdType.MESH,
        ))

    def features(source_ref, first, groups, tile, _):
        at = pl.ds(pl.multiple_of(tile * 8, 8), 8)
        source_at = pl.ds(pl.multiple_of(tile * 8 - first, 8), 8)
        place = tile * 8 - PAD + sub
        in_rows = (place >= -RIM) & (place < rows + RIM) & (place + row_start >= 0) & (place + row_start < row_total)
        for group in groups:
            column = (group - 1) * LANES + lane
            inside = (
                in_rows & (column >= -RIM) & (column < cols + RIM)
                & (column + col_start >= 0) & (column + col_start < col_total)
            )
            if group == 0:
                packed = left_ref[at, :]
                cells = [pltpu.roll(packed, LANES - RIM - RIM * c, 1) for c in range(CHANS)]
            elif group == halves + 1:
                packed = right_ref[at, :]
                cells = [pltpu.roll(packed, LANES - RIM * c, 1) if c else packed for c in range(CHANS)]
            else:
                cells = [source_ref[c, source_at, (group - 1) * LANES : group * LANES] for c in range(CHANS)]
            adjugate, determinant = hermitian_inverse(cells)
            scale = 1.0 / determinant
            for c in range(CHANS):
                feats[group, c, at, :] = jnp.where(inside, cells[c], 0.0)
                feats[group, CHANS + c, at, :] = jnp.where(inside, adjugate[c] * scale, 0.0)
            feats[group, 2 * CHANS, at, :] = jnp.where(inside, 1.0, 0.0)
        return 0

    def shifts(tile, _):
        at = pl.ds(pl.multiple_of(tile * 8, 8), 8)
        zero = jnp.zeros((8, LANES), f32)
        for step in range(-SEARCH, SEARCH + 1):
            for half in range(halves):
                partner_col = half * LANES + lane + step
                moved[step + SEARCH, half, 2 * CHANS, at, :] = jnp.where(
                    (partner_col >= 0) & (partner_col < cols), feats[half + 1, 2 * CHANS, at, :], 0.0
                )
        for c in range(2 * CHANS):
            cells = [zero] + [feats[half + 1, c, at, :] for half in range(halves)] + [zero]
            for step in range(-SEARCH, SEARCH + 1):
                for half in range(halves):
                    here = cells[half + 1]
                    if step > 0:
                        value = pltpu.roll(jnp.where(lane >= step, here, cells[half + 2]), LANES - step, 1)
                    elif step < 0:
                        value = pltpu.roll(jnp.where(lane < LANES + step, here, cells[half]), -step, 1)
                    else:
                        value = here
                    moved[step + SEARCH, half, c, at, :] = value
        return 0

    def own_tiles(tile, _):
        at = pl.ds(pl.multiple_of(tile * 8, 8), 8)
        for half in range(halves):
            for c in range(FEATS):
                own[half, c, at, :] = gain(c) * feats[half + 1, partner(c), pl.ds(tile * 8 + PAD - PATCH, 8), :]
        return 0

    def distances(turn, downs, sides, step, _):
        half, tile = step % halves, step // halves
        at = pl.ds(pl.multiple_of(tile * 8, 8), 8)
        mine = [own[half, c, at, :] for c in range(FEATS)]
        for j in range(BATCH):
            rows_at = pl.ds(tile * 8 + PAD - PATCH + downs[j], 8)
            terms = [None, None]
            for c in range(FEATS):
                term = mine[c] * moved[sides[j], half, c, rows_at, :]
                terms[c % 2] = term if terms[c % 2] is None else terms[c % 2] + term
            dist[turn * BATCH + j, half, at, :] = terms[0] + terms[1]
        return 0

    def distance_batch(spans, turn, _):
        downs = [offs_ref[0, turn * BATCH + j] for j in range(BATCH)]
        sides = [offs_ref[1, turn * BATCH + j] + SEARCH for j in range(BATCH)]
        for start, stop in spans:
            lax.fori_loop(start * halves, stop * halves, functools.partial(distances, turn, downs, sides), 0)
        return 0

    inner = tuple(range(1, halves + 1))
    lax.fori_loop(head, tail, functools.partial(features, field_ref, PAD, inner), 0)
    def distance_span(first_batch, last_batch, start, stop):
        span = functools.partial(distance_batch, ((start, stop),))
        lax.fori_loop(first_batch, last_batch, span, 0)

    lax.fori_loop(head, tail, shifts, 0)
    lax.fori_loop(near_tile, far_tile, own_tiles, 0)
    distance_span(0, AHEAD, near_tile, far_tile)
    over = 1 + (row > 0).astype(jnp.int32) + (row < row_count - 1).astype(jnp.int32)
    across = 1 + (col > 0).astype(jnp.int32) + (col < col_count - 1).astype(jnp.int32)
    pl.semaphore_wait(barrier, over * across - 1)
    for (down, side), copy in zip(around, copies):
        pl.when(present(down, side))(copy.start)
    distance_span(AHEAD, count // BATCH, near_tile, far_tile)

    for (down, side), copy in zip(around, copies):
        if (down, side) == (-1, 0):
            pl.when(present(-down, -side))(copy.wait_recv)
    lax.fori_loop(tail, row_tiles, functools.partial(features, below_ref, PAD + rows, inner), 0)
    lax.fori_loop(tail, row_tiles, shifts, 0)
    lax.fori_loop(far_tile, dist_tiles, own_tiles, 0)
    distance_span(0, count // BATCH, far_tile, dist_tiles)

    for (down, side), copy in zip(around, copies):
        pl.when(present(down, side))(copy.wait_send)
        if (down, side) != (-1, 0):
            pl.when(present(-down, -side))(copy.wait_recv)
    outer = (0, halves + 1)
    lax.fori_loop(0, head, functools.partial(features, above_ref, 0, outer + inner), 0)
    lax.fori_loop(head, tail, functools.partial(features, field_ref, PAD, outer), 0)
    lax.fori_loop(tail, row_tiles, functools.partial(features, below_ref, PAD + rows, outer), 0)
    lax.fori_loop(0, head, shifts, 0)
    lax.fori_loop(0, near_tile, own_tiles, 0)
    distance_span(0, count // BATCH, 0, near_tile)

    def split(value):
        high = value.astype(bf16)
        return high, (value - high.astype(f32)).astype(bf16)

    def edge_columns(tile, _):
        at = pl.ds(pl.multiple_of(tile * 16, 16), 16)
        for c in range(FEATS):
            cells = [feats[group, c, at, :] for group in range(halves + 2)]
            before = pltpu.roll(jnp.where(wide_lane >= 96, cells[0], cells[1]), 32, 1)
            after = pltpu.roll(jnp.where(wide_lane >= 96, cells[halves], cells[halves + 1]), 96, 1)
            value = jnp.where(wide_lane < 64, before, after)
            high = value.astype(bf16)
            middle, low = split(value - high.astype(f32))
            edge_at = pl.ds(pl.multiple_of(c * edge_rows + tile * 16, 16), 16)
            edges[edge_at, :LANES] = high
            edges[edge_at, LANES : 2 * LANES] = middle
            edges[edge_at, 2 * LANES :] = low
        return 0

    def patches(tile, _):
        at = pl.ds(pl.multiple_of(tile * 8, 8), 8)
        valid = feats[1, 2 * CHANS, at, :]
        for step in range(1, SEARCH + 1):
            for move, half in ((step, halves - 1), (-step, 0)):
                column = col_start + half * LANES + lane + move
                moved[move + SEARCH, half, 2 * CHANS, at, :] = jnp.where(
                    (column >= 0) & (column < col_total), valid, 0.0
                )
        for c in range(CHANS):
            before, after = feats[0, c, at, :], feats[halves + 1, c, at, :]
            for step in range(1, SEARCH + 1):
                up, down = (step + SEARCH, halves - 1, c, at), (SEARCH - step, 0, c, at)
                moved[up] = jnp.where(lane >= LANES - step, pltpu.roll(after, LANES - step, 1), moved[up])
                moved[down] = jnp.where(lane < step, pltpu.roll(before, step, 1), moved[down])
        return 0

    lax.fori_loop(1, row_tiles - 1, patches, 0)
    lax.fori_loop(0, row_tiles // 2, edge_columns, 0)
    both = jnp.dot(edges[...], pick_ref[...], preferred_element_type=f32)
    edge_own[...] = both[:, :LANES]
    edge_other[...] = both[:, LANES:]

    def edge_tiles(tile, _):
        at = pl.ds(pl.multiple_of(tile * 8, 8), 8)
        mine = [
            gain(c) * edge_own[pl.ds(partner(c) * edge_rows + tile * 8 + PAD - PATCH, 8), :]
            for c in range(FEATS)
        ]
        for step in range(SPAN):
            value = None
            for c in range(FEATS):
                rows_at = pl.ds(c * edge_rows + tile * 8 + PAD - PATCH - SEARCH + step, 8)
                term = mine[c] * edge_other[rows_at, :]
                value = term if value is None else value + term
            edge_dist[step, at, :] = value
        return 0

    lax.fori_loop(0, dist_tiles, edge_tiles, 0)

    def edge_sums(step, _):
        for part in range(rows // 16):
            value = edge_dist[step, pl.ds(16 * part, 16), :]
            for s in range(1, SIDE):
                value = value + edge_dist[step, pl.ds(16 * part + s, 16), :]
            high, low = split(value)
            edge_sum[step, 16 * part : 16 * part + 16, :LANES] = high
            edge_sum[step, 16 * part : 16 * part + 16, LANES:] = low
        return 0

    lax.fori_loop(0, SPAN, edge_sums, 0)
    out_ref[...] = jnp.zeros_like(out_ref)
    chunk = GROUP * rows // 2

    def window(turn, j, _):
        k = turn * GROUP + j
        down = offs_ref[0, k] + SEARCH
        keep = keep_ref[offs_ref[1, k] + SEARCH]
        for part in range(rows // 16):
            at = pl.ds(pl.multiple_of(j * rows + 16 * part, 16), 16)
            for half in range(halves):
                value = dist[k, half, pl.ds(16 * part, 16), :]
                for s in range(1, SIDE):
                    value = value + dist[k, half, pl.ds(16 * part + s, 16), :]
                high, low = split(value)
                sums[at, half * LANES : (half + 1) * LANES] = high
                sums[at, cols + half * LANES : cols + (half + 1) * LANES] = low
            for which in range(2):
                span = slice(which * LANES, (which + 1) * LANES)
                sums[at, 2 * cols + which * LANES : 2 * cols + (which + 1) * LANES] = (
                    edge_sum[down, 16 * part : 16 * part + 16, span] * keep
                )
        return 0

    def weigh(piece, _):
        at = pl.ds(pl.multiple_of(piece * chunk, chunk), chunk)
        patch = jnp.dot(sums[at, :], band_ref[...], preferred_element_type=f32)
        weights[at, :] = jnp.exp2(patch * EXPONENT)
        return 0

    def accumulate(turn, downs, sides, tile, _):
        at = pl.ds(pl.multiple_of(tile * 8, 8), 8)
        for half in range(halves):
            span = slice(half * LANES, (half + 1) * LANES)
            total = [out_ref[c, at, span] for c in range(CHANS + 1)]
            for j in range(GROUP):
                rows_at = pl.ds(tile * 8 + PAD + downs[j], 8)
                weight = weights[pl.ds(pl.multiple_of(j * rows + tile * 8, 8), 8), span]
                for c in range(CHANS):
                    total[c] = total[c] + weight * moved[sides[j], half, c, rows_at, :]
                total[CHANS] = total[CHANS] + weight * moved[sides[j], half, 2 * CHANS, rows_at, :]
            for c in range(CHANS + 1):
                out_ref[c, at, span] = total[c]
        return 0

    def group(turn, _):
        downs = [offs_ref[0, turn * GROUP + j] for j in range(GROUP)]
        sides = [offs_ref[1, turn * GROUP + j] + SEARCH for j in range(GROUP)]
        lax.fori_loop(0, GROUP, functools.partial(window, turn), 0)
        lax.fori_loop(0, 2, weigh, 0)
        lax.fori_loop(0, rows // 8, functools.partial(accumulate, turn, downs, sides), 0)
        return 0

    lax.fori_loop(0, count // GROUP, group, 0)


def finish(field_ref, sums_ref, out_ref):
    def tile_rows(tile, _):
        at = pl.ds(pl.multiple_of(tile * 8, 8), 8)
        scale = 1.0 / (1.0 + sums_ref[CHANS, at, :])
        for c in range(CHANS):
            out_ref[c, at, :] = (field_ref[c, at, :] + sums_ref[c, at, :]) * scale
        return 0

    lax.fori_loop(0, field_ref.shape[1] // 8, tile_rows, 0)


def filter_block(sizes, offsets, field):
    rows, cols = sizes[:2]
    span_rows = rows + 2 * PAD
    edge_rows = span_rows + BANKS
    halves = cols // LANES
    vmem = pl.BlockSpec(memory_space=pltpu.VMEM)
    smem = pl.BlockSpec(memory_space=pltpu.SMEM)
    f32, bf16 = jnp.float32, jnp.bfloat16
    return pl.pallas_call(
        functools.partial(despeckle, sizes),
        out_shape=jax.ShapeDtypeStruct((CHANS + 1, rows, cols), f32),
        in_specs=[smem] + [vmem] * 4,
        out_specs=vmem,
        scratch_shapes=[
            pltpu.VMEM((CHANS, PAD, cols), f32),
            pltpu.VMEM((CHANS, PAD, cols), f32),
            pltpu.VMEM((span_rows, LANES), f32),
            pltpu.VMEM((span_rows, LANES), f32),
            pltpu.VMEM((2, rows, LANES), f32),
            pltpu.SemaphoreType.DMA((8,)),
            pltpu.SemaphoreType.DMA((8,)),
            pltpu.VMEM((halves + 2, FEATS, span_rows + BANKS, LANES), f32),
            pltpu.VMEM((SPAN, halves, FEATS, span_rows + BANKS, LANES), f32),
            pltpu.VMEM((halves, FEATS, rows + BANKS, LANES), f32),
            pltpu.VMEM((FEATS * edge_rows, 3 * LANES), bf16),
            pltpu.VMEM((FEATS * edge_rows, LANES), f32),
            pltpu.VMEM((FEATS * edge_rows, LANES), f32),
            pltpu.VMEM((SPAN, rows + 8, LANES), f32),
            pltpu.VMEM((SPAN, rows, 2 * LANES), bf16),
            pltpu.VMEM((offsets.shape[0], halves, rows + 8, LANES), f32),
            pltpu.VMEM((GROUP * rows, 2 * cols + 2 * LANES), bf16),
            pltpu.VMEM((GROUP * rows, cols), f32),
        ],
        compiler_params=pltpu.CompilerParams(
            vmem_limit_bytes=62 * 1024 * 1024, collective_id=0, has_side_effects=True
        ),
    )(
        offsets.T, field, jnp.asarray(band_matrix(cols), bf16), jnp.asarray(select_matrix(cols), bf16),
        jnp.asarray(keep_masks(cols), bf16),
    )


def per_device(coherency_field, offsets):
    _, rows, cols = coherency_field.shape
    row_total = rows * lax.axis_size("rows")
    col_total = cols * lax.axis_size("offs")
    sums = filter_block((rows, cols, row_total, col_total), offsets, coherency_field)
    vmem = pl.BlockSpec(memory_space=pltpu.VMEM)
    return pl.pallas_call(
        finish,
        out_shape=jax.ShapeDtypeStruct(coherency_field.shape, jnp.float32),
        in_specs=[vmem, vmem],
        out_specs=vmem,
    )(coherency_field, sums)


def solution(mesh):
    in_specs = (P(None, "rows", "offs"), P())
    out_specs = P(None, "rows", "offs")
    return jax.shard_map(
        per_device, mesh=mesh, in_specs=in_specs, out_specs=out_specs, check_vma=False
    )
```

```python
import functools
import math

import jax
import jax.numpy as jnp
import numpy as np
from jax import lax
from jax.experimental import pallas as pl
from jax.experimental.pallas import tpu as pltpu
from jax.sharding import PartitionSpec as P

SEARCH = 6
PATCH = 3
SIDE = 2 * PATCH + 1
SPAN = 2 * SEARCH + 1
RIM = SEARCH + PATCH
STRENGTH = 1.5
LANES = 128
PAD = 16
CHANS = 9
FEATS = 2 * CHANS + 1
BATCH = 40
AHEAD = 1
GROUP = 40
FAR = 1e30
SPARE = 120
BANKS = 16
EXPONENT = -math.log2(math.e) / (STRENGTH * SIDE * SIDE)


def hermitian_inverse(matrix):
    diag_one, diag_two, diag_three = matrix[0], matrix[1], matrix[2]
    re_onetwo, re_onethree, re_twothree = matrix[3], matrix[4], matrix[5]
    im_onetwo, im_onethree, im_twothree = matrix[6], matrix[7], matrix[8]
    abs_onetwo = re_onetwo * re_onetwo + im_onetwo * im_onetwo
    abs_onethree = re_onethree * re_onethree + im_onethree * im_onethree
    abs_twothree = re_twothree * re_twothree + im_twothree * im_twothree
    yz_real = re_onethree * re_twothree + im_onethree * im_twothree
    yz_imag = im_onethree * re_twothree - re_onethree * im_twothree
    xz_real = re_onetwo * re_twothree - im_onetwo * im_twothree
    xz_imag = re_onetwo * im_twothree + im_onetwo * re_twothree
    yx_real = re_onethree * re_onetwo + im_onethree * im_onetwo
    yx_imag = im_onethree * re_onetwo - re_onethree * im_onetwo
    triple_real = xz_real * re_onethree + xz_imag * im_onethree
    determinant = (
        diag_one * diag_two * diag_three
        + 2.0 * triple_real
        - diag_one * abs_twothree
        - diag_two * abs_onethree
        - diag_three * abs_onetwo
    )
    adjugate = [
        diag_two * diag_three - abs_twothree,
        diag_one * diag_three - abs_onethree,
        diag_one * diag_two - abs_onetwo,
        -(re_onetwo * diag_three - yz_real),
        xz_real - re_onethree * diag_two,
        -(diag_one * re_twothree - yx_real),
        -(im_onetwo * diag_three - yz_imag),
        xz_imag - im_onethree * diag_two,
        -(diag_one * im_twothree - yx_imag),
    ]
    return adjugate, determinant


def edge_pairs(cols):
    pairs = []
    for step in range(-SEARCH, SEARCH + 1):
        for column in range(-PATCH, cols + PATCH):
            if not (0 <= column < cols and 0 <= column + step < cols):
                pairs.append((step, column))
    return pairs


def band_matrix(cols):
    source = np.arange(cols)[:, None]
    target = np.arange(cols)[None, :]
    main = (np.abs(source - target) <= PATCH).astype(np.float32)
    edge = np.zeros((LANES, cols), np.float32)
    for lane, (_, column) in enumerate(edge_pairs(cols)):
        edge[lane] = np.abs(np.arange(cols) - column) <= PATCH
    high, low = edge.copy(), edge.copy()
    for place in range(SEARCH):
        high[SPARE + place, place] = 1.0
        low[SPARE + place, cols - SEARCH + place] = 1.0
    high[SPARE + SEARCH] = 1.0
    return np.concatenate([main, main, high, low], 0)


def select_matrix(cols):
    pick = np.zeros((LANES, 2 * LANES), np.float32)
    for lane, (step, column) in enumerate(edge_pairs(cols)):
        source = column + 32 if column < 32 else column - cols + 96
        pick[source, lane] = 1.0
        pick[source + step, LANES + lane] = 1.0
    return np.concatenate([pick] * 3, 0)


def keep_masks(cols):
    keep = np.zeros((SPAN, 16, LANES), np.float32)
    for lane, (step, _) in enumerate(edge_pairs(cols)):
        keep[step + SEARCH, :, lane] = 1.0
    return keep


def gain(feature):
    if feature == 2 * CHANS:
        return -6.0
    return 1.0 if feature % CHANS < 3 else 2.0


def partner(feature):
    if feature == 2 * CHANS:
        return feature
    return (feature + CHANS) % (2 * CHANS)


def despeckle(
    sizes, offs_ref, field_ref, band_ref, pick_ref, keep_ref, out_ref,
    above_ref, below_ref, left_ref, right_ref, packs, send_sems, recv_sems,
    feats, moved, own, edges, edge_own, edge_other, edge_dist, edge_sum, dist, sums, weights, keeps,
):
    rows, cols, row_total, col_total = sizes
    span_rows = rows + 2 * PAD
    edge_rows = edges.shape[0] // FEATS
    row_tiles = span_rows // 8
    head, tail = PAD // 8, (PAD + rows) // 8
    halves = cols // LANES
    dist_tiles = (rows + 8) // 8
    near_tile, far_tile = 2, dist_tiles - 2
    count = offs_ref.shape[1]
    lane = lax.broadcasted_iota(jnp.int32, (8, LANES), 1)
    sub = lax.broadcasted_iota(jnp.int32, (8, LANES), 0)
    wide_sub = lax.broadcasted_iota(jnp.int32, (16, LANES), 0)
    wide_lane = lax.broadcasted_iota(jnp.int32, (16, LANES), 1)
    row, col = lax.axis_index("rows"), lax.axis_index("offs")
    row_start, col_start = row * rows, col * cols
    row_count, col_count = lax.axis_size("rows"), lax.axis_size("offs")
    f32, bf16 = jnp.float32, jnp.bfloat16

    def present(down, side):
        return (row + down >= 0) & (row + down < row_count) & (col + side >= 0) & (col + side < col_count)

    around = [(down, side) for down in (-1, 0, 1) for side in (-1, 0, 1) if (down, side) != (0, 0)]
    barrier = pltpu.get_barrier_semaphore()
    for down, side in around:

        @pl.when(present(down, side))
        def _(down=down, side=side):
            pl.semaphore_signal(
                barrier, inc=1, device_id=(row + down, col + side), device_id_type=pl.DeviceIdType.MESH
            )


    def pack(tile, _):
        at = pl.ds(pl.multiple_of(tile * 8, 8), 8)
        first = field_ref[0, at, :LANES]
        last = pltpu.roll(field_ref[0, at, cols - LANES :], RIM, 1)
        for c in range(1, CHANS):
            here = (lane >= RIM * c) & (lane < RIM * (c + 1))
            first = jnp.where(here, pltpu.roll(field_ref[c, at, :LANES], RIM * c, 1), first)
            last = jnp.where(here, pltpu.roll(field_ref[c, at, cols - LANES :], (RIM * c + RIM) % LANES, 1), last)
        packs[0, at, :] = first
        packs[1, at, :] = last
        return 0

    lax.fori_loop(0, rows // 8, pack, 0)

    copies = []
    for k, (down, side) in enumerate(around):
        start, size, put = {-1: (0, PAD, PAD + rows), 0: (0, rows, PAD), 1: (rows - PAD, PAD, 0)}[down]
        if side == 0:
            source = field_ref.at[:, start : start + size, :]
            target = below_ref if down < 0 else above_ref
        else:
            source = packs.at[0 if side < 0 else 1, start : start + size, :]
            target = (right_ref if side < 0 else left_ref).at[put : put + size, :]
        copies.append(pltpu.make_async_remote_copy(
            src_ref=source, dst_ref=target, send_sem=send_sems.at[k], recv_sem=recv_sems.at[k],
            device_id=(row + down, col + side), device_id_type=pl.DeviceIdType.MESH,
        ))

    def features(source_ref, first, groups, tile, _):
        at = pl.ds(pl.multiple_of(tile * 8, 8), 8)
        source_at = pl.ds(pl.multiple_of(tile * 8 - first, 8), 8)
        place = tile * 8 - PAD + sub
        in_rows = (place >= -RIM) & (place < rows + RIM) & (place + row_start >= 0) & (place + row_start < row_total)
        for group in groups:
            column = (group - 1) * LANES + lane
            inside = (
                in_rows & (column >= -RIM) & (column < cols + RIM)
                & (column + col_start >= 0) & (column + col_start < col_total)
            )
            if group == 0:
                packed = left_ref[at, :]
                cells = [pltpu.roll(packed, LANES - RIM - RIM * c, 1) for c in range(CHANS)]
            elif group == halves + 1:
                packed = right_ref[at, :]
                cells = [pltpu.roll(packed, LANES - RIM * c, 1) if c else packed for c in range(CHANS)]
            else:
                cells = [source_ref[c, source_at, (group - 1) * LANES : group * LANES] for c in range(CHANS)]
            adjugate, determinant = hermitian_inverse(cells)
            scale = 1.0 / determinant
            for c in range(CHANS):
                feats[group, c, at, :] = jnp.where(inside, cells[c], 0.0)
                feats[group, CHANS + c, at, :] = jnp.where(inside, adjugate[c] * scale, 0.0)
            feats[group, 2 * CHANS, at, :] = jnp.where(inside, 1.0, 0.0)
        return 0

    def shifts(tile, _):
        at = pl.ds(pl.multiple_of(tile * 8, 8), 8)
        zero = jnp.zeros((8, LANES), f32)
        for step in range(-SEARCH, SEARCH + 1):
            for half in range(halves):
                partner_col = half * LANES + lane + step
                moved[step + SEARCH, half, 2 * CHANS, at, :] = jnp.where(
                    (partner_col >= 0) & (partner_col < cols), feats[half + 1, 2 * CHANS, at, :], 0.0
                )
        for c in range(2 * CHANS):
            cells = [zero] + [feats[half + 1, c, at, :] for half in range(halves)] + [zero]
            for step in range(-SEARCH, SEARCH + 1):
                for half in range(halves):
                    here = cells[half + 1]
                    if step > 0:
                        value = pltpu.roll(jnp.where(lane >= step, here, cells[half + 2]), LANES - step, 1)
                    elif step < 0:
                        value = pltpu.roll(jnp.where(lane < LANES + step, here, cells[half]), -step, 1)
                    else:
                        value = here
                    moved[step + SEARCH, half, c, at, :] = value
        return 0

    def own_tiles(tile, _):
        at = pl.ds(pl.multiple_of(tile * 8, 8), 8)
        for half in range(halves):
            for c in range(FEATS):
                own[half, c, at, :] = gain(c) * feats[half + 1, partner(c), pl.ds(tile * 8 + PAD - PATCH, 8), :]
        return 0

    def distances(turn, downs, sides, step, _):
        half, tile = step % halves, step // halves
        at = pl.ds(pl.multiple_of(tile * 8, 8), 8)
        mine = [own[half, c, at, :] for c in range(FEATS)]
        for j in range(BATCH):
            rows_at = pl.ds(tile * 8 + PAD - PATCH + downs[j], 8)
            terms = [None, None]
            for c in range(FEATS):
                term = mine[c] * moved[sides[j], half, c, rows_at, :]
                terms[c % 2] = term if terms[c % 2] is None else terms[c % 2] + term
            dist[turn * BATCH + j, half, at, :] = terms[0] + terms[1]
        return 0

    def distance_batch(spans, turn, _):
        downs = [offs_ref[0, turn * BATCH + j] for j in range(BATCH)]
        sides = [offs_ref[1, turn * BATCH + j] + SEARCH for j in range(BATCH)]
        for start, stop in spans:
            lax.fori_loop(start * halves, stop * halves, functools.partial(distances, turn, downs, sides), 0)
        return 0

    inner = tuple(range(1, halves + 1))
    lax.fori_loop(head, tail, functools.partial(features, field_ref, PAD, inner), 0)
    def distance_span(first_batch, last_batch, start, stop):
        span = functools.partial(distance_batch, ((start, stop),))
        lax.fori_loop(first_batch, last_batch, span, 0)

    lax.fori_loop(head, tail, shifts, 0)
    lax.fori_loop(near_tile, far_tile, own_tiles, 0)
    distance_span(0, AHEAD, near_tile, far_tile)
    over = 1 + (row > 0).astype(jnp.int32) + (row < row_count - 1).astype(jnp.int32)
    across = 1 + (col > 0).astype(jnp.int32) + (col < col_count - 1).astype(jnp.int32)
    pl.semaphore_wait(barrier, over * across - 1)
    for (down, side), copy in zip(around, copies):
        pl.when(present(down, side))(copy.start)
    distance_span(AHEAD, count // BATCH, near_tile, far_tile)

    for (down, side), copy in zip(around, copies):
        if (down, side) == (-1, 0):
            pl.when(present(-down, -side))(copy.wait_recv)
    lax.fori_loop(tail, row_tiles, functools.partial(features, below_ref, PAD + rows, inner), 0)
    lax.fori_loop(tail, row_tiles, shifts, 0)
    lax.fori_loop(far_tile, dist_tiles, own_tiles, 0)
    distance_span(0, count // BATCH, far_tile, dist_tiles)

    for (down, side), copy in zip(around, copies):
        pl.when(present(down, side))(copy.wait_send)
        if (down, side) != (-1, 0):
            pl.when(present(-down, -side))(copy.wait_recv)
    outer = (0, halves + 1)
    lax.fori_loop(0, head, functools.partial(features, above_ref, 0, outer + inner), 0)
    lax.fori_loop(head, tail, functools.partial(features, field_ref, PAD, outer), 0)
    lax.fori_loop(tail, row_tiles, functools.partial(features, below_ref, PAD + rows, outer), 0)
    lax.fori_loop(0, head, shifts, 0)
    lax.fori_loop(0, near_tile, own_tiles, 0)
    distance_span(0, count // BATCH, 0, near_tile)

    def split(value):
        high = value.astype(bf16)
        return high, (value - high.astype(f32)).astype(bf16)

    def edge_columns(tile, _):
        at = pl.ds(pl.multiple_of(tile * 16, 16), 16)
        for c in range(FEATS):
            cells = [feats[group, c, at, :] for group in range(halves + 2)]
            before = pltpu.roll(jnp.where(wide_lane >= 96, cells[0], cells[1]), 32, 1)
            after = pltpu.roll(jnp.where(wide_lane >= 96, cells[halves], cells[halves + 1]), 96, 1)
            value = jnp.where(wide_lane < 64, before, after)
            high = value.astype(bf16)
            middle, low = split(value - high.astype(f32))
            edge_at = pl.ds(pl.multiple_of(c * edge_rows + tile * 16, 16), 16)
            edges[edge_at, :LANES] = high
            edges[edge_at, LANES : 2 * LANES] = middle
            edges[edge_at, 2 * LANES :] = low
        return 0

    def patches(tile, _):
        at = pl.ds(pl.multiple_of(tile * 8, 8), 8)
        for c in range(CHANS):
            before, after = feats[0, c, at, :], feats[halves + 1, c, at, :]
            for step in range(1, SEARCH + 1):
                up, down = (step + SEARCH, halves - 1, c, at), (SEARCH - step, 0, c, at)
                moved[up] = jnp.where(lane >= LANES - step, pltpu.roll(after, LANES - step, 1), moved[up])
                moved[down] = jnp.where(lane < step, pltpu.roll(before, step, 1), moved[down])
        return 0

    lax.fori_loop(0, row_tiles // 2, edge_columns, 0)
    both = jnp.dot(edges[...], pick_ref[...], preferred_element_type=f32)
    edge_own[...] = both[:, :LANES]
    edge_other[...] = both[:, LANES:]

    def edge_tiles(tile, _):
        at = pl.ds(pl.multiple_of(tile * 8, 8), 8)
        mine = [
            gain(c) * edge_own[pl.ds(partner(c) * edge_rows + tile * 8 + PAD - PATCH, 8), :]
            for c in range(FEATS)
        ]
        for step in range(SPAN):
            value = None
            for c in range(FEATS):
                rows_at = pl.ds(c * edge_rows + tile * 8 + PAD - PATCH - SEARCH + step, 8)
                term = mine[c] * edge_other[rows_at, :]
                value = term if value is None else value + term
            edge_dist[step, at, :] = value
        return 0

    lax.fori_loop(0, dist_tiles, edge_tiles, 0)

    def edge_sums(step, _):
        for part in range(rows // 16):
            value = edge_dist[step, pl.ds(16 * part, 16), :]
            for s in range(1, SIDE):
                value = value + edge_dist[step, pl.ds(16 * part + s, 16), :]
            partner_row = row_start + 16 * part + wide_sub + step - SEARCH
            outside = (partner_row < 0) | (partner_row >= row_total)
            high, low = split(jnp.where(wide_lane >= SPARE, 0.0, value))
            far = jnp.where((wide_lane < SPARE + SEARCH) | outside, FAR, 0.0)
            high = jnp.where(wide_lane >= SPARE, far, high.astype(f32)).astype(bf16)
            low = jnp.where(wide_lane >= SPARE, FAR, low.astype(f32)).astype(bf16)
            edge_sum[step, 16 * part : 16 * part + 16, :LANES] = high
            edge_sum[step, 16 * part : 16 * part + 16, LANES:] = low
        return 0

    lax.fori_loop(0, SPAN, edge_sums, 0)

    def keep_tables(step, _):
        place = wide_lane - SPARE
        known = keep_ref[step].astype(f32)
        before = col_start + place + step - SEARCH < 0
        after = col_start + cols - SEARCH + place + step - SEARCH >= col_total
        spare = (place >= 0) & (place < SEARCH)
        high = jnp.where((spare & before) | (place == SEARCH), 1.0, known)
        low = jnp.where(spare & after, 1.0, known)
        keeps[step, :, :LANES] = high.astype(bf16)
        keeps[step, :, LANES:] = low.astype(bf16)
        return 0

    lax.fori_loop(0, SPAN, keep_tables, 0)
    out_ref[...] = jnp.zeros_like(out_ref)
    chunk = GROUP * rows // 2

    def window(turn, j, _):
        k = turn * GROUP + j
        down = offs_ref[0, k] + SEARCH
        keep = keeps[offs_ref[1, k] + SEARCH]
        for part in range(rows // 16):
            at = pl.ds(pl.multiple_of(j * rows + 16 * part, 16), 16)
            for half in range(halves):
                value = dist[k, half, pl.ds(16 * part, 16), :]
                for s in range(1, SIDE):
                    value = value + dist[k, half, pl.ds(16 * part + s, 16), :]
                high, low = split(value)
                sums[at, half * LANES : (half + 1) * LANES] = high
                sums[at, cols + half * LANES : cols + (half + 1) * LANES] = low
            for which in range(2):
                span = slice(which * LANES, (which + 1) * LANES)
                sums[at, 2 * cols + which * LANES : 2 * cols + (which + 1) * LANES] = (
                    edge_sum[down, 16 * part : 16 * part + 16, span] * keep[:, span]
                )
        return 0

    def weigh(piece, _):
        at = pl.ds(pl.multiple_of(piece * chunk, chunk), chunk)
        patch = jnp.dot(sums[at, :], band_ref[...], preferred_element_type=f32)
        weights[at, :] = jnp.exp2(patch * EXPONENT)
        return 0

    def accumulate(turn, downs, sides, tile, _):
        at = pl.ds(pl.multiple_of(tile * 8, 8), 8)
        for half in range(halves):
            span = slice(half * LANES, (half + 1) * LANES)
            total = [out_ref[c, at, span] for c in range(CHANS + 1)]
            for j in range(GROUP):
                rows_at = pl.ds(tile * 8 + PAD + downs[j], 8)
                weight = weights[pl.ds(pl.multiple_of(j * rows + tile * 8, 8), 8), span]
                for c in range(CHANS):
                    total[c] = total[c] + weight * moved[sides[j], half, c, rows_at, :]
                total[CHANS] = total[CHANS] + weight
            for c in range(CHANS + 1):
                out_ref[c, at, span] = total[c]
        return 0

    def weigh_and_add(turn):
        downs = [offs_ref[0, turn * GROUP + j] for j in range(GROUP)]
        sides = [offs_ref[1, turn * GROUP + j] + SEARCH for j in range(GROUP)]
        lax.fori_loop(0, 2, weigh, 0)
        lax.fori_loop(0, rows // 8, functools.partial(accumulate, turn, downs, sides), 0)

    def group(turn, _):
        lax.fori_loop(0, GROUP, functools.partial(window, turn), 0)
        weigh_and_add(turn)
        return 0

    pace = GROUP // (row_tiles - 2)

    def first_group(tile, _):
        patches(tile, 0)
        for j in range(pace):
            window(0, (tile - 1) * pace + j, 0)
        return 0

    lax.fori_loop(1, row_tiles - 1, first_group, 0)
    lax.fori_loop(pace * (row_tiles - 2), GROUP, functools.partial(window, 0), 0)
    weigh_and_add(0)
    lax.fori_loop(1, count // GROUP, group, 0)


def finish(field_ref, sums_ref, out_ref):
    def tile_rows(tile, _):
        at = pl.ds(pl.multiple_of(tile * 8, 8), 8)
        scale = 1.0 / (1.0 + sums_ref[CHANS, at, :])
        for c in range(CHANS):
            out_ref[c, at, :] = (field_ref[c, at, :] + sums_ref[c, at, :]) * scale
        return 0

    lax.fori_loop(0, field_ref.shape[1] // 8, tile_rows, 0)


def filter_block(sizes, offsets, field):
    rows, cols = sizes[:2]
    span_rows = rows + 2 * PAD
    edge_rows = span_rows + BANKS
    halves = cols // LANES
    vmem = pl.BlockSpec(memory_space=pltpu.VMEM)
    smem = pl.BlockSpec(memory_space=pltpu.SMEM)
    f32, bf16 = jnp.float32, jnp.bfloat16
    return pl.pallas_call(
        functools.partial(despeckle, sizes),
        out_shape=jax.ShapeDtypeStruct((CHANS + 1, rows, cols), f32),
        in_specs=[smem] + [vmem] * 4,
        out_specs=vmem,
        scratch_shapes=[
            pltpu.VMEM((CHANS, PAD, cols), f32),
            pltpu.VMEM((CHANS, PAD, cols), f32),
            pltpu.VMEM((span_rows, LANES), f32),
            pltpu.VMEM((span_rows, LANES), f32),
            pltpu.VMEM((2, rows, LANES), f32),
            pltpu.SemaphoreType.DMA((8,)),
            pltpu.SemaphoreType.DMA((8,)),
            pltpu.VMEM((halves + 2, FEATS, span_rows + BANKS, LANES), f32),
            pltpu.VMEM((SPAN, halves, FEATS, span_rows + BANKS, LANES), f32),
            pltpu.VMEM((halves, FEATS, rows + BANKS, LANES), f32),
            pltpu.VMEM((FEATS * edge_rows, 3 * LANES), bf16),
            pltpu.VMEM((FEATS * edge_rows, LANES), f32),
            pltpu.VMEM((FEATS * edge_rows, LANES), f32),
            pltpu.VMEM((SPAN, rows + 8, LANES), f32),
            pltpu.VMEM((SPAN, rows, 2 * LANES), bf16),
            pltpu.VMEM((offsets.shape[0], halves, rows + 8, LANES), f32),
            pltpu.VMEM((GROUP * rows, 2 * cols + 2 * LANES), bf16),
            pltpu.VMEM((GROUP * rows, cols), f32),
            pltpu.VMEM((SPAN, 16, 2 * LANES), bf16),
        ],
        compiler_params=pltpu.CompilerParams(
            vmem_limit_bytes=62 * 1024 * 1024, collective_id=0, has_side_effects=True
        ),
    )(
        offsets.T, field, jnp.asarray(band_matrix(cols), bf16), jnp.asarray(select_matrix(cols), bf16),
        jnp.asarray(keep_masks(cols), bf16),
    )


def per_device(coherency_field, offsets):
    _, rows, cols = coherency_field.shape
    row_total = rows * lax.axis_size("rows")
    col_total = cols * lax.axis_size("offs")
    sums = filter_block((rows, cols, row_total, col_total), offsets, coherency_field)
    vmem = pl.BlockSpec(memory_space=pltpu.VMEM)
    return pl.pallas_call(
        finish,
        out_shape=jax.ShapeDtypeStruct(coherency_field.shape, jnp.float32),
        in_specs=[vmem, vmem],
        out_specs=vmem,
    )(coherency_field, sums)


def solution(mesh):
    in_specs = (P(None, "rows", "offs"), P())
    out_specs = P(None, "rows", "offs")
    return jax.shard_map(
        per_device, mesh=mesh, in_specs=in_specs, out_specs=out_specs, check_vma=False
    )
```

```python
import functools
import math

import jax
import jax.numpy as jnp
import numpy as np
from jax import lax
from jax.experimental import pallas as pl
from jax.experimental.pallas import tpu as pltpu
from jax.sharding import PartitionSpec as P

SEARCH = 6
PATCH = 3
SIDE = 2 * PATCH + 1
SPAN = 2 * SEARCH + 1
RIM = SEARCH + PATCH
STRENGTH = 1.5
LANES = 128
PAD = 16
CHANS = 9
FEATS = 2 * CHANS + 1
BATCH = 40
AHEAD = 2
GROUP = 40
FAR = -1e30
SPARE = 120
BANKS = 16
EXPONENT = -math.log2(math.e) / (STRENGTH * SIDE * SIDE)


def hermitian_inverse(matrix):
    diag_one, diag_two, diag_three = matrix[0], matrix[1], matrix[2]
    re_onetwo, re_onethree, re_twothree = matrix[3], matrix[4], matrix[5]
    im_onetwo, im_onethree, im_twothree = matrix[6], matrix[7], matrix[8]
    abs_onetwo = re_onetwo * re_onetwo + im_onetwo * im_onetwo
    abs_onethree = re_onethree * re_onethree + im_onethree * im_onethree
    abs_twothree = re_twothree * re_twothree + im_twothree * im_twothree
    yz_real = re_onethree * re_twothree + im_onethree * im_twothree
    yz_imag = im_onethree * re_twothree - re_onethree * im_twothree
    xz_real = re_onetwo * re_twothree - im_onetwo * im_twothree
    xz_imag = re_onetwo * im_twothree + im_onetwo * re_twothree
    yx_real = re_onethree * re_onetwo + im_onethree * im_onetwo
    yx_imag = im_onethree * re_onetwo - re_onethree * im_onetwo
    triple_real = xz_real * re_onethree + xz_imag * im_onethree
    determinant = (
        diag_one * diag_two * diag_three
        + 2.0 * triple_real
        - diag_one * abs_twothree
        - diag_two * abs_onethree
        - diag_three * abs_onetwo
    )
    adjugate = [
        diag_two * diag_three - abs_twothree,
        diag_one * diag_three - abs_onethree,
        diag_one * diag_two - abs_onetwo,
        -(re_onetwo * diag_three - yz_real),
        xz_real - re_onethree * diag_two,
        -(diag_one * re_twothree - yx_real),
        -(im_onetwo * diag_three - yz_imag),
        xz_imag - im_onethree * diag_two,
        -(diag_one * im_twothree - yx_imag),
    ]
    return adjugate, determinant


def edge_pairs(cols):
    pairs = []
    for step in range(-SEARCH, SEARCH + 1):
        for column in range(-PATCH, cols + PATCH):
            if not (0 <= column < cols and 0 <= column + step < cols):
                pairs.append((step, column))
    return pairs


def band_matrix(cols):
    source = np.arange(cols)[:, None]
    target = np.arange(cols)[None, :]
    main = (np.abs(source - target) <= PATCH).astype(np.float32)
    edge = np.zeros((LANES, cols), np.float32)
    for lane, (_, column) in enumerate(edge_pairs(cols)):
        edge[lane] = np.abs(np.arange(cols) - column) <= PATCH
    high, low = edge.copy(), edge.copy()
    for place in range(SEARCH):
        high[SPARE + place, place] = 1.0
        low[SPARE + place, cols - SEARCH + place] = 1.0
    high[SPARE + SEARCH] = 1.0
    return np.concatenate([main, main, high, low], 0)


def select_matrix(cols):
    pick = np.zeros((LANES, 2 * LANES), np.float32)
    for lane, (step, column) in enumerate(edge_pairs(cols)):
        source = column + 32 if column < 32 else column - cols + 96
        pick[source, lane] = 1.0
        pick[source + step, LANES + lane] = 1.0
    return np.concatenate([pick] * 3, 0)


def keep_masks(cols):
    keep = np.zeros((SPAN, 16, LANES), np.float32)
    for lane, (step, _) in enumerate(edge_pairs(cols)):
        keep[step + SEARCH, :, lane] = 1.0
    return keep


def gain(feature):
    if feature == 2 * CHANS:
        return -6.0 * EXPONENT
    return (1.0 if feature % CHANS < 3 else 2.0) * EXPONENT


def partner(feature):
    if feature == 2 * CHANS:
        return feature
    return (feature + CHANS) % (2 * CHANS)


def despeckle(
    sizes, offs_ref, field_ref, band_ref, pick_ref, keep_ref, out_ref,
    above_ref, below_ref, left_ref, right_ref, packs, send_sems, recv_sems,
    feats, moved, own, edges, edge_own, edge_other, edge_dist, edge_sum, dist, sums, weights, keeps,
):
    rows, cols, row_total, col_total = sizes
    span_rows = rows + 2 * PAD
    edge_rows = edges.shape[0] // FEATS
    row_tiles = span_rows // 8
    head, tail = PAD // 8, (PAD + rows) // 8
    halves = cols // LANES
    dist_tiles = (rows + 8) // 8
    near_tile, far_tile = 2, dist_tiles - 2
    count = offs_ref.shape[1]
    lane = lax.broadcasted_iota(jnp.int32, (8, LANES), 1)
    sub = lax.broadcasted_iota(jnp.int32, (8, LANES), 0)
    wide_sub = lax.broadcasted_iota(jnp.int32, (16, LANES), 0)
    wide_lane = lax.broadcasted_iota(jnp.int32, (16, LANES), 1)
    row, col = lax.axis_index("rows"), lax.axis_index("offs")
    row_start, col_start = row * rows, col * cols
    row_count, col_count = lax.axis_size("rows"), lax.axis_size("offs")
    f32, bf16 = jnp.float32, jnp.bfloat16

    def present(down, side):
        return (row + down >= 0) & (row + down < row_count) & (col + side >= 0) & (col + side < col_count)

    around = [(down, side) for down in (-1, 0, 1) for side in (-1, 0, 1) if (down, side) != (0, 0)]
    barrier = pltpu.get_barrier_semaphore()
    for down, side in around:

        @pl.when(present(down, side))
        def _(down=down, side=side):
            pl.semaphore_signal(
                barrier, inc=1, device_id=(row + down, col + side), device_id_type=pl.DeviceIdType.MESH
            )


    def pack(tile, _):
        at = pl.ds(pl.multiple_of(tile * 8, 8), 8)
        first = field_ref[0, at, :LANES]
        last = pltpu.roll(field_ref[0, at, cols - LANES :], RIM, 1)
        for c in range(1, CHANS):
            here = (lane >= RIM * c) & (lane < RIM * (c + 1))
            first = jnp.where(here, pltpu.roll(field_ref[c, at, :LANES], RIM * c, 1), first)
            last = jnp.where(here, pltpu.roll(field_ref[c, at, cols - LANES :], (RIM * c + RIM) % LANES, 1), last)
        packs[0, at, :] = first
        packs[1, at, :] = last
        return 0

    lax.fori_loop(0, rows // 8, pack, 0)

    copies = []
    for k, (down, side) in enumerate(around):
        start, size, put = {-1: (0, PAD, PAD + rows), 0: (0, rows, PAD), 1: (rows - PAD, PAD, 0)}[down]
        if side == 0:
            source = field_ref.at[:, start : start + size, :]
            target = below_ref if down < 0 else above_ref
        else:
            source = packs.at[0 if side < 0 else 1, start : start + size, :]
            target = (right_ref if side < 0 else left_ref).at[put : put + size, :]
        copies.append(pltpu.make_async_remote_copy(
            src_ref=source, dst_ref=target, send_sem=send_sems.at[k], recv_sem=recv_sems.at[k],
            device_id=(row + down, col + side), device_id_type=pl.DeviceIdType.MESH,
        ))

    def features(source_ref, first, groups, tile, _):
        at = pl.ds(pl.multiple_of(tile * 8, 8), 8)
        source_at = pl.ds(pl.multiple_of(tile * 8 - first, 8), 8)
        place = tile * 8 - PAD + sub
        in_rows = (place >= -RIM) & (place < rows + RIM) & (place + row_start >= 0) & (place + row_start < row_total)
        for group in groups:
            column = (group - 1) * LANES + lane
            inside = (
                in_rows & (column >= -RIM) & (column < cols + RIM)
                & (column + col_start >= 0) & (column + col_start < col_total)
            )
            if group == 0:
                packed = left_ref[at, :]
                cells = [pltpu.roll(packed, LANES - RIM - RIM * c, 1) for c in range(CHANS)]
            elif group == halves + 1:
                packed = right_ref[at, :]
                cells = [pltpu.roll(packed, LANES - RIM * c, 1) if c else packed for c in range(CHANS)]
            else:
                cells = [source_ref[c, source_at, (group - 1) * LANES : group * LANES] for c in range(CHANS)]
            adjugate, determinant = hermitian_inverse(cells)
            scale = 1.0 / determinant
            for c in range(CHANS):
                feats[group, c, at, :] = jnp.where(inside, cells[c], 0.0)
                feats[group, CHANS + c, at, :] = jnp.where(inside, adjugate[c] * scale, 0.0)
            feats[group, 2 * CHANS, at, :] = jnp.where(inside, 1.0, 0.0)
        return 0

    def shift_validity(tile, _):
        at = pl.ds(pl.multiple_of(tile * 8, 8), 8)
        for step in range(-SEARCH, SEARCH + 1):
            for half in range(halves):
                partner_col = half * LANES + lane + step
                moved[step + SEARCH, half, 2 * CHANS, at, :] = jnp.where(
                    (partner_col >= 0) & (partner_col < cols), feats[half + 1, 2 * CHANS, at, :], 0.0
                )
        return 0

    def shift_piece(tile, c, step, half):
        at = pl.ds(pl.multiple_of(tile * 8, 8), 8)
        value = feats[half + 1, c, at, :]
        if step:
            beyond = half + (1 if step > 0 else -1)
            other = feats[beyond + 1, c, at, :] if 0 <= beyond < halves else jnp.zeros((8, LANES), f32)
            own_lanes = lane >= step if step > 0 else lane < LANES + step
            value = pltpu.roll(jnp.where(own_lanes, value, other), (LANES - step) % LANES, 1)
        moved[step + SEARCH, half, c, at, :] = value

    pieces = [(step, half) for step in range(-SEARCH, SEARCH + 1) for half in range(halves)]

    def shifts(tile, _):
        shift_validity(tile, 0)
        for c in range(2 * CHANS):
            for step, half in pieces:
                shift_piece(tile, c, step, half)
        return 0

    def own_tiles(tile, _):
        at = pl.ds(pl.multiple_of(tile * 8, 8), 8)
        for half in range(halves):
            for c in range(FEATS):
                own[half, c, at, :] = gain(c) * feats[half + 1, partner(c), pl.ds(tile * 8 + PAD - PATCH, 8), :]
        return 0

    def distances(turn, downs, sides, beside, step, _):
        half, tile = step % halves, step // halves
        at = pl.ds(pl.multiple_of(tile * 8, 8), 8)
        mine = [own[half, c, at, :] for c in range(FEATS)]
        for j in range(BATCH):
            rows_at = pl.ds(tile * 8 + PAD - PATCH + downs[j], 8)
            terms = [None, None]
            for c in range(FEATS):
                term = mine[c] * moved[sides[j], half, c, rows_at, :]
                terms[c % 2] = term if terms[c % 2] is None else terms[c % 2] + term
            dist[turn * BATCH + j, half, at, :] = terms[0] + terms[1]
            for piece in beside[j::BATCH]:
                piece()
        return 0

    def distance_batch(spans, turn, _):
        downs = [offs_ref[0, turn * BATCH + j] for j in range(BATCH)]
        sides = [offs_ref[1, turn * BATCH + j] + SEARCH for j in range(BATCH)]
        for start, stop in spans:
            lax.fori_loop(start * halves, stop * halves, functools.partial(distances, turn, downs, sides, ()), 0)
        return 0

    inner = tuple(range(1, halves + 1))
    lax.fori_loop(head, tail, functools.partial(features, field_ref, PAD, inner), 0)
    def distance_span(first_batch, last_batch, start, stop):
        span = functools.partial(distance_batch, ((start, stop),))
        lax.fori_loop(first_batch, last_batch, span, 0)

    parts = halves * (count // BATCH)
    share = 2 * CHANS // parts
    reach = 4

    def inner_distances(shifting, index, _):
        tile, part = index // parts, index % parts
        half, turn = part % halves, part // halves
        downs = [offs_ref[0, turn * BATCH + j] for j in range(BATCH)]
        sides = [offs_ref[1, turn * BATCH + j] + SEARCH for j in range(BATCH)]
        beside = []
        if shifting:
            for k in range(share):
                for step, place in pieces:
                    beside.append(functools.partial(shift_piece, tile + reach, part * share + k, step, place))
        return distances(turn, downs, sides, beside, tile * halves + half, 0)

    lax.fori_loop(head, head + reach, shifts, 0)
    lax.fori_loop(head + reach, tail, shift_validity, 0)
    lax.fori_loop(near_tile, far_tile, own_tiles, 0)
    early, full = (near_tile + AHEAD) * parts, (tail - reach) * parts
    lax.fori_loop(near_tile * parts, early, functools.partial(inner_distances, True), 0)
    over = 1 + (row > 0).astype(jnp.int32) + (row < row_count - 1).astype(jnp.int32)
    across = 1 + (col > 0).astype(jnp.int32) + (col < col_count - 1).astype(jnp.int32)
    pl.semaphore_wait(barrier, over * across - 1)
    for (down, side), copy in zip(around, copies):
        pl.when(present(down, side))(copy.start)
    lax.fori_loop(early, full, functools.partial(inner_distances, True), 0)
    lax.fori_loop(full, far_tile * parts, functools.partial(inner_distances, False), 0)

    for (down, side), copy in zip(around, copies):
        if (down, side) == (-1, 0):
            pl.when(present(-down, -side))(copy.wait_recv)
    lax.fori_loop(tail, row_tiles, functools.partial(features, below_ref, PAD + rows, inner), 0)
    lax.fori_loop(tail, row_tiles, shifts, 0)
    lax.fori_loop(far_tile, dist_tiles, own_tiles, 0)
    distance_span(0, count // BATCH, far_tile, dist_tiles)

    for (down, side), copy in zip(around, copies):
        pl.when(present(down, side))(copy.wait_send)
        if (down, side) != (-1, 0):
            pl.when(present(-down, -side))(copy.wait_recv)
    outer = (0, halves + 1)
    lax.fori_loop(0, head, functools.partial(features, above_ref, 0, outer + inner), 0)
    lax.fori_loop(head, tail, functools.partial(features, field_ref, PAD, outer), 0)
    lax.fori_loop(tail, row_tiles, functools.partial(features, below_ref, PAD + rows, outer), 0)
    lax.fori_loop(0, head, shifts, 0)
    lax.fori_loop(0, near_tile, own_tiles, 0)
    distance_span(0, count // BATCH, 0, near_tile)

    def split(value):
        high = value.astype(bf16)
        return high, (value - high.astype(f32)).astype(bf16)

    def edge_columns(tile, _):
        at = pl.ds(pl.multiple_of(tile * 16, 16), 16)
        for c in range(FEATS):
            cells = [feats[group, c, at, :] for group in range(halves + 2)]
            before = pltpu.roll(jnp.where(wide_lane >= 96, cells[0], cells[1]), 32, 1)
            after = pltpu.roll(jnp.where(wide_lane >= 96, cells[halves], cells[halves + 1]), 96, 1)
            value = jnp.where(wide_lane < 64, before, after)
            high = value.astype(bf16)
            middle, low = split(value - high.astype(f32))
            edge_at = pl.ds(pl.multiple_of(c * edge_rows + tile * 16, 16), 16)
            edges[edge_at, :LANES] = high
            edges[edge_at, LANES : 2 * LANES] = middle
            edges[edge_at, 2 * LANES :] = low
        return 0

    def patches(tile, _):
        at = pl.ds(pl.multiple_of(tile * 8, 8), 8)
        for c in range(CHANS):
            before, after = feats[0, c, at, :], feats[halves + 1, c, at, :]
            for step in range(1, SEARCH + 1):
                up, down = (step + SEARCH, halves - 1, c, at), (SEARCH - step, 0, c, at)
                moved[up] = jnp.where(lane >= LANES - step, pltpu.roll(after, LANES - step, 1), moved[up])
                moved[down] = jnp.where(lane < step, pltpu.roll(before, step, 1), moved[down])
        return 0

    lax.fori_loop(0, row_tiles // 2, edge_columns, 0)
    both = jnp.dot(edges[...], pick_ref[...], preferred_element_type=f32)
    edge_own[...] = both[:, :LANES]
    edge_other[...] = both[:, LANES:]

    def edge_tiles(tile, _):
        at = pl.ds(pl.multiple_of(tile * 8, 8), 8)
        mine = [
            gain(c) * edge_own[pl.ds(partner(c) * edge_rows + tile * 8 + PAD - PATCH, 8), :]
            for c in range(FEATS)
        ]
        for step in range(SPAN):
            value = None
            for c in range(FEATS):
                rows_at = pl.ds(c * edge_rows + tile * 8 + PAD - PATCH - SEARCH + step, 8)
                term = mine[c] * edge_other[rows_at, :]
                value = term if value is None else value + term
            edge_dist[step, at, :] = value
        return 0

    lax.fori_loop(0, dist_tiles, edge_tiles, 0)

    def edge_sums(step, _):
        for part in range(rows // 16):
            value = edge_dist[step, pl.ds(16 * part, 16), :]
            for s in range(1, SIDE):
                value = value + edge_dist[step, pl.ds(16 * part + s, 16), :]
            partner_row = row_start + 16 * part + wide_sub + step - SEARCH
            outside = (partner_row < 0) | (partner_row >= row_total)
            high, low = split(jnp.where(wide_lane >= SPARE, 0.0, value))
            far = jnp.where((wide_lane < SPARE + SEARCH) | outside, FAR, 0.0)
            high = jnp.where(wide_lane >= SPARE, far, high.astype(f32)).astype(bf16)
            low = jnp.where(wide_lane >= SPARE, FAR, low.astype(f32)).astype(bf16)
            edge_sum[step, 16 * part : 16 * part + 16, :LANES] = high
            edge_sum[step, 16 * part : 16 * part + 16, LANES:] = low
        return 0

    lax.fori_loop(0, SPAN, edge_sums, 0)

    def keep_tables(step, _):
        place = wide_lane - SPARE
        known = keep_ref[step].astype(f32)
        before = col_start + place + step - SEARCH < 0
        after = col_start + cols - SEARCH + place + step - SEARCH >= col_total
        spare = (place >= 0) & (place < SEARCH)
        high = jnp.where((spare & before) | (place == SEARCH), 1.0, known)
        low = jnp.where(spare & after, 1.0, known)
        keeps[step, :, :LANES] = high.astype(bf16)
        keeps[step, :, LANES:] = low.astype(bf16)
        return 0

    lax.fori_loop(0, SPAN, keep_tables, 0)
    out_ref[...] = jnp.zeros_like(out_ref)
    chunk = GROUP * rows // 2

    def window(turn, j, _):
        k = turn * GROUP + j
        down = offs_ref[0, k] + SEARCH
        keep = keeps[offs_ref[1, k] + SEARCH]
        for part in range(rows // 16):
            at = pl.ds(pl.multiple_of(j * rows + 16 * part, 16), 16)
            for half in range(halves):
                value = dist[k, half, pl.ds(16 * part, 16), :]
                for s in range(1, SIDE):
                    value = value + dist[k, half, pl.ds(16 * part + s, 16), :]
                high, low = split(value)
                sums[at, half * LANES : (half + 1) * LANES] = high
                sums[at, cols + half * LANES : cols + (half + 1) * LANES] = low
            for which in range(2):
                span = slice(which * LANES, (which + 1) * LANES)
                sums[at, 2 * cols + which * LANES : 2 * cols + (which + 1) * LANES] = (
                    edge_sum[down, 16 * part : 16 * part + 16, span] * keep[:, span]
                )
        return 0

    def weigh(piece, _):
        at = pl.ds(pl.multiple_of(piece * chunk, chunk), chunk)
        patch = jnp.dot(sums[at, :], band_ref[...], preferred_element_type=f32)
        weights[at, :] = jnp.exp2(patch)
        return 0

    def accumulate(turn, downs, sides, tile, _):
        at = pl.ds(pl.multiple_of(tile * 8, 8), 8)
        for half in range(halves):
            span = slice(half * LANES, (half + 1) * LANES)
            total = [out_ref[c, at, span] for c in range(CHANS + 1)]
            for j in range(GROUP):
                rows_at = pl.ds(tile * 8 + PAD + downs[j], 8)
                weight = weights[pl.ds(pl.multiple_of(j * rows + tile * 8, 8), 8), span]
                for c in range(CHANS):
                    total[c] = total[c] + weight * moved[sides[j], half, c, rows_at, :]
                total[CHANS] = total[CHANS] + weight
            for c in range(CHANS + 1):
                out_ref[c, at, span] = total[c]
        return 0

    def weigh_and_add(turn):
        downs = [offs_ref[0, turn * GROUP + j] for j in range(GROUP)]
        sides = [offs_ref[1, turn * GROUP + j] + SEARCH for j in range(GROUP)]
        lax.fori_loop(0, 2, weigh, 0)
        lax.fori_loop(0, rows // 8, functools.partial(accumulate, turn, downs, sides), 0)

    def group(turn, _):
        lax.fori_loop(0, GROUP, functools.partial(window, turn), 0)
        weigh_and_add(turn)
        return 0

    pace = GROUP // (row_tiles - 2)

    def first_group(tile, _):
        patches(tile, 0)
        for j in range(pace):
            window(0, (tile - 1) * pace + j, 0)
        return 0

    lax.fori_loop(1, row_tiles - 1, first_group, 0)
    lax.fori_loop(pace * (row_tiles - 2), GROUP, functools.partial(window, 0), 0)
    weigh_and_add(0)
    lax.fori_loop(1, count // GROUP, group, 0)


def finish(field_ref, sums_ref, out_ref):
    def tile_rows(tile, _):
        at = pl.ds(pl.multiple_of(tile * 8, 8), 8)
        scale = 1.0 / (1.0 + sums_ref[CHANS, at, :])
        for c in range(CHANS):
            out_ref[c, at, :] = (field_ref[c, at, :] + sums_ref[c, at, :]) * scale
        return 0

    lax.fori_loop(0, field_ref.shape[1] // 8, tile_rows, 0)


def filter_block(sizes, offsets, field):
    rows, cols = sizes[:2]
    span_rows = rows + 2 * PAD
    edge_rows = span_rows + BANKS
    halves = cols // LANES
    vmem = pl.BlockSpec(memory_space=pltpu.VMEM)
    smem = pl.BlockSpec(memory_space=pltpu.SMEM)
    f32, bf16 = jnp.float32, jnp.bfloat16
    return pl.pallas_call(
        functools.partial(despeckle, sizes),
        out_shape=jax.ShapeDtypeStruct((CHANS + 1, rows, cols), f32),
        in_specs=[smem] + [vmem] * 4,
        out_specs=vmem,
        scratch_shapes=[
            pltpu.VMEM((CHANS, PAD, cols), f32),
            pltpu.VMEM((CHANS, PAD, cols), f32),
            pltpu.VMEM((span_rows, LANES), f32),
            pltpu.VMEM((span_rows, LANES), f32),
            pltpu.VMEM((2, rows, LANES), f32),
            pltpu.SemaphoreType.DMA((8,)),
            pltpu.SemaphoreType.DMA((8,)),
            pltpu.VMEM((halves + 2, FEATS, span_rows + BANKS, LANES), f32),
            pltpu.VMEM((SPAN, halves, FEATS, span_rows + BANKS, LANES), f32),
            pltpu.VMEM((halves, FEATS, rows + BANKS, LANES), f32),
            pltpu.VMEM((FEATS * edge_rows, 3 * LANES), bf16),
            pltpu.VMEM((FEATS * edge_rows, LANES), f32),
            pltpu.VMEM((FEATS * edge_rows, LANES), f32),
            pltpu.VMEM((SPAN, rows + 8, LANES), f32),
            pltpu.VMEM((SPAN, rows, 2 * LANES), bf16),
            pltpu.VMEM((offsets.shape[0], halves, rows + 8, LANES), f32),
            pltpu.VMEM((GROUP * rows, 2 * cols + 2 * LANES), bf16),
            pltpu.VMEM((GROUP * rows, cols), f32),
            pltpu.VMEM((SPAN, 16, 2 * LANES), bf16),
        ],
        compiler_params=pltpu.CompilerParams(
            vmem_limit_bytes=62 * 1024 * 1024, collective_id=0, has_side_effects=True
        ),
    )(
        offsets.T, field, jnp.asarray(band_matrix(cols), bf16), jnp.asarray(select_matrix(cols), bf16),
        jnp.asarray(keep_masks(cols), bf16),
    )


def per_device(coherency_field, offsets):
    _, rows, cols = coherency_field.shape
    row_total = rows * lax.axis_size("rows")
    col_total = cols * lax.axis_size("offs")
    sums = filter_block((rows, cols, row_total, col_total), offsets, coherency_field)
    vmem = pl.BlockSpec(memory_space=pltpu.VMEM)
    return pl.pallas_call(
        finish,
        out_shape=jax.ShapeDtypeStruct(coherency_field.shape, jnp.float32),
        in_specs=[vmem, vmem],
        out_specs=vmem,
    )(coherency_field, sums)


def solution(mesh):
    in_specs = (P(None, "rows", "offs"), P())
    out_specs = P(None, "rows", "offs")
    return jax.shard_map(
        per_device, mesh=mesh, in_specs=in_specs, out_specs=out_specs, check_vma=False
    )
```

```python
import functools
import math

import jax
import jax.numpy as jnp
import numpy as np
from jax import lax
from jax.experimental import pallas as pl
from jax.experimental.pallas import tpu as pltpu
from jax.sharding import PartitionSpec as P

SEARCH = 6
PATCH = 3
SIDE = 2 * PATCH + 1
SPAN = 2 * SEARCH + 1
RIM = SEARCH + PATCH
STRENGTH = 1.5
LANES = 128
PAD = 16
CHANS = 9
FEATS = 2 * CHANS + 1
BATCH = 40
AHEAD = 1
GROUP = 40
FAR = -1e30
SPARE = 120
BANKS = 16
EXPONENT = -math.log2(math.e) / (STRENGTH * SIDE * SIDE)


def hermitian_inverse(matrix):
    diag_one, diag_two, diag_three = matrix[0], matrix[1], matrix[2]
    re_onetwo, re_onethree, re_twothree = matrix[3], matrix[4], matrix[5]
    im_onetwo, im_onethree, im_twothree = matrix[6], matrix[7], matrix[8]
    abs_onetwo = re_onetwo * re_onetwo + im_onetwo * im_onetwo
    abs_onethree = re_onethree * re_onethree + im_onethree * im_onethree
    abs_twothree = re_twothree * re_twothree + im_twothree * im_twothree
    yz_real = re_onethree * re_twothree + im_onethree * im_twothree
    yz_imag = im_onethree * re_twothree - re_onethree * im_twothree
    xz_real = re_onetwo * re_twothree - im_onetwo * im_twothree
    xz_imag = re_onetwo * im_twothree + im_onetwo * re_twothree
    yx_real = re_onethree * re_onetwo + im_onethree * im_onetwo
    yx_imag = im_onethree * re_onetwo - re_onethree * im_onetwo
    triple_real = xz_real * re_onethree + xz_imag * im_onethree
    determinant = (
        diag_one * diag_two * diag_three
        + 2.0 * triple_real
        - diag_one * abs_twothree
        - diag_two * abs_onethree
        - diag_three * abs_onetwo
    )
    adjugate = [
        diag_two * diag_three - abs_twothree,
        diag_one * diag_three - abs_onethree,
        diag_one * diag_two - abs_onetwo,
        -(re_onetwo * diag_three - yz_real),
        xz_real - re_onethree * diag_two,
        -(diag_one * re_twothree - yx_real),
        -(im_onetwo * diag_three - yz_imag),
        xz_imag - im_onethree * diag_two,
        -(diag_one * im_twothree - yx_imag),
    ]
    return adjugate, determinant


def edge_pairs(cols):
    pairs = []
    for step in range(-SEARCH, SEARCH + 1):
        for column in range(-PATCH, cols + PATCH):
            if not (0 <= column < cols and 0 <= column + step < cols):
                pairs.append((step, column))
    return pairs


def band_matrix(cols):
    source = np.arange(cols)[:, None]
    target = np.arange(cols)[None, :]
    main = (np.abs(source - target) <= PATCH).astype(np.float32)
    edge = np.zeros((LANES, cols), np.float32)
    for lane, (_, column) in enumerate(edge_pairs(cols)):
        edge[lane] = np.abs(np.arange(cols) - column) <= PATCH
    high, low = edge.copy(), edge.copy()
    for place in range(SEARCH):
        high[SPARE + place, place] = 1.0
        low[SPARE + place, cols - SEARCH + place] = 1.0
    high[SPARE + SEARCH] = 1.0
    return np.concatenate([main, main, high, low], 0)


def select_matrix(cols):
    pick = np.zeros((LANES, 2 * LANES), np.float32)
    for lane, (step, column) in enumerate(edge_pairs(cols)):
        source = column + 32 if column < 32 else column - cols + 96
        pick[source, lane] = 1.0
        pick[source + step, LANES + lane] = 1.0
    return np.concatenate([pick] * 3, 0)


def keep_masks(cols):
    keep = np.zeros((SPAN, 16, LANES), np.float32)
    for lane, (step, _) in enumerate(edge_pairs(cols)):
        keep[step + SEARCH, :, lane] = 1.0
    return keep


def gain(feature):
    if feature == 2 * CHANS:
        return -6.0 * EXPONENT
    return (1.0 if feature % CHANS < 3 else 2.0) * EXPONENT


def partner(feature):
    if feature == 2 * CHANS:
        return feature
    return (feature + CHANS) % (2 * CHANS)


def despeckle(
    sizes, offs_ref, field_ref, band_ref, pick_ref, keep_ref, out_ref,
    above_ref, below_ref, left_ref, right_ref, packs, send_sems, recv_sems,
    feats, moved, own, edges, edge_own, edge_other, edge_dist, edge_sum, dist, sums, weights, keeps,
):
    rows, cols, row_total, col_total = sizes
    span_rows = rows + 2 * PAD
    edge_rows = edges.shape[0] // FEATS
    row_tiles = span_rows // 8
    head, tail = PAD // 8, (PAD + rows) // 8
    halves = cols // LANES
    dist_tiles = (rows + 8) // 8
    near_tile, far_tile = 2, dist_tiles - 2
    count = offs_ref.shape[1]
    lane = lax.broadcasted_iota(jnp.int32, (8, LANES), 1)
    sub = lax.broadcasted_iota(jnp.int32, (8, LANES), 0)
    wide_sub = lax.broadcasted_iota(jnp.int32, (16, LANES), 0)
    wide_lane = lax.broadcasted_iota(jnp.int32, (16, LANES), 1)
    row, col = lax.axis_index("rows"), lax.axis_index("offs")
    row_start, col_start = row * rows, col * cols
    row_count, col_count = lax.axis_size("rows"), lax.axis_size("offs")
    f32, bf16 = jnp.float32, jnp.bfloat16

    def present(down, side):
        return (row + down >= 0) & (row + down < row_count) & (col + side >= 0) & (col + side < col_count)

    around = [(down, side) for down in (-1, 0, 1) for side in (-1, 0, 1) if (down, side) != (0, 0)]
    barrier = pltpu.get_barrier_semaphore()
    for down, side in around:

        @pl.when(present(down, side))
        def _(down=down, side=side):
            pl.semaphore_signal(
                barrier, inc=1, device_id=(row + down, col + side), device_id_type=pl.DeviceIdType.MESH
            )


    def pack(tile, _):
        at = pl.ds(pl.multiple_of(tile * 8, 8), 8)
        first = field_ref[0, at, :LANES]
        last = pltpu.roll(field_ref[0, at, cols - LANES :], RIM, 1)
        for c in range(1, CHANS):
            here = (lane >= RIM * c) & (lane < RIM * (c + 1))
            first = jnp.where(here, pltpu.roll(field_ref[c, at, :LANES], RIM * c, 1), first)
            last = jnp.where(here, pltpu.roll(field_ref[c, at, cols - LANES :], (RIM * c + RIM) % LANES, 1), last)
        packs[0, at, :] = first
        packs[1, at, :] = last
        return 0

    lax.fori_loop(0, rows // 8, pack, 0)

    copies = []
    for k, (down, side) in enumerate(around):
        start, size, put = {-1: (0, PAD, PAD + rows), 0: (0, rows, PAD), 1: (rows - PAD, PAD, 0)}[down]
        if side == 0:
            source = field_ref.at[:, start : start + size, :]
            target = below_ref if down < 0 else above_ref
        else:
            source = packs.at[0 if side < 0 else 1, start : start + size, :]
            target = (right_ref if side < 0 else left_ref).at[put : put + size, :]
        copies.append(pltpu.make_async_remote_copy(
            src_ref=source, dst_ref=target, send_sem=send_sems.at[k], recv_sem=recv_sems.at[k],
            device_id=(row + down, col + side), device_id_type=pl.DeviceIdType.MESH,
        ))

    def features(source_ref, first, groups, tile, _):
        at = pl.ds(pl.multiple_of(tile * 8, 8), 8)
        source_at = pl.ds(pl.multiple_of(tile * 8 - first, 8), 8)
        place = tile * 8 - PAD + sub
        in_rows = (place >= -RIM) & (place < rows + RIM) & (place + row_start >= 0) & (place + row_start < row_total)
        for group in groups:
            column = (group - 1) * LANES + lane
            inside = (
                in_rows & (column >= -RIM) & (column < cols + RIM)
                & (column + col_start >= 0) & (column + col_start < col_total)
            )
            if group == 0:
                packed = left_ref[at, :]
                cells = [pltpu.roll(packed, LANES - RIM - RIM * c, 1) for c in range(CHANS)]
            elif group == halves + 1:
                packed = right_ref[at, :]
                cells = [pltpu.roll(packed, LANES - RIM * c, 1) if c else packed for c in range(CHANS)]
            else:
                cells = [source_ref[c, source_at, (group - 1) * LANES : group * LANES] for c in range(CHANS)]
            adjugate, determinant = hermitian_inverse(cells)
            scale = 1.0 / determinant
            for c in range(CHANS):
                feats[group, c, at, :] = jnp.where(inside, cells[c], 0.0)
                feats[group, CHANS + c, at, :] = jnp.where(inside, adjugate[c] * scale, 0.0)
            feats[group, 2 * CHANS, at, :] = jnp.where(inside, 1.0, 0.0)
        return 0

    def shifts(tile, _):
        at = pl.ds(pl.multiple_of(tile * 8, 8), 8)
        zero = jnp.zeros((8, LANES), f32)
        for step in range(-SEARCH, SEARCH + 1):
            for half in range(halves):
                partner_col = half * LANES + lane + step
                moved[step + SEARCH, half, 2 * CHANS, at, :] = jnp.where(
                    (partner_col >= 0) & (partner_col < cols), feats[half + 1, 2 * CHANS, at, :], 0.0
                )
        for c in range(2 * CHANS):
            cells = [zero] + [feats[half + 1, c, at, :] for half in range(halves)] + [zero]
            for step in range(-SEARCH, SEARCH + 1):
                for half in range(halves):
                    here = cells[half + 1]
                    if step > 0:
                        value = pltpu.roll(jnp.where(lane >= step, here, cells[half + 2]), LANES - step, 1)
                    elif step < 0:
                        value = pltpu.roll(jnp.where(lane < LANES + step, here, cells[half]), -step, 1)
                    else:
                        value = here
                    moved[step + SEARCH, half, c, at, :] = value
        return 0

    def own_tiles(tile, _):
        at = pl.ds(pl.multiple_of(tile * 8, 8), 8)
        for half in range(halves):
            for c in range(FEATS):
                own[half, c, at, :] = gain(c) * feats[half + 1, partner(c), pl.ds(tile * 8 + PAD - PATCH, 8), :]
        return 0

    def distances(turn, downs, sides, step, _):
        half, tile = step % halves, step // halves
        at = pl.ds(pl.multiple_of(tile * 8, 8), 8)
        mine = [own[half, c, at, :] for c in range(FEATS)]
        for j in range(BATCH):
            rows_at = pl.ds(tile * 8 + PAD - PATCH + downs[j], 8)
            terms = [None, None]
            for c in range(FEATS):
                term = mine[c] * moved[sides[j], half, c, rows_at, :]
                terms[c % 2] = term if terms[c % 2] is None else terms[c % 2] + term
            dist[turn * BATCH + j, half, at, :] = terms[0] + terms[1]
        return 0

    def distance_batch(spans, turn, _):
        downs = [offs_ref[0, turn * BATCH + j] for j in range(BATCH)]
        sides = [offs_ref[1, turn * BATCH + j] + SEARCH for j in range(BATCH)]
        for start, stop in spans:
            lax.fori_loop(start * halves, stop * halves, functools.partial(distances, turn, downs, sides), 0)
        return 0

    inner = tuple(range(1, halves + 1))
    lax.fori_loop(head, tail, functools.partial(features, field_ref, PAD, inner), 0)
    def distance_span(first_batch, last_batch, start, stop):
        span = functools.partial(distance_batch, ((start, stop),))
        lax.fori_loop(first_batch, last_batch, span, 0)

    lax.fori_loop(head, tail, shifts, 0)
    lax.fori_loop(near_tile, far_tile, own_tiles, 0)
    distance_span(0, AHEAD, near_tile, near_tile + 2)
    over = 1 + (row > 0).astype(jnp.int32) + (row < row_count - 1).astype(jnp.int32)
    across = 1 + (col > 0).astype(jnp.int32) + (col < col_count - 1).astype(jnp.int32)
    pl.semaphore_wait(barrier, over * across - 1)
    for (down, side), copy in zip(around, copies):
        pl.when(present(down, side))(copy.start)
    distance_span(0, AHEAD, near_tile + 2, far_tile)
    distance_span(AHEAD, count // BATCH, near_tile, far_tile)

    for (down, side), copy in zip(around, copies):
        if (down, side) == (-1, 0):
            pl.when(present(-down, -side))(copy.wait_recv)
    lax.fori_loop(tail, row_tiles, functools.partial(features, below_ref, PAD + rows, inner), 0)
    lax.fori_loop(tail, row_tiles, shifts, 0)
    lax.fori_loop(far_tile, dist_tiles, own_tiles, 0)
    distance_span(0, count // BATCH, far_tile, dist_tiles)

    for (down, side), copy in zip(around, copies):
        pl.when(present(down, side))(copy.wait_send)
        if (down, side) != (-1, 0):
            pl.when(present(-down, -side))(copy.wait_recv)
    outer = (0, halves + 1)
    lax.fori_loop(0, head, functools.partial(features, above_ref, 0, outer + inner), 0)
    lax.fori_loop(head, tail, functools.partial(features, field_ref, PAD, outer), 0)
    lax.fori_loop(tail, row_tiles, functools.partial(features, below_ref, PAD + rows, outer), 0)
    lax.fori_loop(0, head, shifts, 0)
    lax.fori_loop(0, near_tile, own_tiles, 0)
    distance_span(0, count // BATCH, 0, near_tile)

    def split(value):
        high = value.astype(bf16)
        return high, (value - high.astype(f32)).astype(bf16)

    def edge_columns(tile, _):
        at = pl.ds(pl.multiple_of(tile * 16, 16), 16)
        for c in range(FEATS):
            cells = [feats[group, c, at, :] for group in range(halves + 2)]
            before = pltpu.roll(jnp.where(wide_lane >= 96, cells[0], cells[1]), 32, 1)
            after = pltpu.roll(jnp.where(wide_lane >= 96, cells[halves], cells[halves + 1]), 96, 1)
            value = jnp.where(wide_lane < 64, before, after)
            high = value.astype(bf16)
            middle, low = split(value - high.astype(f32))
            edge_at = pl.ds(pl.multiple_of(c * edge_rows + tile * 16, 16), 16)
            edges[edge_at, :LANES] = high
            edges[edge_at, LANES : 2 * LANES] = middle
            edges[edge_at, 2 * LANES :] = low
        return 0

    def patches(tile, _):
        at = pl.ds(pl.multiple_of(tile * 8, 8), 8)
        for c in range(CHANS):
            before, after = feats[0, c, at, :], feats[halves + 1, c, at, :]
            for step in range(1, SEARCH + 1):
                up, down = (step + SEARCH, halves - 1, c, at), (SEARCH - step, 0, c, at)
                moved[up] = jnp.where(lane >= LANES - step, pltpu.roll(after, LANES - step, 1), moved[up])
                moved[down] = jnp.where(lane < step, pltpu.roll(before, step, 1), moved[down])
        return 0

    lax.fori_loop(0, row_tiles // 2, edge_columns, 0)
    both = jnp.dot(edges[...], pick_ref[...], preferred_element_type=f32)
    edge_own[...] = both[:, :LANES]
    edge_other[...] = both[:, LANES:]

    def edge_tiles(tile, _):
        at = pl.ds(pl.multiple_of(tile * 8, 8), 8)
        mine = [
            gain(c) * edge_own[pl.ds(partner(c) * edge_rows + tile * 8 + PAD - PATCH, 8), :]
            for c in range(FEATS)
        ]
        for step in range(SPAN):
            value = None
            for c in range(FEATS):
                rows_at = pl.ds(c * edge_rows + tile * 8 + PAD - PATCH - SEARCH + step, 8)
                term = mine[c] * edge_other[rows_at, :]
                value = term if value is None else value + term
            edge_dist[step, at, :] = value
        return 0

    lax.fori_loop(0, dist_tiles, edge_tiles, 0)

    def edge_sums(step, _):
        for part in range(rows // 16):
            value = edge_dist[step, pl.ds(16 * part, 16), :]
            for s in range(1, SIDE):
                value = value + edge_dist[step, pl.ds(16 * part + s, 16), :]
            partner_row = row_start + 16 * part + wide_sub + step - SEARCH
            outside = (partner_row < 0) | (partner_row >= row_total)
            high, low = split(jnp.where(wide_lane >= SPARE, 0.0, value))
            far = jnp.where((wide_lane < SPARE + SEARCH) | outside, FAR, 0.0)
            high = jnp.where(wide_lane >= SPARE, far, high.astype(f32)).astype(bf16)
            low = jnp.where(wide_lane >= SPARE, FAR, low.astype(f32)).astype(bf16)
            edge_sum[step, 16 * part : 16 * part + 16, :LANES] = high
            edge_sum[step, 16 * part : 16 * part + 16, LANES:] = low
        return 0

    lax.fori_loop(0, SPAN, edge_sums, 0)

    def keep_tables(step, _):
        place = wide_lane - SPARE
        known = keep_ref[step].astype(f32)
        before = col_start + place + step - SEARCH < 0
        after = col_start + cols - SEARCH + place + step - SEARCH >= col_total
        spare = (place >= 0) & (place < SEARCH)
        high = jnp.where((spare & before) | (place == SEARCH), 1.0, known)
        low = jnp.where(spare & after, 1.0, known)
        keeps[step, :, :LANES] = high.astype(bf16)
        keeps[step, :, LANES:] = low.astype(bf16)
        return 0

    lax.fori_loop(0, SPAN, keep_tables, 0)
    out_ref[...] = jnp.zeros_like(out_ref)
    chunk = GROUP * rows // 2

    def window(turn, j, _):
        k = turn * GROUP + j
        down = offs_ref[0, k] + SEARCH
        keep = keeps[offs_ref[1, k] + SEARCH]
        for part in range(rows // 16):
            at = pl.ds(pl.multiple_of(j * rows + 16 * part, 16), 16)
            for half in range(halves):
                value = dist[k, half, pl.ds(16 * part, 16), :]
                for s in range(1, SIDE):
                    value = value + dist[k, half, pl.ds(16 * part + s, 16), :]
                high, low = split(value)
                sums[at, half * LANES : (half + 1) * LANES] = high
                sums[at, cols + half * LANES : cols + (half + 1) * LANES] = low
            for which in range(2):
                span = slice(which * LANES, (which + 1) * LANES)
                sums[at, 2 * cols + which * LANES : 2 * cols + (which + 1) * LANES] = (
                    edge_sum[down, 16 * part : 16 * part + 16, span] * keep[:, span]
                )
        return 0

    def weigh(piece, _):
        at = pl.ds(pl.multiple_of(piece * chunk, chunk), chunk)
        patch = jnp.dot(sums[at, :], band_ref[...], preferred_element_type=f32)
        weights[at, :] = jnp.exp2(patch)
        return 0

    def accumulate(turn, downs, sides, tile, _):
        at = pl.ds(pl.multiple_of(tile * 8, 8), 8)
        for half in range(halves):
            span = slice(half * LANES, (half + 1) * LANES)
            total = [out_ref[c, at, span] for c in range(CHANS + 1)]
            for j in range(GROUP):
                rows_at = pl.ds(tile * 8 + PAD + downs[j], 8)
                weight = weights[pl.ds(pl.multiple_of(j * rows + tile * 8, 8), 8), span]
                for c in range(CHANS):
                    total[c] = total[c] + weight * moved[sides[j], half, c, rows_at, :]
                total[CHANS] = total[CHANS] + weight
            for c in range(CHANS + 1):
                out_ref[c, at, span] = total[c]
        return 0

    def weigh_and_add(turn):
        downs = [offs_ref[0, turn * GROUP + j] for j in range(GROUP)]
        sides = [offs_ref[1, turn * GROUP + j] + SEARCH for j in range(GROUP)]
        lax.fori_loop(0, 2, weigh, 0)
        lax.fori_loop(0, rows // 8, functools.partial(accumulate, turn, downs, sides), 0)

    def group(turn, _):
        lax.fori_loop(0, GROUP, functools.partial(window, turn), 0)
        weigh_and_add(turn)
        return 0

    pace = GROUP // (row_tiles - 2)

    def first_group(tile, _):
        patches(tile, 0)
        for j in range(pace):
            window(0, (tile - 1) * pace + j, 0)
        return 0

    lax.fori_loop(1, row_tiles - 1, first_group, 0)
    lax.fori_loop(pace * (row_tiles - 2), GROUP, functools.partial(window, 0), 0)
    weigh_and_add(0)
    lax.fori_loop(1, count // GROUP, group, 0)


def finish(field_ref, sums_ref, out_ref):
    def tile_rows(tile, _):
        at = pl.ds(pl.multiple_of(tile * 8, 8), 8)
        scale = 1.0 / (1.0 + sums_ref[CHANS, at, :])
        for c in range(CHANS):
            out_ref[c, at, :] = (field_ref[c, at, :] + sums_ref[c, at, :]) * scale
        return 0

    lax.fori_loop(0, field_ref.shape[1] // 8, tile_rows, 0)


def filter_block(sizes, offsets, field):
    rows, cols = sizes[:2]
    span_rows = rows + 2 * PAD
    edge_rows = span_rows + BANKS
    halves = cols // LANES
    vmem = pl.BlockSpec(memory_space=pltpu.VMEM)
    smem = pl.BlockSpec(memory_space=pltpu.SMEM)
    f32, bf16 = jnp.float32, jnp.bfloat16
    return pl.pallas_call(
        functools.partial(despeckle, sizes),
        out_shape=jax.ShapeDtypeStruct((CHANS + 1, rows, cols), f32),
        in_specs=[smem] + [vmem] * 4,
        out_specs=vmem,
        scratch_shapes=[
            pltpu.VMEM((CHANS, PAD, cols), f32),
            pltpu.VMEM((CHANS, PAD, cols), f32),
            pltpu.VMEM((span_rows, LANES), f32),
            pltpu.VMEM((span_rows, LANES), f32),
            pltpu.VMEM((2, rows, LANES), f32),
            pltpu.SemaphoreType.DMA((8,)),
            pltpu.SemaphoreType.DMA((8,)),
            pltpu.VMEM((halves + 2, FEATS, span_rows + BANKS, LANES), f32),
            pltpu.VMEM((SPAN, halves, FEATS, span_rows + BANKS, LANES), f32),
            pltpu.VMEM((halves, FEATS, rows + BANKS, LANES), f32),
            pltpu.VMEM((FEATS * edge_rows, 3 * LANES), bf16),
            pltpu.VMEM((FEATS * edge_rows, LANES), f32),
            pltpu.VMEM((FEATS * edge_rows, LANES), f32),
            pltpu.VMEM((SPAN, rows + 8, LANES), f32),
            pltpu.VMEM((SPAN, rows, 2 * LANES), bf16),
            pltpu.VMEM((offsets.shape[0], halves, rows + 8, LANES), f32),
            pltpu.VMEM((GROUP * rows, 2 * cols + 2 * LANES), bf16),
            pltpu.VMEM((GROUP * rows, cols), f32),
            pltpu.VMEM((SPAN, 16, 2 * LANES), bf16),
        ],
        compiler_params=pltpu.CompilerParams(
            vmem_limit_bytes=62 * 1024 * 1024, collective_id=0, has_side_effects=True
        ),
    )(
        offsets.T, field, jnp.asarray(band_matrix(cols), bf16), jnp.asarray(select_matrix(cols), bf16),
        jnp.asarray(keep_masks(cols), bf16),
    )


def per_device(coherency_field, offsets):
    _, rows, cols = coherency_field.shape
    row_total = rows * lax.axis_size("rows")
    col_total = cols * lax.axis_size("offs")
    sums = filter_block((rows, cols, row_total, col_total), offsets, coherency_field)
    vmem = pl.BlockSpec(memory_space=pltpu.VMEM)
    return pl.pallas_call(
        finish,
        out_shape=jax.ShapeDtypeStruct(coherency_field.shape, jnp.float32),
        in_specs=[vmem, vmem],
        out_specs=vmem,
    )(coherency_field, sums)


def solution(mesh):
    in_specs = (P(None, "rows", "offs"), P())
    out_specs = P(None, "rows", "offs")
    return jax.shard_map(
        per_device, mesh=mesh, in_specs=in_specs, out_specs=out_specs, check_vma=False
    )
```
